32 devices in a mesh: fsdp: 4 (over z), ctx: 4 (over y, core), tp: 2 (over x).
Axes of the slice: x: 2, y: 2, z: 4, core: 2. Of those that a mesh axis runs over, the one named last changes fastest.
Arguments:
- tokens: bfloat16 [4, 1024, 1024], P('fsdp', 'ctx'), may hold values from -6 to 6
- segments: int32 [4, 1024], P('fsdp', 'ctx'), may hold values from 0 to 3, never falling along the last dimension, each value on 1 to 512 neighbouring positions
- ln1_gain: bfloat16 [1024], P('fsdp'), may hold values from 0.099609375 to 1.8984375
- ln1_bias: bfloat16 [1024], P('fsdp'), may hold values from -1.75 to 1.75
- w_qkv: bfloat16 [1024, 3, 1024], P('fsdp', None, 'tp'), may hold values from -0.1875 to 0.1875
- b_qv: bfloat16 [2, 16, 64], P(None, 'tp', 'fsdp'), may hold values from -1.25 to 1.25
- w_out: bfloat16 [1024, 1024], P('tp', 'fsdp'), may hold values from -1 to 1
- b_out: bfloat16 [1024], P('fsdp'), may hold values from -1.75 to 1.75
- ln2_gain: bfloat16 [1024], P('fsdp'), may hold values from 0.099609375 to 1.8984375
- ln2_bias: bfloat16 [1024], P('fsdp'), may hold values from -1.75 to 1.75
- w_up: bfloat16 [1024, 4096], P('fsdp', 'tp'), may hold values from -0.1875 to 0.1875
- b_up: bfloat16 [32, 128], P('tp', 'fsdp'), may hold values from -3 to 3
- w_down: bfloat16 [4096, 1024], P('tp', 'fsdp'), may hold values from -0.09375 to 0.09375
- b_down: bfloat16 [1024], P('fsdp'), may hold values from -1.75 to 1.75
- cotangent: bfloat16 [4, 1024, 1024], P('fsdp', 'ctx'), may hold values from -6 to 6
Outputs:
- output: bfloat16 [4, 1024, 1024], P('fsdp', 'ctx')
- grad_tokens: bfloat16 [4, 1024, 1024], P('fsdp', 'ctx')
- grad_ln1_gain: float32 [1024], P('fsdp')
- grad_ln1_bias: float32 [1024], P('fsdp')
- grad_w_qkv: float32 [1024, 3, 1024], P('fsdp', None, 'tp')
- grad_b_qv: float32 [2, 16, 64], P(None, 'tp', 'fsdp')
- grad_w_out: float32 [1024, 1024], P('tp', 'fsdp')
- grad_b_out: float32 [1024], P('fsdp')
- grad_ln2_gain: float32 [1024], P('fsdp')
- grad_ln2_bias: float32 [1024], P('fsdp')
- grad_w_up: float32 [1024, 4096], P('fsdp', 'tp')
- grad_b_up: float32 [32, 128], P('tp', 'fsdp')
- grad_w_down: float32 [4096, 1024], P('tp', 'fsdp')
- grad_b_down: float32 [1024], P('fsdp')
The draws below stay inside these ranges and needn't reach their ends.
Inputs may be any that keep to these rules, and one draw needn't show every extreme that they name: `segments`: segment numbers never fall along a sequence; a document may cross the spans of several devices.
All inputs are finite; a program needn't handle non-finite values.
Results may differ from the reference program's by a relative error of at most 0.02.
Values may be sent and summed in bfloat16 or wider, within the bound.
No kernel may reach another device: no remote copies, remote signals or barrier semaphores. Data moves between devices by JAX's collectives and lax.ppermute only.
A program may use at most 128 MiB of HBM per device.

```python
import math
import jax
import jax.numpy as jnp
import numpy as np
from jax import lax

D = 1024
HEADS = 16
HD = 64
FF = 4096
SEQ_LEN = 1024
SEQS = 4
DOCS = 4
DOC_MOST = 512


def steps_of(stream_key, extent, shards, least, largest):
    gain = 1.0
    for axis_at, parts in shards:
        draws = jax.random.uniform(jax.random.fold_in(jax.random.fold_in(stream_key, 6), axis_at), (parts,), jnp.float32, least / len(shards), largest / len(shards))
        gain = gain * jnp.repeat(jnp.exp(draws), extent[axis_at] // parts).reshape((-1,) + (1,) * (len(extent) - 1 - axis_at))
    return gain


def split_up(amount, total, limit, slope):
    portions = [(1 << 20) // math.isqrt(grade ** slope) + 1 for grade in range(2, amount + 1)]
    spare, holding = total - limit - (amount - 1), [1] * (amount - 1)
    while spare > 0:
        free = [i for i in range(amount - 1) if holding[i] < limit]
        mass, remaining = sum([portions[i] for i in free]), spare
        for i in free:
            addition = min(limit - holding[i], max(1, remaining * portions[i] // mass), spare)
            holding[i] = holding[i] + addition
            spare = spare - addition
    return np.array([limit] + holding)


def ragged(rng, count, total, limit, lean):
    if count == 2:
        one = jax.random.randint(rng, (), max(1, total - limit), min(limit, total - 1) + 1)
        return jnp.stack([one, total - one])
    tallies = jnp.asarray(split_up(count, total, limit, lean), jnp.int32)
    pairs = (count - 1) // 2
    donor, taker = tallies[1:1 + 2 * pairs:2], tallies[2:2 + 2 * pairs:2]
    margin = jnp.minimum(donor - 1, limit - taker)
    moved = jax.random.randint(jax.random.fold_in(rng, 1), (pairs,), 0, 1 << 20) % (margin + 1)
    tallies = tallies.at[1:1 + 2 * pairs:2].set(donor - moved).at[2:2 + 2 * pairs:2].set(taker + moved)
    return tallies[jax.random.permutation(jax.random.fold_in(rng, 2), count)]


def normal_values(stream_key, shape, scale, reach, split=(), held_as=jnp.bfloat16):
    values = scale * jax.random.normal(stream_key, shape, jnp.float32)
    if split:
        values = values * steps_of(stream_key, shape, split, -0.22, 0.18)
    return jnp.clip(values, -reach, reach).astype(held_as)


def setup_inputs(seed: int = 0) -> dict:
    keys = jax.random.split(jax.random.key(seed), 16)
    tokens = normal_values(keys[0], (SEQS, SEQ_LEN, D), 1.0, 6.0, ((0, 4), (1, 4)))
    segments = jax.vmap(lambda own: jnp.searchsorted(jnp.cumsum(ragged(own, DOCS, SEQ_LEN, DOC_MOST, 2)), jnp.arange(SEQ_LEN), side="right"))(jax.random.split(keys[1], SEQS)).reshape((SEQS, SEQ_LEN)).astype(jnp.int32)
    ln1_gain = jnp.clip(1.0 + 0.18 * jax.random.normal(keys[2], (D,), jnp.float32), 0.099609375, 1.8984375).astype(jnp.bfloat16)
    ln1_bias = normal_values(keys[3], (D,), 0.3, 1.75, ((0, 4),))
    w_qkv = normal_values(keys[4], (D, 3, D), D ** -0.5, 0.1875, ((0, 4), (2, 2)))
    b_qv = normal_values(keys[5], (2, HEADS, HD), 0.2, 1.25, ((1, 2), (2, 4)))
    w_out = normal_values(keys[6], (D, D), (D // 32) ** -0.5, 1.0, ((0, 2), (1, 4)))
    b_out = normal_values(keys[7], (D,), 0.3, 1.75, ((0, 4),))
    ln2_gain = jnp.clip(1.0 + 0.18 * jax.random.normal(keys[8], (D,), jnp.float32), 0.099609375, 1.8984375).astype(jnp.bfloat16)
    ln2_bias = normal_values(keys[9], (D,), 0.3, 1.75, ((0, 4),))
    w_up = normal_values(keys[10], (D, FF), D ** -0.5, 0.1875, ((0, 4), (1, 2)))
    b_up = normal_values(keys[11], (FF // 128, 128), 0.5, 3.0, ((0, 2), (1, 4)))
    w_down = normal_values(keys[12], (FF, D), FF ** -0.5, 0.09375, ((0, 2), (1, 4)))
    b_down = normal_values(keys[13], (D,), 0.3, 1.75, ((0, 4),))
    cotangent = normal_values(keys[14], (SEQS, SEQ_LEN, D), 1.0, 6.0, ((0, 4), (1, 4)))
    return dict(tokens=tokens, segments=segments, ln1_gain=ln1_gain, ln1_bias=ln1_bias, w_qkv=w_qkv, b_qv=b_qv, w_out=w_out, b_out=b_out, ln2_gain=ln2_gain, ln2_bias=ln2_bias, w_up=w_up, b_up=b_up, w_down=w_down, b_down=b_down, cotangent=cotangent)


@jax.custom_vjp
def low(v):
    return lax.optimization_barrier(v.astype(jnp.bfloat16)).astype(jnp.float32)

@jax.custom_vjp
def low_back(v):
    return v

def low_keep(v):
    return (low(v), None)

def low_pass(kept, grad):
    return (grad,)

def back_keep(v):
    return (v, None)

def back_low(kept, grad):
    return (low(grad),)
low.defvjp(low_keep, low_pass)
low_back.defvjp(back_keep, back_low)
EPSILON = 1e-05
NEGATIVE = -1e+30
HIGHEST = lax.Precision.HIGHEST

def layer_norm(values, scaling, offset):
    centred = values - lax.optimization_barrier(jnp.mean(values, axis=-1, keepdims=True))
    variance = lax.optimization_barrier(jnp.mean(centred * centred, axis=-1, keepdims=True))
    return centred * lax.rsqrt(variance + EPSILON) * scaling + offset

def gelu_tanh(values):
    return 0.5 * values * (1.0 + jnp.tanh(0.7978845608028654 * (values + 0.044715 * values * values * values)))

def attention(queries, key_heads, values, seq_segs):
    length = queries.shape[0]
    block_rows = min(512, length)
    score_scale = HD ** (-0.5)
    key_pos = jnp.arange(length, dtype=jnp.int32)

    def attend(first_row):
        query_blk = lax.dynamic_slice_in_dim(queries, first_row, block_rows, 0)
        query_seg = lax.dynamic_slice_in_dim(seq_segs, first_row, block_rows, 0)
        query_pos = first_row + jnp.arange(block_rows, dtype=jnp.int32)
        scores = low_back(jnp.einsum('qhe,khe->hqk', query_blk, key_heads, precision=HIGHEST) * score_scale)
        allowed = (key_pos[None, :] <= query_pos[:, None]) & (seq_segs[None, :] == query_seg[:, None])
        masked = jnp.where(allowed[None], scores, NEGATIVE)
        row_max = lax.optimization_barrier(jnp.max(masked, axis=-1, keepdims=True))
        expo = jnp.where(allowed[None], jnp.exp(masked - row_max), 0.0)
        probs = expo / lax.optimization_barrier(jnp.sum(expo, axis=-1, keepdims=True))
        return jnp.einsum('hqk,khe->qhe', low(probs), values, precision=HIGHEST)
    starts = jnp.arange(length // block_rows, dtype=jnp.int32) * block_rows
    blocks = lax.map(jax.checkpoint(attend), starts)
    return blocks.reshape(length, HEADS, HD)

def block_forward(params, inputs, seq_segs):
    ln1_gain, ln1_bias, w_qkv, b_qv, w_out, b_out, ln2_gain, ln2_bias, w_up, b_up, w_down, b_down = params
    length = inputs.shape[0]
    normed_one = low(layer_norm(inputs, ln1_gain, ln1_bias))
    project = jnp.einsum('td,dke->tke', normed_one, w_qkv, precision=HIGHEST)
    qv_bias = b_qv.reshape(2, D)
    queries = low(low_back(project[:, 0] + qv_bias[0])).reshape(length, HEADS, HD)
    key_heads = low(low_back(project[:, 1])).reshape(length, HEADS, HD)
    values = low(low_back(project[:, 2] + qv_bias[1])).reshape(length, HEADS, HD)
    mixed = attention(queries, key_heads, values, seq_segs)
    attn_mix = low(low_back(mixed.reshape(length, D)))
    residual = inputs + low_back(jnp.dot(attn_mix, w_out, precision=HIGHEST)) + b_out
    normed_two = low(layer_norm(residual, ln2_gain, ln2_bias))
    up_proj = low_back(jnp.dot(normed_two, w_up, precision=HIGHEST) + b_up.reshape(FF))
    activated = low(gelu_tanh(up_proj))
    return residual + jnp.dot(activated, w_down, precision=HIGHEST) + b_down

def reference(tokens, segments, ln1_gain, ln1_bias, w_qkv, b_qv, w_out, b_out, ln2_gain, ln2_bias, w_up, b_up, w_down, b_down, cotangent):
    params = tuple((parameter.astype(jnp.float32) for parameter in (ln1_gain, ln1_bias, w_qkv, b_qv, w_out, b_out, ln2_gain, ln2_bias, w_up, b_up, w_down, b_down)))
    zeros = tuple((jnp.zeros(parameter.shape, jnp.float32) for parameter in params))

    def one_sequence(totals, sequence_item):
        seq_tokens, seq_segs, seq_cot = sequence_item

        def forward(weights, inputs):
            return block_forward(weights, inputs, seq_segs)
        result, pull = jax.vjp(forward, params, seq_tokens.astype(jnp.float32))
        grad_params, grad_inputs = pull(seq_cot.astype(jnp.float32))
        totals = tuple((total + extra for total, extra in zip(totals, grad_params)))
        return (totals, (result.astype(jnp.bfloat16), grad_inputs.astype(jnp.bfloat16)))
    totals, outputs = lax.scan(one_sequence, zeros, (tokens, segments, cotangent))
    return (outputs[0], outputs[1], totals[0], totals[1], totals[2], totals[3], totals[4], totals[5], totals[6], totals[7], totals[8], totals[9], totals[10], totals[11])
```

```python
import jax
import jax.numpy as jnp
import numpy as np
from jax import lax
from jax.sharding import Mesh
from jax.sharding import PartitionSpec as P

HD = 64
EPSILON = 1e-05
NEGATIVE = -1e30
F32 = jnp.float32
BF16 = jnp.bfloat16

CTX = ("y", "core")
PLANE = ("y", "core", "tp")


def size_of(axes):
    return int(np.prod([lax.axis_size(a) for a in axes]))


def index_of(axes):
    index = 0
    for a in axes:
        index = index * lax.axis_size(a) + lax.axis_index(a)
    return index


def swap(value, axes, bits):
    count = size_of(axes)
    return lax.ppermute(value, axes, [(i, i ^ bits) for i in range(count)])


def bits_of(axes):
    bits, at = [], 1
    for a in reversed(axes):
        mine = []
        while len(mine) < (lax.axis_size(a) - 1).bit_length():
            mine.append(at)
            at *= 2
        bits = mine + bits if a == "core" else bits + mine
    return bits


def gather_blocks(value, axes):
    blocks, masks = [value], [0]
    bits = bits_of(axes)
    for r in range(1, size_of(axes)):
        low = r & -r
        bit = bits[low.bit_length() - 1]
        blocks.append(swap(blocks[r ^ low], axes, bit))
        masks.append(masks[r ^ low] | bit)
    return blocks, masks


def placed(blocks, positions, axis):
    shape = list(blocks[0].shape)
    step = shape[axis]
    shape[axis] = step * len(blocks)
    out = jnp.zeros(shape, blocks[0].dtype)
    for block, position in zip(blocks, positions):
        out = lax.dynamic_update_slice_in_dim(out, block, position * step, axis)
    return out


def gather_ordered(value, axes, axis):
    me = index_of(axes)
    blocks, masks = gather_blocks(value, axes)
    return placed(blocks, [me ^ mask for mask in masks], axis)


def scatter_sum(pieces_of, axes):
    count = size_of(axes)
    total = {r: pieces_of(r) for r in range(count)}
    for r in range(count - 1, 0, -1):
        low = r & -r
        arrived = swap(total[r].astype(BF16), axes, low).astype(F32)
        total[r ^ low] = total[r ^ low] + arrived
    return total[0]


def normalise(values):
    centred = values - jnp.mean(values, axis=-1, keepdims=True)
    variance = jnp.mean(centred * centred, axis=-1, keepdims=True)
    scale = lax.rsqrt(variance + EPSILON)
    return centred * scale, scale


def norm_grad(vhat, scale, weighted):
    return scale * (
        weighted
        - jnp.mean(weighted, axis=-1, keepdims=True)
        - vhat * jnp.mean(weighted * vhat, axis=-1, keepdims=True)
    )


def gelu_tanh(values):
    return (
        0.5
        * values
        * (1.0 + jnp.tanh(0.7978845608028654 * (values + 0.044715 * values * values * values)))
    )


def dot(a, b, dims):
    return lax.dot_general(a, b, (dims, ((), ())), preferred_element_type=F32)


def body(
    tokens,
    segments,
    ln1_gain,
    ln1_bias,
    w_qkv,
    b_qv,
    w_out,
    b_out,
    ln2_gain,
    ln2_bias,
    w_up,
    b_up,
    w_down,
    b_down,
    cotangent,
):
    z_count, z_me = lax.axis_size("fsdp"), lax.axis_index("fsdp")
    c_count, c_me = size_of(CTX), index_of(CTX)
    t_count, t_me = lax.axis_size("tp"), lax.axis_index("tp")
    p_count, p_me = c_count * t_count, index_of(PLANE)
    span, width = tokens.shape[1], tokens.shape[2]
    length = span * c_count
    own = span // t_count
    feats = w_qkv.shape[2] // c_count
    heads = feats // HD
    units = w_up.shape[1] // c_count
    part = width // z_count
    score_scale = HD ** (-0.5)

    qkv_own = lax.dynamic_slice_in_dim(jnp.swapaxes(w_qkv, 0, 1), c_me * feats, feats, 2)
    out_own = lax.dynamic_slice_in_dim(w_out, c_me * feats, feats, 0)
    up_own = lax.dynamic_slice_in_dim(w_up, c_me * units, units, 1)
    down_own = lax.dynamic_slice_in_dim(w_down, c_me * units, units, 0)
    bqv_own = lax.dynamic_slice_in_dim(b_qv, c_me * heads, heads, 1)
    up_rows = b_up.shape[0] // c_count
    bup_own = lax.dynamic_slice_in_dim(b_up, c_me * up_rows, up_rows, 0)
    vectors = jnp.stack([ln1_gain, ln1_bias, b_out, ln2_gain, ln2_bias, b_down])
    small_own = jnp.concatenate(
        [vectors.reshape(-1), bqv_own.reshape(-1), bup_own.reshape(-1)]
    )

    x_full = gather_ordered(tokens[0], CTX, 0)
    seg_full = gather_ordered(segments, CTX, 1)[0]
    qkv_full = gather_ordered(qkv_own, ("fsdp",), 1)
    small_all = gather_ordered(small_own[None], ("fsdp",), 0)
    out_part = gather_ordered(out_own, ("fsdp",), 1)
    up_full = gather_ordered(up_own, ("fsdp",), 0)
    down_full = gather_ordered(down_own, ("fsdp",), 1)
    cot_full = gather_ordered(cotangent[0], CTX, 0)

    v_size = 6 * part
    q_size = 2 * heads * (HD // z_count)
    vec_full = small_all[:, :v_size].reshape(z_count, 6, part).swapaxes(0, 1).reshape(6, width)
    vec_full = vec_full.astype(F32)
    gain_one, bias_one, bias_out, gain_two, bias_two, bias_down = [vec_full[i] for i in range(6)]
    bias_qv = (
        small_all[:, v_size : v_size + q_size]
        .reshape(z_count, 2, heads, HD // z_count)
        .transpose(1, 2, 0, 3)
        .reshape(2, feats)
        .astype(F32)
    )
    bias_up = (
        small_all[:, v_size + q_size :]
        .reshape(z_count, up_rows, b_up.shape[1])
        .transpose(1, 0, 2)
        .reshape(units)
        .astype(F32)
    )

    out_full = gather_ordered(out_part, PLANE, 0)

    vhat_one, _ = normalise(x_full.astype(F32))
    normed_one = (vhat_one * gain_one + bias_one).astype(BF16)
    queries = (dot(normed_one, qkv_full[0], ((1,), (0,))) + bias_qv[0]).astype(BF16)
    keys = dot(normed_one, qkv_full[1], ((1,), (0,))).astype(BF16)
    values = (dot(normed_one, qkv_full[2], ((1,), (0,))) + bias_qv[1]).astype(BF16)

    def as_heads(flat):
        return flat.reshape(length, heads, HD)

    places = jnp.arange(length, dtype=jnp.int32)
    allowed = (places[None, :] <= places[:, None]) & (seg_full[None, :] == seg_full[:, None])
    scores = (
        jnp.einsum("qhe,khe->hqk", as_heads(queries), as_heads(keys), preferred_element_type=F32)
        * score_scale
    )
    top = jnp.max(jnp.where(allowed, scores, NEGATIVE), axis=-1, keepdims=True)
    expo = jnp.where(allowed, jnp.exp(scores - top), 0.0)
    log_total = top + jnp.log(jnp.sum(expo, axis=-1, keepdims=True))
    probs = jnp.where(allowed, jnp.exp(scores - log_total), 0.0)
    weights = probs.astype(BF16)
    mixed = jnp.einsum("hqk,khe->qhe", weights, as_heads(values), preferred_element_type=F32)
    attn_mix = mixed.reshape(length, feats).astype(BF16)

    attn_rows = lax.all_to_all(attn_mix, PLANE, 0, 1, tiled=True)
    x_own = lax.dynamic_slice_in_dim(tokens[0], t_me * own, own, 0).astype(F32)
    cot_own = lax.dynamic_slice_in_dim(cotangent[0], t_me * own, own, 0).astype(F32)
    residual = x_own + dot(attn_rows, out_full, ((1,), (0,))) + bias_out
    vhat_two, scale_two = normalise(residual)
    normed_own = (vhat_two * gain_two + bias_two).astype(BF16)

    def plane_sum(partial):
        core = lax.axis_index("core")
        parts = partial.astype(BF16).reshape(c_count // 2, 2, t_count, own, width)
        keep = lax.dynamic_index_in_dim(parts, core, 1, keepdims=False)
        give = lax.dynamic_index_in_dim(parts, 1 - core, 1, keepdims=False)
        both = keep.astype(F32) + swap(give, CTX, 1).astype(F32)
        both = both.astype(BF16).reshape(-1, own, width)
        landed = lax.all_to_all(both, ("y", "tp"), 0, 0, tiled=True)
        return jnp.sum(landed.astype(F32), axis=0)

    normed_two = gather_ordered(normed_own, PLANE, 0)
    up_proj = dot(normed_two, up_full, ((1,), (0,))) + bias_up
    activated_f, gelu_pull = jax.vjp(gelu_tanh, up_proj)
    activated = activated_f.astype(BF16)
    d_activated = dot(cot_full, down_full, ((1,), (1,)))
    d_up = gelu_pull(d_activated)[0].astype(BF16)
    grad_b_up = jnp.sum(d_up.astype(F32), axis=0)

    d_norm_two = plane_sum(dot(d_up, up_full, ((1,), (1,))))
    down_sum = plane_sum(dot(activated, down_full, ((1,), (0,))))
    output_own = (residual + down_sum + bias_down).astype(BF16)

    def span_rows(rows):
        other = swap(rows, ("tp",), 1) if t_count == 2 else None
        return placed([rows, other], [t_me, 1 - t_me], 0)[None]

    output = span_rows(output_own)

    grad_gain_two = jnp.sum(vhat_two * d_norm_two, axis=0)
    grad_bias_two = jnp.sum(d_norm_two, axis=0)
    d_residual = cot_own + norm_grad(vhat_two, scale_two, gain_two * d_norm_two)
    grad_b_out = jnp.sum(d_residual, axis=0)
    grad_b_down = jnp.sum(cot_own, axis=0)
    d_branch = d_residual.astype(BF16)
    d_mix_rows = dot(d_branch, out_full, ((1,), (1,))).astype(BF16)
    d_mix = lax.all_to_all(d_mix_rows, PLANE, 1, 0, tiled=True)
    d_branch_full = gather_ordered(d_branch, PLANE, 0)
    grad_w_out = dot(attn_mix, d_branch_full, ((0,), (0,)))
    grad_w_down = dot(activated, cot_full, ((0,), (0,)))
    grad_w_up = dot(normed_two, d_up, ((0,), (0,)))

    d_mix_heads = as_heads(d_mix)
    row_dot = jnp.einsum("qhe,qhe->hq", d_mix_heads.astype(F32), mixed)[..., None]
    d_values = jnp.einsum("hqk,qhe->khe", weights, d_mix_heads, preferred_element_type=F32)
    d_probs = jnp.einsum("qhe,khe->hqk", d_mix_heads, as_heads(values), preferred_element_type=F32)
    d_scores = (probs * (d_probs - row_dot)).astype(BF16)
    d_queries = (
        jnp.einsum("hqk,khe->qhe", d_scores, as_heads(keys), preferred_element_type=F32)
        * score_scale
    )
    d_keys = (
        jnp.einsum("hqk,qhe->khe", d_scores, as_heads(queries), preferred_element_type=F32)
        * score_scale
    )
    d_qkv = [d.reshape(length, feats).astype(BF16) for d in (d_queries, d_keys, d_values)]
    grad_b_qv = jnp.stack([jnp.sum(d.astype(F32), axis=0) for d in (d_qkv[0], d_qkv[2])])
    grad_w_qkv = jnp.stack([dot(normed_one, d, ((0,), (0,))) for d in d_qkv])
    d_norm_part = sum(dot(d_qkv[i], qkv_full[i], ((1,), (1,))) for i in range(3))
    grad_gain_one = jnp.sum(vhat_one * d_norm_part, axis=0)
    grad_bias_one = jnp.sum(d_norm_part, axis=0)
    d_norm_one = plane_sum(d_norm_part)
    vhat_own, scale_own = normalise(x_own)
    grad_rows = (d_residual + norm_grad(vhat_own, scale_own, gain_one * d_norm_one)).astype(BF16)
    grad_tokens = span_rows(grad_rows)

    def z_sum(full, axis):
        size = full.shape[axis] // z_count
        return scatter_sum(
            lambda r: lax.dynamic_slice_in_dim(full, (z_me ^ r) * size, size, axis), ("fsdp",)
        )

    def ctx_gather(owned, axis):
        return gather_ordered(owned.astype(BF16), CTX, axis).astype(F32)

    full_down = ctx_gather(z_sum(grad_w_down, 1), 0)
    full_up = ctx_gather(z_sum(grad_w_up, 0), 1)
    full_out = ctx_gather(z_sum(grad_w_out, 1), 0)
    full_qkv = jnp.swapaxes(ctx_gather(z_sum(grad_w_qkv, 1), 2), 0, 1)

    vec_grads = jnp.stack(
        [grad_gain_one, grad_bias_one, grad_b_out, grad_gain_two, grad_bias_two, grad_b_down]
    )
    small_grads = jnp.concatenate(
        [
            vec_grads.reshape(6, z_count, part).swapaxes(0, 1).reshape(z_count, -1),
            grad_b_qv.reshape(2, heads, z_count, HD // z_count)
            .transpose(2, 0, 1, 3)
            .reshape(z_count, -1),
            grad_b_up.reshape(up_rows, z_count, -1).transpose(1, 0, 2).reshape(z_count, -1),
        ],
        axis=1,
    )
    small_sum = z_sum(small_grads, 0)
    small_plane = gather_ordered(small_sum.astype(BF16), PLANE, 0).astype(F32)
    vec_sum = jnp.sum(small_plane[:, :v_size], axis=0).reshape(6, part)
    by_ctx = lax.dynamic_index_in_dim(
        small_plane.reshape(c_count, t_count, -1), t_me, 1, keepdims=False
    )
    full_bqv = (
        by_ctx[:, v_size : v_size + q_size]
        .reshape(c_count, 2, heads, HD // z_count)
        .swapaxes(0, 1)
        .reshape(b_qv.shape)
    )
    full_bup = by_ctx[:, v_size + q_size :].reshape(b_up.shape)
    return (
        output,
        grad_tokens,
        vec_sum[0],
        vec_sum[1],
        full_qkv,
        full_bqv,
        full_out,
        vec_sum[2],
        vec_sum[3],
        vec_sum[4],
        full_up,
        full_bup,
        full_down,
        vec_sum[5],
    )


def solution(mesh):
    fsdp, ctx, tp = (mesh.shape[a] for a in ("fsdp", "ctx", "tp"))
    split = Mesh(mesh.devices.reshape(fsdp, ctx // 2, 2, tp), ("fsdp", "y", "core", "tp"))
    rows = P("fsdp", CTX, None)
    shares = (
        P("fsdp"),
        P("fsdp"),
        P("fsdp", None, "tp"),
        P(None, "tp", "fsdp"),
        P("tp", "fsdp"),
        P("fsdp"),
        P("fsdp"),
        P("fsdp"),
        P("fsdp", "tp"),
        P("tp", "fsdp"),
        P("tp", "fsdp"),
        P("fsdp"),
    )
    return jax.shard_map(
        body,
        mesh=split,
        in_specs=(rows, P("fsdp", CTX), *shares, rows),
        out_specs=(rows, rows, *shares),
        check_vma=False,
    )
```

```python
import functools

import jax
import jax.numpy as jnp
import numpy as np
from jax import lax
from jax.experimental import pallas as pl
from jax.experimental.pallas import tpu as pltpu
from jax.sharding import Mesh
from jax.sharding import PartitionSpec as P

HD = 64
DOC_MOST = 512
EPSILON = 1e-05
NEGATIVE = -1e30
F32 = jnp.float32
BF16 = jnp.bfloat16

CTX = ("y", "core")
PLANE = ("y", "core", "tp")
CHIPS = ("y", "tp")


def size_of(axes):
    return int(np.prod([lax.axis_size(a) for a in axes]))


def index_of(axes):
    index = 0
    for a in axes:
        index = index * lax.axis_size(a) + lax.axis_index(a)
    return index


def swap(value, axes, bits):
    count = size_of(axes)
    return lax.ppermute(value, axes, [(i, i ^ bits) for i in range(count)])


def bits_of(axes):
    bits, at = [], 1
    for a in reversed(axes):
        mine = []
        while len(mine) < (lax.axis_size(a) - 1).bit_length():
            mine.append(at)
            at *= 2
        bits = mine + bits if a == "core" else bits + mine
    return bits


def masks_of(axes):
    bits = bits_of(axes)
    masks = [0]
    for r in range(1, size_of(axes)):
        low = r & -r
        masks.append(masks[r ^ low] | bits[low.bit_length() - 1])
    return masks


def gather_blocks(value, axes):
    blocks = [value]
    bits = bits_of(axes)
    for r in range(1, size_of(axes)):
        low = r & -r
        blocks.append(swap(blocks[r ^ low], axes, bits[low.bit_length() - 1]))
    return blocks


def positions(axes):
    me = index_of(axes)
    return jnp.stack([me ^ mask for mask in masks_of(axes)]).astype(jnp.int32)


def scatter_sum(pieces, axes):
    total = {r: piece for r, piece in enumerate(pieces)}
    for r in range(len(pieces) - 1, 0, -1):
        low = r & -r
        arrived = swap(total[r].astype(BF16), axes, low)
        total[r ^ low] = total[r ^ low].astype(F32) + arrived.astype(F32)
    return total[0]


def kernel_call(kernel, outs, scalars, arrays, scratch=(), flops=0, name=None, vmem=16):
    spec = pl.BlockSpec(memory_space=pltpu.VMEM)
    nbytes = sum(int(np.prod(a.shape)) * a.dtype.itemsize for a in list(arrays) + list(outs))
    return pl.pallas_call(
        kernel,
        out_shape=[jax.ShapeDtypeStruct(s.shape, s.dtype) for s in outs],
        in_specs=[pl.BlockSpec(memory_space=pltpu.SMEM)] * len(scalars) + [spec] * len(arrays),
        out_specs=[spec] * len(outs),
        scratch_shapes=list(scratch),
        compiler_params=pltpu.CompilerParams(vmem_limit_bytes=vmem << 20),
        cost_estimate=pl.CostEstimate(flops=flops, bytes_accessed=nbytes, transcendentals=0),
        name=name,
    )(*scalars, *arrays)


def shape(dims, dtype):
    return jax.ShapeDtypeStruct(tuple(dims), dtype)


NN = (((1,), (0,)), ((), ()))
NT = (((1,), (1,)), ((), ()))
TN = (((0,), (0,)), ((), ()))


def mm(a, b, dims):
    return lax.dot_general(a, b, dims, preferred_element_type=F32)


def rows_at(start, size, unit):
    return pl.ds(pl.multiple_of(start, unit), size)


def normalise(values):
    centred = values - jnp.mean(values, axis=-1, keepdims=True)
    variance = jnp.mean(centred * centred, axis=-1, keepdims=True)
    scale = lax.rsqrt(variance + EPSILON)
    return centred * scale, scale


def norm_grad(vhat, scale, weighted):
    return scale * (
        weighted
        - jnp.mean(weighted, axis=-1, keepdims=True)
        - vhat * jnp.mean(weighted * vhat, axis=-1, keepdims=True)
    )


def first_norm_kernel(count, pos, gain, bias, *refs):
    blocks, (normed, vhat_out) = refs[:count], refs[count:]
    span = blocks[0].shape[0]
    step = min(64, span)
    for r in range(count):

        def chunk(i, carry, r=r):
            at = i * step
            vhat, _ = normalise(blocks[r][pl.ds(pl.multiple_of(at, step), step), :].astype(F32))
            out = rows_at(pos[r] * span + at, step, step)
            vhat_out[out, :] = vhat.astype(BF16)
            normed[out, :] = (vhat * gain[...] + bias[...]).astype(BF16)
            return carry

        lax.fori_loop(0, span // step, chunk, 0)


def head_mask(width, head):
    lane = lax.broadcasted_iota(jnp.int32, (1, width), 1)
    return (lane // HD) == head


def attend_kernel(count, pos, normed, bias_qv, seg_row, seg_col, *refs):
    blocks, (qkv, weight, attn, k_heads, v_heads) = refs[:count], refs[count:]
    part, feats = blocks[0].shape[1], blocks[0].shape[2]
    length = normed.shape[0]
    heads = feats // HD
    tile = min(256, length)
    for r in range(count):
        where = rows_at(pos[r] * part, part, part)
        for k in range(3):
            weight[where, k * feats : (k + 1) * feats] = blocks[r][k]

    def project(i, carry):
        rows = rows_at(i * tile, tile, tile)
        out = mm(normed[rows, :], weight[...], NN)
        q = (out[:, :feats] + bias_qv[0:1, :]).astype(BF16)
        k = out[:, feats : 2 * feats].astype(BF16)
        v = (out[:, 2 * feats :] + bias_qv[1:2, :]).astype(BF16)
        qkv[rows, :feats] = q
        qkv[rows, feats : 2 * feats] = k
        qkv[rows, 2 * feats :] = v
        for h in range(heads):
            mask = head_mask(feats, h)
            k_heads[h, rows, :] = jnp.where(mask, k, jnp.zeros_like(k))
            v_heads[h, rows, :] = jnp.where(mask, v, jnp.zeros_like(v))
        return carry

    lax.fori_loop(0, length // tile, project, 0)
    back = -(-DOC_MOST // tile)
    for i in range(length // tile):
        first = max(0, i - back) * tile
        keys = (i + 1) * tile - first
        rows = slice(i * tile, (i + 1) * tile)
        q = qkv[rows, :feats] * BF16(HD ** (-0.5))
        q_pos = i * tile + lax.broadcasted_iota(jnp.int32, (tile, keys), 0)
        k_pos = first + lax.broadcasted_iota(jnp.int32, (tile, keys), 1)
        allowed = (k_pos <= q_pos) & (seg_col[rows, :] == seg_row[:, first : first + keys])

        def head(h, total):
            s = mm(q, k_heads[h, first : first + keys, :], NT)
            s = jnp.where(allowed, s, NEGATIVE)
            e = jnp.exp(s - jnp.max(s, axis=1, keepdims=True))
            p = e * (1.0 / jnp.sum(e, axis=1, keepdims=True))
            return total + mm(p.astype(BF16), v_heads[h, first : first + keys, :], NN)

        mixed = lax.fori_loop(0, heads, head, jnp.zeros((tile, feats), F32))
        attn[rows, :] = mixed.astype(BF16)


def out_norm_kernel(mates, others, attn, w_mates, w_others, x, vecs, residual, normed):
    own, copies = x.shape[0], normed.shape[0] // x.shape[0]
    feats = attn.shape[1]
    total = x[...].astype(F32) + vecs[2:3, :]
    for i in range(copies):
        rows = slice(i * feats, (i + 1) * feats)
        total += mm(attn[rows_at(mates[i] * own, own, own), :], w_mates[rows, :], NN)
        total += mm(attn[rows_at(others[i] * own, own, own), :], w_others[rows, :], NN)
    residual[...] = total
    vhat, _ = normalise(total)
    out = (vhat * vecs[3:4, :] + vecs[4:5, :]).astype(BF16)
    for i in range(copies):
        normed[i * own : (i + 1) * own, :] = out


def place_out_kernel(count, pos, *refs):
    blocks, (out,) = refs[:count], refs[count:]
    feats, part = blocks[0].shape
    for r in range(count):
        for i in range(out.shape[0] // feats):
            out[i * feats : (i + 1) * feats, rows_at(pos[r] * part, part, part)] = blocks[r][...]


def place_mlp_kernel(count, pos, *refs):
    blocks, (up, down) = refs[:count], refs[count:]
    part = blocks[0].shape[1]
    for r in range(count):
        where = rows_at(pos[r] * part, part, part)
        up[where, :] = blocks[r][0]
        down[where, :] = blocks[r][1]


def d_act_kernel(count, pos, down, *refs):
    blocks, (cot, d_act) = refs[:count], refs[count:]
    span = blocks[0].shape[0]
    for r in range(count):
        where = rows_at(pos[r] * span, span, span)
        cot[where, :] = blocks[r][...]
        d_act[where, :] = mm(blocks[r][...], down[...], NN)


def mlp_kernel(half, normed, up, bias_up, d_act, act, d_up, d_norm, grad_bias):
    count = normed.shape[0]
    step = min(256, count)

    def chunk(i, total):
        rows = rows_at(i * step, step, step)
        u = mm(normed[rows, :], up[...], NN) + bias_up[...]
        square = u * u
        th = jnp.tanh(0.7978845608028654 * (u + 0.044715 * square * u))
        act[rows, :] = (0.5 * u * (1.0 + th)).astype(BF16)
        slope = 0.5 * (1.0 + th) + 0.5 * u * (1.0 - th * th) * (
            0.7978845608028654 * (1.0 + 3.0 * 0.044715 * square)
        )
        g = (d_act[rows_at(half * count + i * step, step, step), :] * slope).astype(BF16)
        d_up[rows, :] = g
        d_norm[rows, :] = mm(g, up[...], NT).astype(BF16)
        return total + jnp.sum(g.astype(F32), axis=0, keepdims=True)

    grad_bias[...] = lax.fori_loop(0, count // step, chunk, jnp.zeros(bias_up.shape, F32))


def down_kernel(act_a, act_b, down, keep, give):
    step = min(256, act_a.shape[0])
    for act, out in ((act_b, give), (act_a, keep)):

        def chunk(i, carry, act=act, out=out):
            rows = rows_at(i * step, step, step)
            out[rows, :] = mm(act[rows, :], down[...], NT).astype(BF16)
            return carry

        lax.fori_loop(0, act.shape[0] // step, chunk, 0)


def mlp_grad_kernel(z_me, normed_a, normed_b, act_a, act_b, d_up_a, d_up_b, cot, out):
    count = act_a.shape[0]
    blocks, _, part, units = out.shape
    for r in range(blocks):
        cols = rows_at((z_me[0] ^ r) * part, part, part)
        up = mm(normed_a[:, cols], d_up_a[...], TN) + mm(normed_b[:, cols], d_up_b[...], TN)
        out[r, 0] = up.astype(BF16)
        down = mm(cot[0:count, cols], act_a[...], TN) + mm(cot[count:, cols], act_b[...], TN)
        out[r, 1] = down.astype(BF16)


def second_back_kernel(
    mates, others, landed, residual, cot, vecs, w_mates, w_others, d_res, branch, d_mix, grads
):
    own = residual.shape[0]
    copies = landed.shape[0] // own
    feats = d_mix.shape[1]
    d_norm = landed[0:own, :].astype(F32)
    for i in range(1, copies):
        d_norm += landed[i * own : (i + 1) * own, :].astype(F32)
    vhat, scale = normalise(residual[...])
    c = cot[...].astype(F32)
    d_residual = c + norm_grad(vhat, scale, vecs[3:4, :] * d_norm)
    d_res[...] = d_residual
    b = d_residual.astype(BF16)
    grads[0:1, :] = jnp.sum(d_residual, axis=0, keepdims=True)
    grads[1:2, :] = jnp.sum(vhat * d_norm, axis=0, keepdims=True)
    grads[2:3, :] = jnp.sum(d_norm, axis=0, keepdims=True)
    grads[3:4, :] = jnp.sum(c, axis=0, keepdims=True)
    for i in range(copies):
        rows = slice(i * feats, (i + 1) * feats)
        branch[i * own : (i + 1) * own, :] = b
        d_mix[rows_at(mates[i] * own, own, own), :] = mm(b, w_mates[rows, :], NT).astype(BF16)
        d_mix[rows_at(others[i] * own, own, own), :] = mm(b, w_others[rows, :], NT).astype(BF16)


def attend_back_kernel(qkv, d_mix, seg_row, seg_col, d_qkv, sums, k_heads, v_heads, q_heads, m_heads, dk, dv):
    length, feats = d_mix.shape
    heads = feats // HD
    tile = min(256, length)
    scale = HD ** (-0.5)

    def prepare(i, carry):
        rows = rows_at(i * tile, tile, tile)
        for h in range(heads):
            mask = head_mask(feats, h)
            for at, ref in ((0, q_heads), (1, k_heads), (2, v_heads)):
                part = qkv[rows, at * feats : (at + 1) * feats]
                if at == 0:
                    part = part * BF16(scale)
                ref[h, rows, :] = jnp.where(mask, part, jnp.zeros_like(part))
            m = d_mix[rows, :]
            m_heads[h, rows, :] = jnp.where(mask, m, jnp.zeros_like(m))
        dk[rows, :] = jnp.zeros((tile, feats), F32)
        dv[rows, :] = jnp.zeros((tile, feats), F32)
        return carry

    lax.fori_loop(0, length // tile, prepare, 0)
    back = -(-DOC_MOST // tile)
    for i in range(length // tile):
        first = max(0, i - back) * tile
        keys = (i + 1) * tile - first
        rows = slice(i * tile, (i + 1) * tile)
        span = slice(first, first + keys)
        k_pos = first + lax.broadcasted_iota(jnp.int32, (keys, tile), 0)
        q_pos = i * tile + lax.broadcasted_iota(jnp.int32, (keys, tile), 1)
        allowed = (k_pos <= q_pos) & (seg_col[span, :] == seg_row[:, rows])

        def head(h, dq):
            k, v, q, m = k_heads[h, span, :], v_heads[h, span, :], q_heads[h, rows, :], m_heads[h, rows, :]
            s = jnp.where(allowed, mm(k, q, NT), NEGATIVE)
            e = jnp.exp(s - jnp.max(s, axis=0, keepdims=True))
            p = e * (1.0 / jnp.sum(e, axis=0, keepdims=True))
            dp = mm(v, m, NT)
            row_dot = jnp.sum(p * dp, axis=0, keepdims=True)
            ds = (p * (dp - row_dot)).astype(BF16)
            dv[span, :] += mm(p.astype(BF16), m, NN)
            dk[span, :] += mm(ds, q, NN)
            return dq + mm(ds, k, TN)

        dq = lax.fori_loop(0, heads, head, jnp.zeros((tile, feats), F32))
        d_qkv[rows, :feats] = (dq * scale).astype(BF16)

    def finish(i, carry):
        rows = rows_at(i * tile, tile, tile)
        d_qkv[rows, feats : 2 * feats] = dk[rows, :].astype(BF16)
        d_qkv[rows, 2 * feats :] = dv[rows, :].astype(BF16)
        return carry + jnp.sum(d_qkv[rows, :].astype(F32), axis=0, keepdims=True)

    sums[...] = lax.fori_loop(0, length // tile, finish, jnp.zeros((1, 3 * feats), F32))


def first_back_kernel(unit, core, d_qkv, weight, vhat, keep, give, grads):
    total = (jnp.zeros((1, vhat.shape[1]), F32),) * 2
    for out, side in ((give, 1), (keep, 0)):

        def chunk(i, total, out=out, side=side):
            rows = rows_at((2 * i + (core[0] ^ side)) * unit, unit, unit)
            d = mm(d_qkv[rows, :], weight[...], NT)
            out[rows_at(i * unit, unit, unit), :] = d.astype(BF16)
            gain = jnp.sum(vhat[rows, :].astype(F32) * d, axis=0, keepdims=True)
            return total[0] + gain, total[1] + jnp.sum(d, axis=0, keepdims=True)

        total = lax.fori_loop(0, out.shape[0] // unit, chunk, total)
    grads[0:1, :] = total[0]
    grads[1:2, :] = total[1]


def attn_grad_kernel(z_me, order, normed, d_qkv, attn, branch_a, branch_b, out):
    blocks, _, part, feats = out.shape
    half = branch_a.shape[0]
    own = half // (order.shape[0] // 2)
    for r in range(blocks):
        cols = rows_at((z_me[0] ^ r) * part, part, part)
        g = mm(normed[:, cols], d_qkv[...], TN)
        for k in range(3):
            out[r, k] = g[:, k * feats : (k + 1) * feats].astype(BF16)
        total = jnp.zeros((part, feats), F32)
        for i in range(order.shape[0]):
            branch = branch_a if i * own < half else branch_b
            rows = slice(i * own % half, i * own % half + own)
            total += mm(branch[rows, cols], attn[rows_at(order[i] * own, own, own), :], TN)
        out[r, 3] = total.astype(BF16)


def last_kernel(landed, x, vecs, d_res, out):
    own = x.shape[0]
    d_norm = landed[0:own, :].astype(F32)
    for i in range(1, landed.shape[0] // own):
        d_norm += landed[i * own : (i + 1) * own, :].astype(F32)
    vhat, scale = normalise(x[...].astype(F32))
    out[...] = (d_res[...] + norm_grad(vhat, scale, vecs[0:1, :] * d_norm)).astype(BF16)


def output_kernel(landed, residual, vecs, out):
    own = residual.shape[0]
    total = residual[...] + vecs[5:6, :]
    for i in range(landed.shape[0] // own):
        total += landed[i * own : (i + 1) * own, :].astype(F32)
    out[...] = total.astype(BF16)


def pair_kernel(place, mine, other, out):
    own = mine.shape[0]
    out[rows_at(place[0] * own, own, own), :] = mine[...]
    out[rows_at((1 - place[0]) * own, own, own), :] = other[...]


def mlp_place_kernel(count, pos, *refs):
    blocks, (up, down) = refs[:count], refs[count:]
    units = blocks[0].shape[2]
    for r in range(count):
        at = rows_at(pos[r] * units, units, units)
        up[:, at] = blocks[r][0].astype(F32)
        down[at, :] = blocks[r][1].astype(F32).T


def attn_place_kernel(count, pos, *refs):
    blocks, (qkv, out) = refs[:count], refs[count:]
    feats = blocks[0].shape[2]
    for r in range(count):
        at = rows_at(pos[r] * feats, feats, feats)
        for k in range(3):
            qkv[k, :, at] = blocks[r][k].astype(F32)
        out[at, :] = blocks[r][3].astype(F32).T


def body(
    tokens,
    segments,
    ln1_gain,
    ln1_bias,
    w_qkv,
    b_qv,
    w_out,
    b_out,
    ln2_gain,
    ln2_bias,
    w_up,
    b_up,
    w_down,
    b_down,
    cotangent,
):
    z_count, z_me = lax.axis_size("fsdp"), lax.axis_index("fsdp")
    c_count, c_me = size_of(CTX), index_of(CTX)
    t_count, t_me = lax.axis_size("tp"), lax.axis_index("tp")
    y_count, y_me, core = lax.axis_size("y"), lax.axis_index("y"), lax.axis_index("core")
    chips = y_count * t_count
    span, width = tokens.shape[1], tokens.shape[2]
    length = span * c_count
    half = length // 2
    own = span // t_count
    feats = w_qkv.shape[2] // c_count
    heads = feats // HD
    units = w_up.shape[1] // c_count
    part = width // z_count
    z_pos = positions(("fsdp",))
    c_pos = positions(CTX)
    z_one = z_me.astype(jnp.int32).reshape(1)
    one = lambda v: v.astype(jnp.int32).reshape(1)
    chip_ids = [(y, t) for y in range(y_count) for t in range(t_count)]
    mates = jnp.stack([(y * 2 + core) * t_count + t for y, t in chip_ids]).astype(jnp.int32)
    others = jnp.stack([(y * 2 + 1 - core) * t_count + t for y, t in chip_ids]).astype(jnp.int32)

    qkv_own = lax.dynamic_slice_in_dim(jnp.swapaxes(w_qkv, 0, 1), c_me * feats, feats, 2)
    qkv_blocks = gather_blocks(qkv_own, ("fsdp",))
    bqv_own = lax.dynamic_slice_in_dim(b_qv, c_me * heads, heads, 1)
    up_rows = b_up.shape[0] // c_count
    bup_own = lax.dynamic_slice_in_dim(b_up, c_me * up_rows, up_rows, 0)
    small_own = jnp.concatenate(
        [ln1_gain, ln1_bias, b_out, ln2_gain, ln2_bias, b_down, bqv_own.reshape(-1), bup_own.reshape(-1)]
    )
    x_blocks = gather_blocks(tokens[0], CTX)
    small_blocks = gather_blocks(small_own[None], ("fsdp",))
    seg_blocks = gather_blocks(segments, CTX)
    out_own = lax.dynamic_slice_in_dim(w_out, c_me * feats, feats, 0)
    out_blocks = gather_blocks(out_own, ("fsdp",))
    up_own = lax.dynamic_slice_in_dim(w_up, c_me * units, units, 1)
    down_own = lax.dynamic_slice_in_dim(w_down, c_me * units, units, 0).T
    mlp_blocks = gather_blocks(jnp.stack([up_own, down_own]), ("fsdp",))
    cot_blocks = gather_blocks(cotangent[0], CTX)

    def ordered(blocks, pos):
        out = jnp.concatenate(blocks, axis=0)
        return jnp.stack(
            [lax.dynamic_index_in_dim(out, pos[r], 0, keepdims=False) for r in range(len(blocks))]
        )

    small_all = ordered(small_blocks, z_pos)
    c_masks = masks_of(CTX)
    c_back = jnp.stack(
        [sum(jnp.where(c_me ^ c == m, r, 0) for r, m in enumerate(c_masks)) for c in range(c_count)]
    )
    seg_full = ordered(seg_blocks, c_back)
    seg_row = seg_full.reshape(1, length)
    seg_col = seg_full.reshape(length, 1)

    v_size = 6 * part
    q_size = 2 * heads * (HD // z_count)
    vecs = small_all[:, :v_size].reshape(z_count, 6, part).swapaxes(0, 1).reshape(6, width).astype(F32)
    bias_qv = (
        small_all[:, v_size : v_size + q_size]
        .reshape(z_count, 2, heads, HD // z_count)
        .transpose(1, 2, 0, 3)
        .reshape(2, feats)
        .astype(F32)
    )
    bias_up = (
        small_all[:, v_size + q_size :]
        .reshape(z_count, up_rows, b_up.shape[1])
        .transpose(1, 0, 2)
        .reshape(1, units)
        .astype(F32)
    )

    normed_one, vhat_one = kernel_call(
        functools.partial(first_norm_kernel, c_count),
        [shape((length, width), BF16)] * 2,
        [c_pos],
        [vecs[0:1], vecs[1:2], *x_blocks],
        flops=10 * length * width,
        name="first_norm",
    )
    qkv, qkv_full, attn_mix = kernel_call(
        functools.partial(attend_kernel, z_count),
        [shape((length, 3 * feats), BF16), shape((width, 3 * feats), BF16), shape((length, feats), BF16)],
        [z_pos],
        [normed_one, bias_qv, seg_row, seg_col, *qkv_blocks],
        scratch=[pltpu.VMEM((heads, length, feats), BF16)] * 2,
        flops=2 * length * width * 3 * feats + 8 * length * length * feats,
        name="attend",
    )

    (out_part,) = kernel_call(
        functools.partial(place_out_kernel, z_count),
        [shape((chips * feats, width), BF16)],
        [z_pos],
        out_blocks,
        name="place_out",
    )
    out_mates = lax.all_to_all(out_part, CHIPS, 0, 0, tiled=True)
    out_others = swap(out_mates, CTX, 1)

    attn_rows = lax.all_to_all(attn_mix, PLANE, 0, 0, tiled=True)
    x_own = lax.dynamic_slice_in_dim(tokens[0], t_me * own, own, 0)
    cot_own = lax.dynamic_slice_in_dim(cotangent[0], t_me * own, own, 0)
    residual, normed_rep = kernel_call(
        out_norm_kernel,
        [shape((own, width), F32), shape((chips * own, width), BF16)],
        [mates, others],
        [attn_rows, out_mates, out_others, x_own, vecs],
        flops=2 * own * width * width,
        name="out_norm",
    )
    normed_a = lax.all_to_all(normed_rep, CHIPS, 0, 0, tiled=True)
    normed_b = swap(normed_a, CTX, 1)

    up_full, down_full = kernel_call(
        functools.partial(place_mlp_kernel, z_count),
        [shape((width, units), BF16)] * 2,
        [z_pos],
        mlp_blocks,
        name="place_mlp",
    )
    m_pos = jnp.stack([(m & 1) * y_count + (y_me ^ (m >> 1)) for m in c_masks]).astype(jnp.int32)
    cot_full, d_act = kernel_call(
        functools.partial(d_act_kernel, c_count),
        [shape((length, width), BF16), shape((length, units), F32)],
        [m_pos],
        [down_full, *cot_blocks],
        flops=2 * length * width * units,
        name="d_act",
    )

    def feed(side, normed):
        return kernel_call(
            functools.partial(mlp_kernel, side),
            [
                shape((half, units), BF16),
                shape((half, units), BF16),
                shape((half, width), BF16),
                shape((1, units), F32),
            ],
            [],
            [normed, up_full, bias_up, d_act],
            flops=4 * half * width * units,
            name="mlp",
        )

    act_a, d_up_a, keep_two, grad_bup_a = feed(0, normed_a)
    act_b, d_up_b, give_two, grad_bup_b = feed(1, normed_b)
    grad_b_up = grad_bup_a + grad_bup_b

    def plane_sum(keep, give):
        both = (keep.astype(F32) + swap(give, CTX, 1).astype(F32)).astype(BF16)
        return lax.all_to_all(both, CHIPS, 0, 0, tiled=True)

    landed_two = plane_sum(keep_two, give_two)
    keep_down, give_down = kernel_call(
        down_kernel,
        [shape((half, width), BF16)] * 2,
        [],
        [act_a, act_b, down_full],
        flops=2 * length * width * units,
        name="down",
    )
    (mlp_grads,) = kernel_call(
        mlp_grad_kernel,
        [shape((z_count, 2, part, units), BF16)],
        [z_one],
        [normed_a, normed_b, act_a, act_b, d_up_a, d_up_b, cot_full],
        flops=4 * length * width * units,
        name="mlp_grad",
    )
    landed_down = plane_sum(keep_down, give_down)
    (output_own,) = kernel_call(
        output_kernel,
        [shape((own, width), BF16)],
        [],
        [landed_down, residual, vecs],
        name="output",
    )

    def span_rows(rows):
        other = swap(rows, ("tp",), 1)
        (out,) = kernel_call(
            pair_kernel, [shape((span, width), BF16)], [one(t_me)], [rows, other], name="pair"
        )
        return out[None]

    output = span_rows(output_own)

    d_residual, branch_rep, d_mix_rows, grads_two = kernel_call(
        second_back_kernel,
        [
            shape((own, width), F32),
            shape((chips * own, width), BF16),
            shape((length, feats), BF16),
            shape((4, width), F32),
        ],
        [mates, others],
        [landed_two, residual, cot_own, vecs, out_mates, out_others],
        flops=2 * own * width * width,
        name="second_back",
    )
    d_mix = lax.all_to_all(d_mix_rows, PLANE, 0, 0, tiled=True)
    branch_a = lax.all_to_all(branch_rep, CHIPS, 0, 0, tiled=True)
    branch_b = swap(branch_a, CTX, 1)
    d_qkv, sums_qkv = kernel_call(
        attend_back_kernel,
        [shape((length, 3 * feats), BF16), shape((1, 3 * feats), F32)],
        [],
        [qkv, d_mix, seg_row, seg_col],
        scratch=[pltpu.VMEM((heads, length, feats), BF16)] * 4 + [pltpu.VMEM((length, feats), F32)] * 2,
        flops=20 * length * length * feats,
        name="attend_back",
    )
    keep_one, give_one, grads_one = kernel_call(
        functools.partial(first_back_kernel, span),
        [shape((half, width), BF16), shape((half, width), BF16), shape((2, width), F32)],
        [one(core)],
        [d_qkv, qkv_full, vhat_one],
        flops=2 * length * width * 3 * feats,
        name="first_back",
    )
    landed_one = plane_sum(keep_one, give_one)
    (attn_grads,) = kernel_call(
        attn_grad_kernel,
        [shape((z_count, 4, part, feats), BF16)],
        [z_one, jnp.concatenate([mates, others])],
        [normed_one, d_qkv, attn_mix, branch_a, branch_b],
        flops=2 * length * width * 4 * feats,
        name="attn_grad",
    )
    (grad_rows,) = kernel_call(
        last_kernel,
        [shape((own, width), BF16)],
        [],
        [landed_one, x_own, vecs, d_residual],
        name="last",
    )
    grad_tokens = span_rows(grad_rows)

    def z_sum(pieces):
        return scatter_sum([pieces[r] for r in range(z_count)], ("fsdp",))

    mlp_sum = gather_blocks(z_sum(mlp_grads).astype(BF16), CTX)
    full_up, full_down = kernel_call(
        functools.partial(mlp_place_kernel, c_count),
        [shape((part, c_count * units), F32), shape((c_count * units, part), F32)],
        [c_pos],
        mlp_sum,
        name="mlp_place",
    )
    attn_sum = gather_blocks(z_sum(attn_grads).astype(BF16), CTX)
    if feats % 128 == 0:
        full_qkv, full_out = kernel_call(
            functools.partial(attn_place_kernel, c_count),
            [shape((3, part, c_count * feats), F32), shape((c_count * feats, part), F32)],
            [c_pos],
            attn_sum,
            name="attn_place",
        )
    else:
        by_ctx = ordered([b[None] for b in attn_sum], c_back).astype(F32)
        full_qkv = by_ctx[:, :3].transpose(1, 2, 0, 3).reshape(3, part, c_count * feats)
        full_out = by_ctx[:, 3].swapaxes(1, 2).reshape(c_count * feats, part)

    vec_grads = jnp.concatenate([grads_one, grads_two])
    grad_b_qv = jnp.stack([sums_qkv[0, :feats], sums_qkv[0, 2 * feats :]])
    small_grads = jnp.concatenate(
        [
            vec_grads.reshape(6, z_count, part).swapaxes(0, 1).reshape(z_count, -1),
            grad_b_qv.reshape(2, heads, z_count, HD // z_count)
            .transpose(2, 0, 1, 3)
            .reshape(z_count, -1),
            grad_b_up.reshape(up_rows, z_count, -1).transpose(1, 0, 2).reshape(z_count, -1),
        ],
        axis=1,
    )
    pieces = [lax.dynamic_slice_in_dim(small_grads, z_pos[r], 1, 0) for r in range(z_count)]
    small_sum = scatter_sum(pieces, ("fsdp",)).astype(BF16)
    both_tp = small_sum.astype(F32) + swap(small_sum, ("tp",), 1).astype(F32)
    ctx_small = gather_blocks(jnp.concatenate([both_tp[:, :v_size].astype(BF16), small_sum[:, v_size:]], 1), CTX)
    ctx_small = ordered(ctx_small, c_back).astype(F32)
    vec_sum = jnp.sum(ctx_small[:, :v_size], axis=0).reshape(6, part)
    full_bqv = (
        ctx_small[:, v_size : v_size + q_size]
        .reshape(c_count, 2, heads, HD // z_count)
        .swapaxes(0, 1)
        .reshape(b_qv.shape)
    )
    full_bup = ctx_small[:, v_size + q_size :].reshape(b_up.shape)
    return (
        output,
        grad_tokens,
        vec_sum[0],
        vec_sum[1],
        jnp.swapaxes(full_qkv, 0, 1),
        full_bqv,
        full_out,
        vec_sum[2],
        vec_sum[3],
        vec_sum[4],
        full_up,
        full_bup,
        full_down,
        vec_sum[5],
    )


def solution(mesh):
    fsdp, ctx, tp = (mesh.shape[a] for a in ("fsdp", "ctx", "tp"))
    split = Mesh(mesh.devices.reshape(fsdp, ctx // 2, 2, tp), ("fsdp", "y", "core", "tp"))
    rows = P("fsdp", CTX, None)
    shares = (
        P("fsdp"),
        P("fsdp"),
        P("fsdp", None, "tp"),
        P(None, "tp", "fsdp"),
        P("tp", "fsdp"),
        P("fsdp"),
        P("fsdp"),
        P("fsdp"),
        P("fsdp", "tp"),
        P("tp", "fsdp"),
        P("tp", "fsdp"),
        P("fsdp"),
    )
    return jax.shard_map(
        body,
        mesh=split,
        in_specs=(rows, P("fsdp", CTX), *shares, rows),
        out_specs=(rows, rows, *shares),
        check_vma=False,
    )
```

```python
import functools

import jax
import jax.numpy as jnp
import numpy as np
from jax import lax
from jax.experimental import pallas as pl
from jax.experimental.pallas import tpu as pltpu
from jax.sharding import Mesh
from jax.sharding import PartitionSpec as P

HD = 64
DOC_MOST = 512
EPSILON = 1e-05
NEGATIVE = -1e30
F32 = jnp.float32
FLOPS_PER_US = 2e9
BF16 = jnp.bfloat16

CTX = ("y", "core")
PLANE = ("y", "core", "tp")
CHIPS = ("y", "tp")


def size_of(axes):
    return int(np.prod([lax.axis_size(a) for a in axes]))


def swap(value, axes, bits):
    count = size_of(axes)
    return lax.ppermute(value, axes, [(i, i ^ bits) for i in range(count)])


def masks_of(axes):
    bits, at = [], 1
    for a in reversed(axes):
        mine = []
        while len(mine) < (lax.axis_size(a) - 1).bit_length():
            mine.append(at)
            at *= 2
        bits = mine + bits if a == "core" else bits + mine
    masks = [0]
    for r in range(1, size_of(axes)):
        low = r & -r
        masks.append(masks[r ^ low] | bits[low.bit_length() - 1])
    return masks


def gather_blocks(value, axes):
    masks = masks_of(axes)
    blocks = [value]
    for r in range(1, len(masks)):
        low = r & -r
        blocks.append(swap(blocks[r ^ low], axes, masks[low]))
    return blocks


def to_chips(value):
    return [value] + [swap(value, CHIPS, m) for m in masks_of(CHIPS)[1:]]


def trade(pieces, axes):
    return [pieces[0]] + [swap(p, axes, m) for p, m in zip(pieces[1:], masks_of(axes)[1:])]


def after(value, *others):
    return lax.optimization_barrier((value, *others))[0]


def kernel_call(kernel, outs, ids, arrays, scratch=(), cost=1.0, name=None, vmem=12, deps=(), anys=()):
    deps = list(deps)
    extra = len(deps)

    def run(*refs):
        kernel(*refs[:1], *refs[1 + extra :])

    def place(space):
        return pl.BlockSpec(memory_space=space)

    return pl.pallas_call(
        run,
        out_shape=[jax.ShapeDtypeStruct(s.shape, s.dtype) for s in outs],
        in_specs=[place(pltpu.SMEM)]
        + [place(pl.ANY)] * extra
        + [place(pltpu.HBM)] * len(anys)
        + [place(pltpu.VMEM)] * len(arrays),
        out_specs=[place(pltpu.VMEM)] * len(outs),
        scratch_shapes=list(scratch),
        compiler_params=pltpu.CompilerParams(vmem_limit_bytes=vmem << 20),
        cost_estimate=pl.CostEstimate(
            flops=int(cost * FLOPS_PER_US), bytes_accessed=int(cost * 1e5), transcendentals=0
        ),
        name=name,
    )(ids, *deps, *[pltpu.with_memory_space_constraint(a, pltpu.HBM) for a in anys], *arrays)


def shape(dims, dtype=BF16):
    return jax.ShapeDtypeStruct(tuple(dims), dtype)


NN = (((1,), (0,)), ((), ()))
NT = (((1,), (1,)), ((), ()))
TN = (((0,), (0,)), ((), ()))


def mm(a, b, dims):
    return lax.dot_general(a, b, dims, preferred_element_type=F32)


def at(start, size, unit=None):
    return pl.ds(pl.multiple_of(start, unit or size), size)


def normalise(values):
    centred = values - jnp.mean(values, axis=-1, keepdims=True)
    variance = jnp.mean(centred * centred, axis=-1, keepdims=True)
    scale = lax.rsqrt(variance + EPSILON)
    return centred * scale, scale


def norm_grad(vhat, scale, weighted):
    return scale * (
        weighted
        - jnp.mean(weighted, axis=-1, keepdims=True)
        - vhat * jnp.mean(weighted * vhat, axis=-1, keepdims=True)
    )


class Ids:
    def __init__(self, ref, t_count):
        self.z, self.y, self.core, self.t = ref[0], ref[1], ref[2], ref[3]
        self.c = self.y * 2 + self.core
        self.p = self.c * t_count + self.t
        self.t_count = t_count

    def rows(self, side, mask, own):
        c = (self.y ^ (mask // self.t_count)) * 2 + (self.core ^ side)
        return at((c * self.t_count + (self.t ^ (mask % self.t_count))) * own, own)


def small_rows(part, heads, z_count, rows_up, cols_up, wide):
    vec = 6 * part // wide
    q = 2 * heads * (HD // z_count)
    u = rows_up * cols_up
    q_rows, u_rows = -(-q // wide), -(-u // wide)
    total = vec + q_rows + u_rows
    return vec, q, q_rows, u, u_rows, -(-total // 16) * 16


def pick(table, index):
    row = lax.broadcasted_iota(jnp.int32, table.shape, 0)
    return jnp.sum(jnp.where(row == index, table.astype(F32), 0.0), axis=0, keepdims=True).astype(BF16)


def lay_rows(out, first, pieces, wide):
    line, used = [], 0
    for piece in [*pieces, None]:
        if piece is None or used + piece.shape[1] > wide:
            if line:
                gap = wide - used
                if gap:
                    line.append(jnp.zeros((1, gap), line[0].dtype))
                out[first : first + 1, :] = jnp.concatenate(line, axis=1) if len(line) > 1 else line[0]
                first, line, used = first + 1, [], 0
        if piece is not None:
            line.append(piece)
            used += piece.shape[1]


def pack_kernel(cfg, ids_ref, w_qkv, w_out, x, seg, cot, *refs):
    params, (out, rows, cot_half, cot_both) = refs[:8], refs[8:12]
    buf, seg_buf, bufs, sems = refs[12], refs[13], refs[14:22], refs[22]
    c, t = ids_ref[1] * 2 + ids_ref[2], ids_ref[3]
    feats = out.shape[1]
    part = w_out.shape[1]
    span, own = x.shape[0], cot_half.shape[0]
    pairs = [
        (w_qkv.at[k, :, at(c * feats, feats)], out.at[k * part : (k + 1) * part, :]) for k in range(3)
    ]
    pairs.append((w_out.at[at(c * feats, feats), :], buf))
    pairs += list(zip(params, bufs))
    pairs += [(seg, seg_buf)]
    pairs += [(x, rows.at[:span, :])]
    pairs += [
        (cot.at[at(t * own, own), :], cot_half),
        (cot.at[at(t * own, own), :], cot_both.at[:own, :]),
        (cot.at[at((1 - t) * own, own), :], cot_both.at[own:, :]),
    ]
    copies = [pltpu.make_async_copy(a, b, sems.at[i]) for i, (a, b) in enumerate(pairs)]
    for copy in copies:
        copy.start()
    rows[span:, :] = jnp.zeros((rows.shape[0] - span, rows.shape[1]), rows.dtype)
    for copy in copies[3:13]:
        copy.wait()
    out[3 * part : 4 * part, :] = buf[...].T
    pack_small(cfg, c, bufs[:6], bufs[6], bufs[7], out, 4 * part)
    rows[span : span + 1, :span] = seg_buf[...].astype(F32).astype(BF16)
    for copy in copies[:3] + copies[13:]:
        copy.wait()


def pack_plain_kernel(cfg, ids_ref, w_qkv, w_out, *refs):
    z_count, heads, rows_up, cols_up = cfg
    vectors, (b_qv, b_up, out) = refs[:6], refs[6:]
    part = w_out.shape[1]
    for k in range(3):
        out[k * part : (k + 1) * part, :] = w_qkv[k]
    out[3 * part : 4 * part, :] = w_out[...].T
    pack_small(cfg, ids_ref[1] * 2 + ids_ref[2], vectors, b_qv, b_up, out, 4 * part)


def pack_small(cfg, c, vectors, b_qv, b_up, out, base):
    z_count, heads, rows_up, cols_up = cfg
    wide = out.shape[1]
    part = vectors[0].shape[-1]
    vec, q, q_rows, u, u_rows, total = small_rows(part, heads, z_count, rows_up, cols_up, wide)
    out[base : base + total, :] = jnp.zeros((total, wide), out.dtype)
    per = part // wide
    for i, ref in enumerate(vectors):
        line = ref[...].reshape(1, part)
        for j in range(per):
            row = base + i * per + j
            out[row : row + 1, :] = line[:, j * wide : (j + 1) * wide]
    q_lines = [pick(b_qv[k], c * heads + h) for k in range(2) for h in range(heads)]
    lay_rows(out, base + vec, q_lines, wide)
    lay_rows(out, base + vec + q_rows, [pick(b_up[...], c * rows_up + i) for i in range(rows_up)], wide)


def pack_tokens_kernel(ids_ref, x, seg, out):
    span, width = x.shape
    out[:span, :] = x[...]
    out[span:, :] = jnp.zeros((out.shape[0] - span, width), out.dtype)
    out[span : span + 1, :span] = seg[...].astype(F32).astype(BF16)


def first_norm_kernel(cfg, ids_ref, *refs):
    c_masks, t_count, span = cfg
    me = Ids(ids_ref, t_count)
    x, (vhat_out, seg_row, seg_col) = refs[: len(c_masks)], refs[len(c_masks) :]
    for r, mask in enumerate(c_masks):
        seg_row[:, at((me.c ^ mask) * span, span)] = x[r][span : span + 1, :span].astype(F32)
    for i in range(seg_row.shape[1] // 128):
        block = jnp.broadcast_to(seg_row[:, i * 128 : (i + 1) * 128], (128, 128))
        seg_col[i * 128 : (i + 1) * 128, :] = block.T
    step = min(64, span)
    for r, mask in enumerate(c_masks):

        def chunk(i, carry, r=r, mask=mask):
            vhat, _ = normalise(x[r][at(i * step, step), :].astype(F32))
            vhat_out[at((me.c ^ mask) * span + i * step, step), :] = vhat
            return carry

        lax.fori_loop(0, span // step, chunk, 0)


def unpack_kernel(cfg, ids_ref, *refs):
    z_count, heads, rows_up, cols_up = cfg
    small, (weight, out_w, vecs, bias_qv, bias_up) = refs[:z_count], refs[z_count:]
    width = weight.shape[0]
    part = width // z_count
    feats = bias_qv.shape[1]
    units = bias_up.shape[1]
    each = HD // z_count
    wide = small[0].shape[1]
    vec, q, q_rows, u, u_rows, total = small_rows(part, heads, z_count, rows_up, cols_up, wide)
    base = 4 * part
    per = part // wide
    qv = [jnp.zeros((1, feats), F32), jnp.zeros((1, feats), F32)]
    ups = jnp.zeros((1, units), F32)
    if wide % 128:
        vecs[...] = jnp.zeros(vecs.shape, F32)
    for r in range(z_count):
        z = ids_ref[0] ^ r
        where = at(z * part, part)
        for k in range(3):
            weight[where, k * feats : (k + 1) * feats] = small[r][k * part : (k + 1) * part, :]
        out_w[where, :] = small[r][3 * part : 4 * part, :]
        for i in range(6):
            for j in range(per):
                row = base + i * per + j
                line = small[r][row : row + 1, :]
                if wide % 128 == 0:
                    vecs[i : i + 1, at(z * part + j * wide, wide)] = line.astype(F32)
                else:
                    lane = lax.broadcasted_iota(jnp.int32, (wide, width), 0)
                    goal = lax.broadcasted_iota(jnp.int32, (wide, width), 1)
                    move = jnp.where(goal == z * part + j * wide + lane, 1.0, 0.0).astype(BF16)
                    vecs[i : i + 1, :] += mm(line, move, NN)
        lane = lax.broadcasted_iota(jnp.int32, (wide, feats), 0)
        goal = lax.broadcasted_iota(jnp.int32, (wide, feats), 1)
        for k in range(2):
            for i in range(q_rows):
                place = lane + i * wide - k * heads * each
                move = (place >= 0) & (place < heads * each)
                move &= goal == (place // each) * HD + z * each + place % each
                row = base + vec + i
                qv[k] += mm(small[r][row : row + 1, :], jnp.where(move, 1.0, 0.0).astype(BF16), NN)
        lane = lax.broadcasted_iota(jnp.int32, (wide, units), 0)
        goal = lax.broadcasted_iota(jnp.int32, (wide, units), 1)
        for i in range(u_rows):
            place = lane + i * wide
            move = (place < u) & (goal == (place // cols_up) * 128 + z * cols_up + place % cols_up)
            row = base + vec + q_rows + i
            ups += mm(small[r][row : row + 1, :], jnp.where(move, 1.0, 0.0).astype(BF16), NN)
    for k in range(2):
        bias_qv[k : k + 1, :] = qv[k]
    bias_up[...] = ups


def head_mask(width, head):
    lane = lax.broadcasted_iota(jnp.int32, (1, width), 1)
    return (lane // HD) == head


def attend_kernel(
    cfg, ids_ref, vhat, weight, vecs, bias_qv, seg_row, seg_col, normed, qkv, attn, keep, give, k_heads, v_heads
):
    chip_masks, t_count = cfg
    me = Ids(ids_ref, t_count)
    length, feats = attn.shape
    heads = feats // HD
    tile = min(256, length)

    def project(i, carry):
        rows = at(i * tile, tile)
        x = (vhat[rows, :] * vecs[0:1, :] + vecs[1:2, :]).astype(BF16)
        normed[rows, :] = x
        out = mm(x, weight[...], NN)
        q = (out[:, :feats] + bias_qv[0:1, :]).astype(BF16)
        k = out[:, feats : 2 * feats].astype(BF16)
        v = (out[:, 2 * feats :] + bias_qv[1:2, :]).astype(BF16)
        qkv[rows, :feats] = q
        qkv[rows, feats : 2 * feats] = k
        qkv[rows, 2 * feats :] = v
        for h in range(heads):
            mask = head_mask(feats, h)
            k_heads[h, rows, :] = jnp.where(mask, k, jnp.zeros_like(k))
            v_heads[h, rows, :] = jnp.where(mask, v, jnp.zeros_like(v))
        return carry

    lax.fori_loop(0, length // tile, project, 0)
    back = -(-DOC_MOST // tile)
    for i in range(length // tile):
        first = max(0, i - back) * tile
        keys = (i + 1) * tile - first
        rows = slice(i * tile, (i + 1) * tile)
        q = qkv[rows, :feats] * BF16(HD ** (-0.5))
        q_pos = i * tile + lax.broadcasted_iota(jnp.int32, (tile, keys), 0)
        k_pos = first + lax.broadcasted_iota(jnp.int32, (tile, keys), 1)
        allowed = (k_pos <= q_pos) & (seg_col[rows, 0:1] == seg_row[:, first : first + keys])

        def head(h, total):
            s = mm(q, k_heads[h, first : first + keys, :], NT)
            s = jnp.where(allowed, s, NEGATIVE)
            e = jnp.exp(s - jnp.max(s, axis=1, keepdims=True))
            p = e * (1.0 / jnp.sum(e, axis=1, keepdims=True))
            return total + mm(p.astype(BF16), v_heads[h, first : first + keys, :], NN)

        mixed = lax.fori_loop(0, heads, head, jnp.zeros((tile, feats), F32))
        attn[rows, :] = mixed.astype(BF16)
    own = keep.shape[0] // len(chip_masks)
    for side, out in ((1, give), (0, keep)):
        for k in range(len(chip_masks)):
            out[k * own : (k + 1) * own, :] = attn[me.rows(side, chip_masks[k], own), :]


def cat_kernel(ids_ref, *refs):
    rows = refs[0].shape[0]
    for k, ref in enumerate(refs[:-1]):
        refs[-1][k * rows : (k + 1) * rows, :] = ref[...]


def beside_kernel(ids_ref, keep, landed, *pieces):
    own, both = pieces[0].shape
    for k, piece in enumerate(pieces):
        rows = slice(k * own, (k + 1) * own)
        piece[:, : both // 2] = keep[rows, :]
        piece[:, both // 2 :] = landed[rows, :]


def apart_kernel(ids_ref, *refs):
    pieces, out = refs[:-1], refs[-1]
    own, feats = pieces[0].shape[0], out.shape[1]
    for k, piece in enumerate(pieces):
        out[k * own : (k + 1) * own, :] = piece[:, feats:]


def out_norm_kernel(t_count, ids_ref, *refs):
    me = Ids(ids_ref, t_count)
    w_mine, w_other, x, vecs, residual, normed = refs[-6:]
    own, width = residual.shape
    feats = w_mine.shape[1]
    total = x[at(me.t * own, own), :].astype(F32) + vecs[2:3, :]
    for k, piece in enumerate(refs[:-6]):
        rows = slice(k * width, (k + 1) * width)
        total += mm(piece[:, :feats], w_mine[rows, :], NT) + mm(piece[:, feats:], w_other[rows, :], NT)
    residual[...] = total
    vhat, _ = normalise(total)
    normed[...] = (vhat * vecs[3:4, :] + vecs[4:5, :]).astype(BF16)


def place_kernel(ids_ref, *refs):
    blocks, out = refs[:-1], refs[-1]
    part = blocks[0].shape[0]
    for r, block in enumerate(blocks):
        out[at((ids_ref[0] ^ r) * part, part), :] = block[...]


def cut_mlp_kernel(ids_ref, w_up, w_down, up, down, buf, sems):
    c = ids_ref[1] * 2 + ids_ref[2]
    units = up.shape[1]
    one = pltpu.make_async_copy(w_up.at[:, at(c * units, units)], up, sems.at[0])
    two = pltpu.make_async_copy(w_down.at[at(c * units, units), :], buf, sems.at[1])
    one.start()
    two.start()
    two.wait()
    down[...] = buf[...].T
    one.wait()


def cot_kernel(chip_masks, t_count, ids_ref, *refs):
    both, pieces, cot = refs[:2], refs[2:-1], refs[-1]
    chips = len(chip_masks)
    own = cot.shape[0] // (2 * chips)
    for side in range(2):
        for k, mask in enumerate(chip_masks):
            to = (side * chips + k) * own
            y, t = mask // t_count, mask % t_count
            if y == 0:
                cot[to : to + own, :] = both[side][t * own : (t + 1) * own, :]
            else:
                cot[to : to + own, :] = pieces[((y - 1) * t_count + t) * 2 + side][...]


def hidden_kernel(ids_ref, normed_a, normed_b, up, bias_up, act_a, act_b, slope_a, slope_b):
    step = min(256, normed_a.shape[0])
    for normed, act, slope in ((normed_a, act_a, slope_a), (normed_b, act_b, slope_b)):

        def chunk(i, carry, normed=normed, act=act, slope=slope):
            rows = at(i * step, step)
            u = mm(normed[rows, :], up[...], NN) + bias_up[...]
            square = u * u
            th = jnp.tanh(0.7978845608028654 * (u + 0.044715 * square * u))
            act[rows, :] = (0.5 * u * (1.0 + th)).astype(BF16)
            slope[rows, :] = 0.5 * (1.0 + th) + 0.5 * u * (1.0 - th * th) * (
                0.7978845608028654 * (1.0 + 3.0 * 0.044715 * square)
            )
            return carry

        lax.fori_loop(0, normed.shape[0] // step, chunk, 0)


def hidden_back_kernel(side, ids_ref, slope, cot, down, up, d_up, d_norm, grad_bias):
    half = slope.shape[0]
    step = min(256, half)

    def chunk(i, total):
        rows = at(i * step, step)
        d_act = mm(cot[at(side * half + i * step, step), :], down[...], NN)
        g = (d_act * slope[rows, :]).astype(BF16)
        d_up[rows, :] = g
        d_norm[rows, :] = mm(g, up[...], NT).astype(BF16)
        return total + jnp.sum(g.astype(F32), axis=0, keepdims=True)

    grad_bias[...] = lax.fori_loop(0, half // step, chunk, jnp.zeros(grad_bias.shape, F32))


def down_kernel(ids_ref, act_a, act_b, down, keep, give):
    step = min(256, act_a.shape[0])
    for act, out in ((act_b, give), (act_a, keep)):

        def chunk(i, carry, act=act, out=out):
            rows = at(i * step, step)
            out[rows, :] = mm(act[rows, :], down[...], NT).astype(BF16)
            return carry

        lax.fori_loop(0, act.shape[0] // step, chunk, 0)


def join_kernel(ids_ref, keep, landed, *pieces):
    own = pieces[0].shape[0]
    for k, piece in enumerate(pieces):
        rows = slice(k * own, (k + 1) * own)
        piece[...] = (keep[rows, :].astype(F32) + landed[rows, :].astype(F32)).astype(BF16)


def add_kernel(ids_ref, *refs):
    total = refs[0][...].astype(F32)
    for ref in refs[1:-1]:
        total += ref[...].astype(F32)
    refs[-1][...] = total.astype(refs[-1].dtype)


def mlp_grad_kernel(ids_ref, normed_a, normed_b, act_a, act_b, d_up_a, d_up_b, cot, *outs):
    count = act_a.shape[0]
    part = outs[0].shape[0] // 2
    for r in range(len(outs) - 1, -1, -1):
        cols = at((ids_ref[0] ^ r) * part, part)
        up = mm(normed_a[:, cols], d_up_a[...], TN) + mm(normed_b[:, cols], d_up_b[...], TN)
        outs[r][:part, :] = up.astype(BF16)
        down = mm(cot[0:count, cols], act_a[...], TN) + mm(cot[count:, cols], act_b[...], TN)
        outs[r][part:, :] = down.astype(BF16)


def second_back_kernel(cfg, ids_ref, *refs):
    chips = cfg
    landed, refs = refs[:chips], refs[chips:]
    residual, cot, vecs, w_mine, w_other, d_res, branch, grads = refs[:8]
    d_mix = refs[8:]
    own, width = residual.shape
    feats = w_mine.shape[1]
    d_norm = landed[0][...].astype(F32)
    for ref in landed[1:]:
        d_norm += ref[...].astype(F32)
    vhat, scale = normalise(residual[...])
    c = cot[...].astype(F32)
    d_residual = c + norm_grad(vhat, scale, vecs[3:4, :] * d_norm)
    d_res[...] = d_residual
    b = d_residual.astype(BF16)
    branch[...] = b
    for k, piece in enumerate(d_mix):
        rows = slice(k * width, (k + 1) * width)
        piece[:, :feats] = mm(b, w_mine[rows, :], NN).astype(BF16)
        piece[:, feats:] = mm(b, w_other[rows, :], NN).astype(BF16)
    grads[0:1, :] = jnp.sum(d_residual, axis=0, keepdims=True)
    grads[1:2, :] = jnp.sum(vhat * d_norm, axis=0, keepdims=True)
    grads[2:3, :] = jnp.sum(d_norm, axis=0, keepdims=True)
    grads[3:4, :] = jnp.sum(c, axis=0, keepdims=True)


def attend_back_kernel(cfg, ids_ref, qkv, seg_row, seg_col, *refs):
    chip_masks, t_count = cfg
    me = Ids(ids_ref, t_count)
    mixes, refs = refs[: len(chip_masks)], refs[len(chip_masks) :]
    landed, d_qkv, sums, k_heads, v_heads, q_heads, m_heads, dk, dv = refs
    length, feats = qkv.shape[0], dk.shape[1]
    own = mixes[0].shape[0]
    heads = feats // HD
    tile = min(256, length)
    scale = HD ** (-0.5)
    for h in range(heads):
        mask = head_mask(feats, h)
        for k, m in enumerate(chip_masks):
            piece = mixes[k][:, :feats]
            m_heads[h, me.rows(0, m, own), :] = jnp.where(mask, piece, jnp.zeros_like(piece))
            piece = landed[k * own : (k + 1) * own, :]
            m_heads[h, me.rows(1, m, own), :] = jnp.where(mask, piece, jnp.zeros_like(piece))

    def prepare(i, carry):
        rows = at(i * tile, tile)
        for h in range(heads):
            mask = head_mask(feats, h)
            for k, ref in ((0, q_heads), (1, k_heads), (2, v_heads)):
                piece = qkv[rows, k * feats : (k + 1) * feats]
                if k == 0:
                    piece = piece * BF16(scale)
                ref[h, rows, :] = jnp.where(mask, piece, jnp.zeros_like(piece))
        dk[rows, :] = jnp.zeros((tile, feats), F32)
        dv[rows, :] = jnp.zeros((tile, feats), F32)
        return carry

    lax.fori_loop(0, length // tile, prepare, 0)
    back = -(-DOC_MOST // tile)
    for i in range(length // tile):
        first = max(0, i - back) * tile
        keys = (i + 1) * tile - first
        rows = slice(i * tile, (i + 1) * tile)
        span = slice(first, first + keys)
        k_pos = first + lax.broadcasted_iota(jnp.int32, (keys, tile), 0)
        q_pos = i * tile + lax.broadcasted_iota(jnp.int32, (keys, tile), 1)
        allowed = (k_pos <= q_pos) & (seg_col[span, 0:1] == seg_row[:, rows])

        def head(h, dq):
            k, v, q, m = k_heads[h, span, :], v_heads[h, span, :], q_heads[h, rows, :], m_heads[h, rows, :]
            s = jnp.where(allowed, mm(k, q, NT), NEGATIVE)
            e = jnp.exp(s - jnp.max(s, axis=0, keepdims=True))
            p = e * (1.0 / jnp.sum(e, axis=0, keepdims=True))
            dp = mm(v, m, NT)
            row_dot = jnp.sum(p * dp, axis=0, keepdims=True)
            ds = (p * (dp - row_dot)).astype(BF16)
            dv[span, :] += mm(p.astype(BF16), m, NN)
            dk[span, :] += mm(ds, q, NN)
            return dq + mm(ds, k, TN)

        dq = lax.fori_loop(0, heads, head, jnp.zeros((tile, feats), F32))
        d_qkv[rows, :feats] = (dq * scale).astype(BF16)

    def finish(i, carry):
        rows = at(i * tile, tile)
        d_qkv[rows, feats : 2 * feats] = dk[rows, :].astype(BF16)
        d_qkv[rows, 2 * feats :] = dv[rows, :].astype(BF16)
        return carry + jnp.sum(d_qkv[rows, :].astype(F32), axis=0, keepdims=True)

    sums[...] = lax.fori_loop(0, length // tile, finish, jnp.zeros((1, 3 * feats), F32))


def first_back_kernel(cfg, ids_ref, d_qkv, weight, vhat, keep, give, grads):
    chip_masks, own, t_count = cfg
    me = Ids(ids_ref, t_count)
    gain = jnp.zeros((1, vhat.shape[1]), F32)
    bias = gain
    for out, side in ((give, 1), (keep, 0)):
        for k, mask in enumerate(chip_masks):
            rows = me.rows(side, mask, own)
            d = mm(d_qkv[rows, :], weight[...], NT)
            out[k * own : (k + 1) * own, :] = d.astype(BF16)
            gain += jnp.sum(vhat[rows, :] * d, axis=0, keepdims=True)
            bias += jnp.sum(d, axis=0, keepdims=True)
    grads[0:1, :] = gain
    grads[1:2, :] = bias


def attn_grad_kernel(cfg, ids_ref, normed, d_qkv, attn, branch_a, branch_b, small, *refs):
    chip_masks, t_count = cfg
    me = Ids(ids_ref, t_count)
    outs, branch = refs[:-1], refs[-1]
    own = branch_a.shape[0] // len(chip_masks)
    for side, ref in ((0, branch_a), (1, branch_b)):
        for k, mask in enumerate(chip_masks):
            branch[me.rows(side, mask, own), :] = ref[k * own : (k + 1) * own, :]
    count = small.shape[0] // len(outs)
    feats = outs[0].shape[1]
    part = (outs[0].shape[0] - count) // 4
    for r in range(len(outs) - 1, -1, -1):
        cols = at((me.z ^ r) * part, part)
        g = mm(normed[:, cols], d_qkv[...], TN)
        for k in range(3):
            outs[r][k * part : (k + 1) * part, :] = g[:, k * feats : (k + 1) * feats].astype(BF16)
        outs[r][3 * part : 4 * part, :] = mm(branch[:, cols], attn[...], TN).astype(BF16)
        outs[r][4 * part :, :] = small[r * count : (r + 1) * count, :]


def last_kernel(t_count, ids_ref, *refs):
    me = Ids(ids_ref, t_count)
    x, vecs, d_res, out = refs[-4:]
    own = out.shape[0]
    d_norm = refs[0][...].astype(F32)
    for ref in refs[1:-4]:
        d_norm += ref[...].astype(F32)
    vhat, scale = normalise(x[at(me.t * own, own), :].astype(F32))
    out[...] = (d_res[...] + norm_grad(vhat, scale, vecs[0:1, :] * d_norm)).astype(BF16)


def output_kernel(ids_ref, *refs):
    residual, vecs, out = refs[-3:]
    total = residual[...] + vecs[5:6, :]
    for ref in refs[:-3]:
        total += ref[...].astype(F32)
    out[...] = total.astype(BF16)


def pair_kernel(ids_ref, mine, other, out):
    own = mine.shape[0]
    out[at(ids_ref[3] * own, own), :] = mine[...]
    out[at((1 - ids_ref[3]) * own, own), :] = other[...]


def small_grad_kernel(cfg, ids_ref, one, two, sums, bup_a, bup_b, out):
    z_count, heads, rows_up, cols_up = cfg
    width = one.shape[1]
    part = width // z_count
    feats = sums.shape[1] // 3
    units = bup_a.shape[1]
    each = HD // z_count
    wide = out.shape[1]
    vec, q, q_rows, u, u_rows, total = small_rows(part, heads, z_count, rows_up, cols_up, wide)
    per = part // wide
    bqv = (sums[:, :feats].astype(BF16), sums[:, 2 * feats :].astype(BF16))
    bup = (bup_a[...] + bup_b[...]).astype(BF16)
    out[...] = jnp.zeros(out.shape, out.dtype)
    for r in range(z_count):
        z = ids_ref[0] ^ r
        base = r * total
        for i in range(6):
            ref, row = (one, i) if i < 2 else (two, i - 2)
            for j in range(per):
                k = base + i * per + j
                if wide % 128 == 0:
                    out[k : k + 1, :] = ref[row : row + 1, at(z * part + j * wide, wide)].astype(BF16)
                else:
                    lane = lax.broadcasted_iota(jnp.int32, (wide, width), 0)
                    goal = lax.broadcasted_iota(jnp.int32, (wide, width), 1)
                    move = jnp.where(goal == z * part + j * wide + lane, 1.0, 0.0).astype(BF16)
                    out[k : k + 1, :] = mm(ref[row : row + 1, :].astype(BF16), move, NT).astype(BF16)
        lane = lax.broadcasted_iota(jnp.int32, (wide, feats), 0)
        goal = lax.broadcasted_iota(jnp.int32, (wide, feats), 1)
        for i in range(q_rows):
            line = jnp.zeros((1, wide), F32)
            for k in range(2):
                place = lane + i * wide - k * heads * each
                move = (place >= 0) & (place < heads * each)
                move &= goal == (place // each) * HD + z * each + place % each
                line += mm(bqv[k], jnp.where(move, 1.0, 0.0).astype(BF16), NT)
            out[base + vec + i : base + vec + i + 1, :] = line.astype(BF16)
        lane = lax.broadcasted_iota(jnp.int32, (wide, units), 0)
        goal = lax.broadcasted_iota(jnp.int32, (wide, units), 1)
        for i in range(u_rows):
            place = lane + i * wide
            move = (place < u) & (goal == (place // cols_up) * 128 + z * cols_up + place % cols_up)
            row = base + vec + q_rows + i
            out[row : row + 1, :] = mm(bup, jnp.where(move, 1.0, 0.0).astype(BF16), NT).astype(BF16)


def mlp_place_kernel(c_masks, ids_ref, *refs):
    blocks, (up, down) = refs[:-2], refs[-2:]
    c = ids_ref[1] * 2 + ids_ref[2]
    units = blocks[0].shape[1]
    part = blocks[0].shape[0] // 2
    for r, mask in enumerate(c_masks):
        where = at((c ^ mask) * units, units)
        up[:, where] = blocks[r][:part, :].astype(F32)
        down[where, :] = blocks[r][part:, :].astype(F32).T


def attn_place_kernel(cfg, ids_ref, *refs):
    c_masks, heads, rows_up, vec, q_rows = cfg
    blocks = refs[: len(c_masks)]
    qkv, out, vecs, b_qv, b_up = refs[len(c_masks) :]
    c = ids_ref[1] * 2 + ids_ref[2]
    wide = blocks[0].shape[1]
    part = vecs.shape[1]
    each, cols_up = b_qv.shape[2], b_up.shape[1]
    aligned = wide % 128 == 0
    for r, mask in enumerate(c_masks):
        where = at((c ^ mask) * wide, wide)
        if aligned:
            for k in range(3):
                qkv[k, :, where] = blocks[r][k * part : (k + 1) * part, :].astype(F32)
        else:
            for k in range(3):
                qkv[c ^ mask, k] = blocks[r][k * part : (k + 1) * part, :].astype(F32)
        out[where, :] = blocks[r][3 * part : 4 * part, :].astype(F32).T
        base = 4 * part + vec
        for k in range(2):
            for h in range(heads):
                flat = (k * heads + h) * each
                row, lane = base + flat // wide, flat % wide
                b_qv[k, pl.ds((c ^ mask) * heads + h, 1), :] = blocks[r][
                    row : row + 1, lane : lane + each
                ].astype(F32)
        for i in range(rows_up):
            row, lane = base + q_rows + (i * cols_up) // wide, (i * cols_up) % wide
            b_up[pl.ds((c ^ mask) * rows_up + i, 1), :] = blocks[r][
                row : row + 1, lane : lane + cols_up
            ].astype(F32)
    total = blocks[0][4 * part : 4 * part + vec, :].astype(F32)
    for block in blocks[1:]:
        total += block[4 * part : 4 * part + vec, :].astype(F32)
    per = part // wide
    for i in range(6):
        for j in range(per):
            vecs[i : i + 1, j * wide : (j + 1) * wide] = total[i * per + j : i * per + j + 1, :]


def body(
    tokens,
    segments,
    ln1_gain,
    ln1_bias,
    w_qkv,
    b_qv,
    w_out,
    b_out,
    ln2_gain,
    ln2_bias,
    w_up,
    b_up,
    w_down,
    b_down,
    cotangent,
):
    z_count, t_count, y_count = (lax.axis_size(a) for a in ("fsdp", "tp", "y"))
    z_me, y_me, core, t_me = (lax.axis_index(a) for a in ("fsdp", "y", "core", "tp"))
    ids = jnp.stack([z_me, y_me, core, t_me]).astype(jnp.int32)
    c_me = y_me * 2 + core
    c_count = size_of(CTX)
    c_masks, p_masks, chip_masks = masks_of(CTX), masks_of(PLANE), masks_of(CHIPS)
    chips, plane = len(chip_masks), len(p_masks)
    x_span, cot_span = tokens[0], cotangent[0]
    span, width = x_span.shape
    length = span * c_count
    half = length // 2
    own = span // t_count
    feats = w_qkv.shape[2] // c_count
    heads = feats // HD
    units = w_up.shape[1] // c_count
    part = width // z_count
    rows_up, cols_up = b_up.shape[0] // c_count, b_up.shape[1]
    vec, _, q_rows, _, _, small_count = small_rows(part, heads, z_count, rows_up, cols_up, feats)
    Z = ("fsdp",)

    turned = jnp.swapaxes(w_qkv, 0, 1)
    small = [ln1_gain, ln1_bias, b_out, ln2_gain, ln2_bias, b_down]
    pack_cfg = (z_count, heads, rows_up, cols_up)
    packed = [shape((4 * part + small_count, feats)), shape((span + 16, width)), shape((own, width)), shape((span, width))]
    if feats % 128 == 0:
        raw = [*small, b_qv, b_up]
        attn_own, x_packed, cot_half, cot_both = kernel_call(
            functools.partial(pack_kernel, pack_cfg),
            packed,
            ids,
            [],
            anys=[turned, w_out, x_span, segments, cot_span, *raw],
            scratch=[
                pltpu.VMEM((feats, part), BF16),
                pltpu.VMEM((1, span), jnp.int32),
                *[pltpu.VMEM(v.shape, BF16) for v in raw],
                pltpu.SemaphoreType.DMA((17,)),
            ],
            cost=2,
            name="pack",
        )
    else:
        (attn_own,) = kernel_call(
            functools.partial(pack_plain_kernel, pack_cfg),
            packed[:1],
            ids,
            [
                lax.dynamic_slice_in_dim(turned, c_me * feats, feats, 2),
                lax.dynamic_slice_in_dim(w_out, c_me * feats, feats, 0),
                *small,
                b_qv,
                b_up,
            ],
            name="pack",
        )
        (x_packed,) = kernel_call(pack_tokens_kernel, packed[1:2], ids, [x_span, segments], name="pack_tokens")
        cot_half = lax.dynamic_slice_in_dim(cot_span, t_me * own, own, 0)
        cot_both = jnp.concatenate([cot_half, lax.dynamic_slice_in_dim(cot_span, (1 - t_me) * own, own, 0)])
    attn_blocks = gather_blocks(attn_own, Z)
    x_blocks = [x_packed]
    for r in range(1, c_count):
        low = r & -r
        source = after(x_blocks[r ^ low], attn_blocks[2]) if r ^ low else x_packed
        x_blocks.append(swap(source, CTX, low))
    vhat_one, seg_row, seg_col = kernel_call(
        functools.partial(first_norm_kernel, (c_masks, t_count, span)),
        [shape((length, width), F32), shape((1, length), F32), shape((length, 128), F32)],
        ids,
        x_blocks,
        cost=4,
        name="first_norm",
    )
    up_own, down_own = kernel_call(
        cut_mlp_kernel,
        [shape((part, units))] * 2,
        ids,
        [],
        anys=[w_up, w_down],
        scratch=[pltpu.VMEM((units, part), BF16), pltpu.SemaphoreType.DMA((2,))],
        deps=[seg_row],
        cost=0.7,
        name="cut_mlp",
    )
    up_blocks = gather_blocks(up_own, Z)
    down_blocks = gather_blocks(down_own, Z)

    cot_core = swap(cot_both, CTX, 1)
    cot_first = [swap(cot_half, CTX, 2 * y) for y in range(1, y_count)]

    qkv_full, out_part, vecs, bias_qv, bias_up = kernel_call(
        functools.partial(unpack_kernel, pack_cfg),
        [
            shape((width, 3 * feats)),
            shape((width, feats)),
            shape((8, width), F32),
            shape((2, feats), F32),
            shape((1, units), F32),
        ],
        ids,
        attn_blocks,
        deps=[seg_row],
        cost=1,
        name="unpack",
    )

    def cat(blocks, deps=()):
        rows, cols = blocks[0].shape
        whole = [shape((rows * len(blocks), cols))]
        (out,) = kernel_call(cat_kernel, whole, ids, blocks, deps=deps, cost=0.6, name="cat")
        return out

    out_chips = to_chips(out_part)
    normed_one, qkv, attn_mix, keep_mix, give_mix = kernel_call(
        functools.partial(attend_kernel, (chip_masks, t_count)),
        [
            shape((length, width)),
            shape((length, 3 * feats)),
            shape((length, feats)),
            shape((half, feats)),
            shape((half, feats)),
        ],
        ids,
        [vhat_one, qkv_full, vecs, bias_qv, seg_row, seg_col],
        deps=[up_own],
        scratch=[pltpu.VMEM((heads, length, feats), BF16)] * 2,
        cost=9,
        name="attend",
    )
    w_mine = cat(out_chips, deps=[give_mix, *up_blocks[1:3]])
    w_other = swap(w_mine, CTX, 1)
    beside = kernel_call(
        beside_kernel,
        [shape((own, 2 * feats))] * chips,
        ids,
        [keep_mix, swap(give_mix, CTX, 1)],
        deps=[w_mine],
        cost=0.6,
        name="beside",
    )
    attn_rows = trade(beside, CHIPS)
    residual, normed_own = kernel_call(
        functools.partial(out_norm_kernel, t_count),
        [shape((own, width), F32), shape((own, width))],
        ids,
        [*attn_rows, w_mine, w_other, x_packed, vecs],
        deps=[*up_blocks[3:], *cot_first, cot_core],
        cost=1.5,
        name="out_norm",
    )
    normed_a = cat(to_chips(normed_own), deps=[*down_blocks[1:3]])
    normed_b = swap(normed_a, CTX, 1)

    cot_pieces = []
    for first in cot_first:
        for piece in (first, swap(after(first, normed_own), ("tp",), 1)):
            cot_pieces += [piece, swap(piece, CTX, 1)]
    (up_full,) = kernel_call(
        place_kernel, [shape((width, units))], ids, up_blocks, deps=[residual], cost=0.5, name="place_up"
    )
    act_a, act_b, slope_a, slope_b = kernel_call(
        hidden_kernel,
        [shape((half, units))] * 2 + [shape((half, units), F32)] * 2,
        ids,
        [normed_a, normed_b, up_full, bias_up],
        cost=3,
        name="hidden",
    )
    (cot_full,) = kernel_call(
        functools.partial(cot_kernel, chip_masks, t_count),
        [shape((length, width))],
        ids,
        [cot_both, cot_core, *cot_pieces],
        deps=[act_a],
        cost=0.5,
        name="cot",
    )
    (down_full,) = kernel_call(
        place_kernel, [shape((width, units))], ids, down_blocks, deps=[cot_full], cost=0.5, name="place_down"
    )

    def back(side, slope):
        return kernel_call(
            functools.partial(hidden_back_kernel, side),
            [shape((half, units)), shape((half, width)), shape((1, units), F32)],
            ids,
            [slope, cot_full, down_full, up_full],
            cost=2,
            name="hidden_back",
        )

    d_up_b, give_two, bup_b = back(1, slope_b)
    d_up_a, keep_two, bup_a = back(0, slope_a)

    def join(keep, give, deps=()):
        landed = swap(give, CTX, 1)
        pieces = [shape((own, width))] * chips
        return kernel_call(join_kernel, pieces, ids, [keep, landed], deps=deps, cost=0.8, name="join")

    pieces_two = join(keep_two, give_two)
    landed_two = trade(pieces_two, CHIPS)
    keep_down, give_down = kernel_call(
        down_kernel,
        [shape((half, width))] * 2,
        ids,
        [act_a, act_b, down_full],
        deps=[pieces_two[0]],
        cost=3,
        name="down",
    )
    mlp_pieces = kernel_call(
        mlp_grad_kernel,
        [shape((2 * part, units))] * z_count,
        ids,
        [normed_a, normed_b, act_a, act_b, d_up_a, d_up_b, cot_full],
        deps=[pieces_two[0]],
        cost=3,
        name="mlp_grad",
    )
    def add(*terms, deps=()):
        (out,) = kernel_call(
            add_kernel, [shape(terms[0].shape)], ids, terms, deps=deps, cost=0.6, name="add"
        )
        return out

    def z_sum(pieces, deps=()):
        total, arrived = list(pieces), []
        for r in range(len(pieces) - 1, 0, -1):
            low = r & -r
            landed = swap(total[r], Z, low)
            if r ^ low:
                total[r ^ low] = add(total[r ^ low], landed, deps=deps)
            else:
                arrived.append(landed)
        return total, arrived

    d_residual, branch_own, grads_two, *mix_pieces = kernel_call(
        functools.partial(second_back_kernel, chips),
        [shape((own, width), F32), shape((own, width)), shape((4, width), F32)]
        + [shape((own, 2 * feats))] * chips,
        ids,
        [*landed_two, residual, cot_half, vecs, w_mine, w_other],
        deps=[keep_down, mlp_pieces[0]],
        cost=2,
        name="second_back",
    )
    mixes = trade(mix_pieces, CHIPS)
    mlp_total, mlp_ends = z_sum(mlp_pieces, deps=[mix_pieces[0]])
    (mix_give,) = kernel_call(apart_kernel, [shape((half, feats))], ids, mixes, deps=[mlp_total[2]], cost=0.5, name="apart")
    mix_landed = swap(mix_give, CTX, 1)
    branch_chips = to_chips(after(branch_own, mix_give))
    d_qkv, sums_qkv = kernel_call(
        functools.partial(attend_back_kernel, (chip_masks, t_count)),
        [shape((length, 3 * feats)), shape((1, 3 * feats), F32)],
        ids,
        [qkv, seg_row, seg_col, *mixes, mix_landed],
        scratch=[pltpu.VMEM((heads, length, feats), BF16)] * 4 + [pltpu.VMEM((length, feats), F32)] * 2,
        cost=8,
        name="attend_back",
    )
    branch_a = cat(branch_chips, deps=[d_qkv])
    branch_b = swap(branch_a, CTX, 1)
    keep_one, give_one, grads_one = kernel_call(
        functools.partial(first_back_kernel, (chip_masks, own, t_count)),
        [shape((half, width)), shape((half, width)), shape((2, width), F32)],
        ids,
        [d_qkv, qkv_full, vhat_one],
        deps=[branch_a],
        cost=0.3,
        name="first_back",
    )
    mlp_sum = add(mlp_total[0], *mlp_ends, deps=[keep_one])
    (small_grads,) = kernel_call(
        functools.partial(small_grad_kernel, (z_count, heads, rows_up, cols_up)),
        [shape((z_count * small_count, feats))],
        ids,
        [grads_one, grads_two, sums_qkv, bup_a, bup_b],
        name="small_grad",
    )
    attn_grads = kernel_call(
        functools.partial(attn_grad_kernel, (chip_masks, t_count)),
        [shape((4 * part + small_count, feats))] * z_count,
        ids,
        [normed_one, d_qkv, attn_mix, branch_a, branch_b, small_grads],
        deps=[mlp_sum],
        scratch=[pltpu.VMEM((length, width), BF16)],
        cost=3,
        name="attn_grad",
    )
    pieces_one = join(keep_one, give_one, deps=[attn_grads[0]])
    attn_total, attn_ends = z_sum(attn_grads, deps=[pieces_one[0]])
    landed_one = trade(pieces_one, CHIPS)
    landed_down = trade(join(keep_down, give_down, deps=[pieces_one[0]]), CHIPS)
    (grad_rows,) = kernel_call(
        functools.partial(last_kernel, t_count),
        [shape((own, width))],
        ids,
        [*landed_one, x_packed, vecs, d_residual],
        name="last",
    )
    (output_own,) = kernel_call(
        output_kernel, [shape((own, width))], ids, [*landed_down, residual, vecs], deps=[grad_rows], name="output"
    )

    def span_rows(rows):
        other = swap(rows, ("tp",), 1)
        (out,) = kernel_call(pair_kernel, [shape((span, width))], ids, [rows, other], name="pair")
        return out[None]

    output = span_rows(output_own)
    grad_tokens = span_rows(grad_rows)

    mlp_all = gather_blocks(mlp_sum, CTX)
    full_up, full_down = kernel_call(
        functools.partial(mlp_place_kernel, c_masks),
        [shape((part, c_count * units), F32), shape((c_count * units, part), F32)],
        ids,
        mlp_all,
        name="mlp_place",
    )
    attn_sum = gather_blocks(add(attn_total[0], *attn_ends), CTX)
    full_qkv, full_out, vec_sum, full_bqv, full_bup = kernel_call(
        functools.partial(attn_place_kernel, (c_masks, heads, rows_up, vec, q_rows)),
        [
            shape((3, part, c_count * feats) if feats % 128 == 0 else (c_count, 3, part, feats), F32),
            shape((c_count * feats, part), F32),
            shape((8, part), F32),
            shape(b_qv.shape, F32),
            shape(b_up.shape, F32),
        ],
        ids,
        attn_sum,
        name="attn_place",
    )
    if feats % 128:
        full_qkv = full_qkv.transpose(1, 2, 0, 3).reshape(3, part, c_count * feats)
    vec_half = vec_sum.astype(BF16)
    vec_sum = vec_half.astype(F32) + swap(vec_half, ("tp",), 1).astype(F32)
    return (
        output,
        grad_tokens,
        vec_sum[0],
        vec_sum[1],
        jnp.swapaxes(full_qkv, 0, 1),
        full_bqv,
        full_out,
        vec_sum[2],
        vec_sum[3],
        vec_sum[4],
        full_up,
        full_bup,
        full_down,
        vec_sum[5],
    )


def solution(mesh):
    fsdp, ctx, tp = (mesh.shape[a] for a in ("fsdp", "ctx", "tp"))
    split = Mesh(mesh.devices.reshape(fsdp, ctx // 2, 2, tp), ("fsdp", "y", "core", "tp"))
    rows = P("fsdp", CTX, None)
    shares = (
        P("fsdp"),
        P("fsdp"),
        P("fsdp", None, "tp"),
        P(None, "tp", "fsdp"),
        P("tp", "fsdp"),
        P("fsdp"),
        P("fsdp"),
        P("fsdp"),
        P("fsdp", "tp"),
        P("tp", "fsdp"),
        P("tp", "fsdp"),
        P("fsdp"),
    )
    return jax.shard_map(
        body,
        mesh=split,
        in_specs=(rows, P("fsdp", CTX), *shares, rows),
        out_specs=(rows, rows, *shares),
        check_vma=False,
    )
```

```python
import functools

import jax
import jax.numpy as jnp
import numpy as np
from jax import lax
from jax.experimental import pallas as pl
from jax.experimental.pallas import tpu as pltpu
from jax.sharding import Mesh
from jax.sharding import PartitionSpec as P

HD = 64
DOC_MOST = 512
EPSILON = 1e-05
NEGATIVE = -1e30
F32 = jnp.float32
FLOPS_PER_US = 2e9
ORDER = {
    "rows": ["pack.0"],
    "x.3": ["attn.1", "attn.2"],
    "cut": ["norm.1"],
    "unpack": ["norm.1", "cut.0", "cot_core", "cot_a.1"],
    "attend": ["up.1", "cot_b.1"],
    "wcat": ["attend.4", "up.1", "up.2"],
    "beside": ["wcat.0"],
    "out_norm": ["up.3", "cot_a_core.1", "cot_b_core.1"],
    "ncat": ["down_w.1", "down_w.2"],
    "cots": ["ncat.0"],
    "up_full": ["cots.0"],
    "down_full": ["hidden.0"],
    "grad_down": ["up_full.0"],
    "back_a": ["grad_down.0"],
    "back_b": ["grad_down.0"],
    "grad_up": ["join_two.0"],
    "down": ["grad_up.0"],
    "dd_sum.2": ["down.0"],
    "res_back": ["down.0", "dd_sum.2"],
    "du_sum.2": ["res_back.3"],
    "apart": ["du_sum.2"],
    "branch.1": ["apart.0"],
    "branch.2": ["apart.0"],
    "branch.3": ["apart.0"],
    "attend_back": ["dd_in.2"],
    "mlp_sums": ["attend_back.0"],
    "bcat": ["mlp_sums.0"],
    "norm_back": ["bcat.0"],
    "join_one": ["grad_attn.0"],
    "mlp_all.3": ["join_one.0"],
    "da_sum.2": ["join_one.0"],
    "join_down": ["join_one.0"],
    "last": ["da_sum.2", "mlp_all.1", "mlp_all.2", "mlp_all.3"],
    "out": ["last.0"],
}
COST = {
    "pack": 2,
    "rows": 0.1,
    "norm": 4,
    "cut": 0.7,
    "unpack": 1,
    "attend": 9,
    "out_norm": 1.5,
    "cots": 0.5,
    "up_full": 0.5,
    "down_full": 0.5,
    "hidden": 3,
    "grad_down": 1.5,
    "back_a": 2,
    "back_b": 2,
    "grad_up": 1.5,
    "down": 2.5,
    "res_back": 2,
    "attend_back": 8,
    "small": 1,
    "grad_attn": 2.5,
    "last": 1,
    "out": 1,
    "pair_out": 1,
    "pair_tok": 1,
    "mlp_place": 1,
    "attn_place": 1,
    "apart": 0.1,
}
BF16 = jnp.bfloat16

CTX = ("y", "core")
CHIPS = ("y", "tp")


def size_of(axes):
    return int(np.prod([lax.axis_size(a) for a in axes]))


def swap(value, axes, bits):
    count = size_of(axes)
    return lax.ppermute(value, axes, [(i, i ^ bits) for i in range(count)])


def masks_of(axes):
    bits, at = [], 1
    for a in reversed(axes):
        mine = []
        while len(mine) < (lax.axis_size(a) - 1).bit_length():
            mine.append(at)
            at *= 2
        bits = mine + bits if a == "core" else bits + mine
    masks = [0]
    for r in range(1, size_of(axes)):
        low = r & -r
        masks.append(masks[r ^ low] | bits[low.bit_length() - 1])
    return masks


def after(value, *others):
    return lax.optimization_barrier((value, *others))[0]


def kernel_call(kernel, outs, ids, arrays, scratch=(), cost=1.0, name=None, vmem=12, deps=(), anys=()):
    deps = list(deps)
    extra = len(deps)

    def run(*refs):
        kernel(*refs[:1], *refs[1 + extra :])

    def place(space):
        return pl.BlockSpec(memory_space=space)

    return pl.pallas_call(
        run,
        out_shape=[jax.ShapeDtypeStruct(s.shape, s.dtype) for s in outs],
        in_specs=[place(pltpu.SMEM)]
        + [place(pl.ANY)] * extra
        + [place(pltpu.HBM)] * len(anys)
        + [place(pltpu.VMEM)] * len(arrays),
        out_specs=[place(pltpu.VMEM)] * len(outs),
        scratch_shapes=list(scratch),
        compiler_params=pltpu.CompilerParams(vmem_limit_bytes=vmem << 20),
        cost_estimate=pl.CostEstimate(
            flops=int(cost * FLOPS_PER_US), bytes_accessed=int(cost * 1e5), transcendentals=0
        ),
        name=name,
    )(ids, *deps, *[pltpu.with_memory_space_constraint(a, pltpu.HBM) for a in anys], *arrays)


def shape(dims, dtype=BF16):
    return jax.ShapeDtypeStruct(tuple(dims), dtype)


NN = (((1,), (0,)), ((), ()))
NT = (((1,), (1,)), ((), ()))
TN = (((0,), (0,)), ((), ()))


def mm(a, b, dims):
    return lax.dot_general(a, b, dims, preferred_element_type=F32)


def at(start, size, unit=None):
    return pl.ds(pl.multiple_of(start, unit or size), size)


def normalise(values):
    centred = values - jnp.mean(values, axis=-1, keepdims=True)
    variance = jnp.mean(centred * centred, axis=-1, keepdims=True)
    scale = lax.rsqrt(variance + EPSILON)
    return centred * scale, scale


def norm_grad(vhat, scale, weighted):
    return scale * (
        weighted
        - jnp.mean(weighted, axis=-1, keepdims=True)
        - vhat * jnp.mean(weighted * vhat, axis=-1, keepdims=True)
    )


class Ids:
    def __init__(self, ref, t_count):
        self.z, self.y, self.core, self.t = ref[0], ref[1], ref[2], ref[3]
        self.c = self.y * 2 + self.core
        self.p = self.c * t_count + self.t
        self.t_count = t_count

    def rows(self, side, mask, own):
        c = (self.y ^ (mask // self.t_count)) * 2 + (self.core ^ side)
        return at((c * self.t_count + (self.t ^ (mask % self.t_count))) * own, own)


def small_rows(part, heads, z_count, rows_up, cols_up, wide):
    vec = 6 * part // wide
    q = 2 * heads * (HD // z_count)
    u = rows_up * cols_up
    q_rows, u_rows = -(-q // wide), -(-u // wide)
    total = vec + q_rows + u_rows
    return vec, q, q_rows, u, u_rows, -(-total // 16) * 16


def pick(table, index):
    row = lax.broadcasted_iota(jnp.int32, table.shape, 0)
    return jnp.sum(jnp.where(row == index, table.astype(F32), 0.0), axis=0, keepdims=True).astype(BF16)


def lay_rows(out, first, pieces, wide):
    line, used = [], 0
    for piece in [*pieces, None]:
        if piece is None or used + piece.shape[1] > wide:
            if line:
                gap = wide - used
                if gap:
                    line.append(jnp.zeros((1, gap), line[0].dtype))
                out[first : first + 1, :] = jnp.concatenate(line, axis=1) if len(line) > 1 else line[0]
                first, line, used = first + 1, [], 0
        if piece is not None:
            line.append(piece)
            used += piece.shape[1]


def copy_in(pairs, sems):
    copies = [pltpu.make_async_copy(a, b, sems.at[i]) for i, (a, b) in enumerate(pairs)]
    for copy in copies:
        copy.start()
    return copies


def pack_kernel(cfg, ids_ref, w_qkv, w_out, *refs):
    params, out, buf, bufs, sems = refs[:8], refs[8], refs[9], refs[10:18], refs[18]
    c = ids_ref[1] * 2 + ids_ref[2]
    feats = out.shape[1]
    part = w_out.shape[1]
    pairs = [
        (w_qkv.at[k, :, at(c * feats, feats)], out.at[k * part : (k + 1) * part, :]) for k in range(3)
    ]
    pairs.append((w_out.at[at(c * feats, feats), :], buf))
    copies = copy_in(pairs + list(zip(params, bufs)), sems)
    for copy in copies[3:]:
        copy.wait()
    out[3 * part : 4 * part, :] = buf[...].T
    pack_small(cfg, c, bufs[:6], bufs[6], bufs[7], out, 4 * part)
    for copy in copies[:3]:
        copy.wait()


def pack_rows_kernel(ids_ref, x, seg, cot, rows, mine, other, both, seg_buf, sems):
    t = ids_ref[3]
    span, own = x.shape[0], mine.shape[0]
    near, far = cot.at[at(t * own, own), :], cot.at[at((1 - t) * own, own), :]
    pairs = [(seg, seg_buf), (x, rows.at[:span, :])]
    pairs += [(near, mine), (far, other), (near, both.at[:own, :]), (far, both.at[own:, :])]
    copies = copy_in(pairs, sems)
    rows[span:, :] = jnp.zeros((rows.shape[0] - span, rows.shape[1]), rows.dtype)
    copies[0].wait()
    rows[span : span + 1, :span] = seg_buf[...].astype(F32).astype(BF16)
    for copy in copies[1:]:
        copy.wait()


def pack_plain_kernel(cfg, ids_ref, w_qkv, w_out, *refs):
    z_count, heads, rows_up, cols_up = cfg
    vectors, (b_qv, b_up, out) = refs[:6], refs[6:]
    part = w_out.shape[1]
    for k in range(3):
        out[k * part : (k + 1) * part, :] = w_qkv[k]
    out[3 * part : 4 * part, :] = w_out[...].T
    pack_small(cfg, ids_ref[1] * 2 + ids_ref[2], vectors, b_qv, b_up, out, 4 * part)


def pack_small(cfg, c, vectors, b_qv, b_up, out, base):
    z_count, heads, rows_up, cols_up = cfg
    wide = out.shape[1]
    part = vectors[0].shape[-1]
    vec, q, q_rows, u, u_rows, total = small_rows(part, heads, z_count, rows_up, cols_up, wide)
    out[base : base + total, :] = jnp.zeros((total, wide), out.dtype)
    per = part // wide
    for i, ref in enumerate(vectors):
        line = ref[...].reshape(1, part)
        for j in range(per):
            row = base + i * per + j
            out[row : row + 1, :] = line[:, j * wide : (j + 1) * wide]
    q_lines = [pick(b_qv[k], c * heads + h) for k in range(2) for h in range(heads)]
    lay_rows(out, base + vec, q_lines, wide)
    lay_rows(out, base + vec + q_rows, [pick(b_up[...], c * rows_up + i) for i in range(rows_up)], wide)


def first_norm_kernel(cfg, ids_ref, *refs):
    c_masks, t_count, span = cfg
    me = Ids(ids_ref, t_count)
    x, (vhat_out, seg_row, seg_col) = refs[: len(c_masks)], refs[len(c_masks) :]
    for r, mask in enumerate(c_masks):
        seg_row[:, at((me.c ^ mask) * span, span)] = x[r][span : span + 1, :span].astype(F32)
    for i in range(seg_row.shape[1] // 128):
        block = jnp.broadcast_to(seg_row[:, i * 128 : (i + 1) * 128], (128, 128))
        seg_col[i * 128 : (i + 1) * 128, :] = block.T
    step = min(64, span)
    for r, mask in enumerate(c_masks):

        def chunk(i, carry, r=r, mask=mask):
            vhat, _ = normalise(x[r][at(i * step, step), :].astype(F32))
            vhat_out[at((me.c ^ mask) * span + i * step, step), :] = vhat
            return carry

        lax.fori_loop(0, span // step, chunk, 0)


def unpack_kernel(cfg, ids_ref, *refs):
    z_count, heads, rows_up, cols_up = cfg
    small, (weight, out_w, vecs, bias_qv, bias_up) = refs[:z_count], refs[z_count:]
    width = weight.shape[0]
    part = width // z_count
    feats = bias_qv.shape[1]
    units = bias_up.shape[1]
    each = HD // z_count
    wide = small[0].shape[1]
    vec, q, q_rows, u, u_rows, total = small_rows(part, heads, z_count, rows_up, cols_up, wide)
    base = 4 * part
    per = part // wide
    qv = [jnp.zeros((1, feats), F32), jnp.zeros((1, feats), F32)]
    ups = jnp.zeros((1, units), F32)
    if wide % 128:
        vecs[...] = jnp.zeros(vecs.shape, F32)
    for r in range(z_count):
        z = ids_ref[0] ^ r
        where = at(z * part, part)
        for k in range(3):
            weight[where, k * feats : (k + 1) * feats] = small[r][k * part : (k + 1) * part, :]
        out_w[where, :] = small[r][3 * part : 4 * part, :]
        for i in range(6):
            for j in range(per):
                row = base + i * per + j
                line = small[r][row : row + 1, :]
                if wide % 128 == 0:
                    vecs[i : i + 1, at(z * part + j * wide, wide)] = line.astype(F32)
                else:
                    lane = lax.broadcasted_iota(jnp.int32, (wide, width), 0)
                    goal = lax.broadcasted_iota(jnp.int32, (wide, width), 1)
                    move = jnp.where(goal == z * part + j * wide + lane, 1.0, 0.0).astype(BF16)
                    vecs[i : i + 1, :] += mm(line, move, NN)
        lane = lax.broadcasted_iota(jnp.int32, (wide, feats), 0)
        goal = lax.broadcasted_iota(jnp.int32, (wide, feats), 1)
        for k in range(2):
            for i in range(q_rows):
                place = lane + i * wide - k * heads * each
                move = (place >= 0) & (place < heads * each)
                move &= goal == (place // each) * HD + z * each + place % each
                row = base + vec + i
                qv[k] += mm(small[r][row : row + 1, :], jnp.where(move, 1.0, 0.0).astype(BF16), NN)
        lane = lax.broadcasted_iota(jnp.int32, (wide, units), 0)
        goal = lax.broadcasted_iota(jnp.int32, (wide, units), 1)
        for i in range(u_rows):
            place = lane + i * wide
            move = (place < u) & (goal == (place // cols_up) * 128 + z * cols_up + place % cols_up)
            row = base + vec + q_rows + i
            ups += mm(small[r][row : row + 1, :], jnp.where(move, 1.0, 0.0).astype(BF16), NN)
    for k in range(2):
        bias_qv[k : k + 1, :] = qv[k]
    bias_up[...] = ups


def head_mask(width, head):
    lane = lax.broadcasted_iota(jnp.int32, (1, width), 1)
    return (lane // HD) == head


def attend_kernel(
    cfg, ids_ref, vhat, weight, vecs, bias_qv, seg_row, seg_col, normed, qkv, attn, keep, give, k_heads, v_heads
):
    chip_masks, t_count = cfg
    me = Ids(ids_ref, t_count)
    length, feats = attn.shape
    heads = feats // HD
    tile = min(256, length)

    def project(i, carry):
        rows = at(i * tile, tile)
        x = (vhat[rows, :] * vecs[0:1, :] + vecs[1:2, :]).astype(BF16)
        normed[rows, :] = x
        out = mm(x, weight[...], NN)
        q = (out[:, :feats] + bias_qv[0:1, :]).astype(BF16)
        k = out[:, feats : 2 * feats].astype(BF16)
        v = (out[:, 2 * feats :] + bias_qv[1:2, :]).astype(BF16)
        qkv[rows, :feats] = q
        qkv[rows, feats : 2 * feats] = k
        qkv[rows, 2 * feats :] = v
        for h in range(heads):
            mask = head_mask(feats, h)
            k_heads[h, rows, :] = jnp.where(mask, k, jnp.zeros_like(k))
            v_heads[h, rows, :] = jnp.where(mask, v, jnp.zeros_like(v))
        return carry

    lax.fori_loop(0, length // tile, project, 0)
    back = -(-DOC_MOST // tile)
    for i in range(length // tile):
        first = max(0, i - back) * tile
        keys = (i + 1) * tile - first
        rows = slice(i * tile, (i + 1) * tile)
        q = qkv[rows, :feats] * BF16(HD ** (-0.5))
        q_pos = i * tile + lax.broadcasted_iota(jnp.int32, (tile, keys), 0)
        k_pos = first + lax.broadcasted_iota(jnp.int32, (tile, keys), 1)
        allowed = (k_pos <= q_pos) & (seg_col[rows, 0:1] == seg_row[:, first : first + keys])

        def head(h, total):
            s = mm(q, k_heads[h, first : first + keys, :], NT)
            s = jnp.where(allowed, s, NEGATIVE)
            e = jnp.exp(s - jnp.max(s, axis=1, keepdims=True))
            p = e * (1.0 / jnp.sum(e, axis=1, keepdims=True))
            return total + mm(p.astype(BF16), v_heads[h, first : first + keys, :], NN)

        mixed = lax.fori_loop(0, heads, head, jnp.zeros((tile, feats), F32))
        attn[rows, :] = mixed.astype(BF16)
    own = keep.shape[0] // len(chip_masks)
    for side, out in ((1, give), (0, keep)):
        for k in range(len(chip_masks)):
            out[k * own : (k + 1) * own, :] = attn[me.rows(side, chip_masks[k], own), :]


def cat_kernel(ids_ref, *refs):
    rows = refs[0].shape[0]
    for k, ref in enumerate(refs[:-1]):
        refs[-1][k * rows : (k + 1) * rows, :] = ref[...]


def beside_kernel(ids_ref, keep, landed, *pieces):
    own, both = pieces[0].shape
    for k, piece in enumerate(pieces):
        rows = slice(k * own, (k + 1) * own)
        piece[:, : both // 2] = keep[rows, :]
        piece[:, both // 2 :] = landed[rows, :]


def apart_kernel(ids_ref, *refs):
    pieces, out = refs[:-1], refs[-1]
    own, feats = pieces[0].shape[0], out.shape[1]
    for k, piece in enumerate(pieces):
        out[k * own : (k + 1) * own, :] = piece[:, feats:]


def out_norm_kernel(t_count, ids_ref, *refs):
    me = Ids(ids_ref, t_count)
    w_mine, w_other, x, vecs, residual, normed = refs[-6:]
    own, width = residual.shape
    feats = w_mine.shape[1]
    total = x[at(me.t * own, own), :].astype(F32) + vecs[2:3, :]
    for k, piece in enumerate(refs[:-6]):
        rows = slice(k * width, (k + 1) * width)
        total += mm(piece[:, :feats], w_mine[rows, :], NT) + mm(piece[:, feats:], w_other[rows, :], NT)
    residual[...] = total
    vhat, _ = normalise(total)
    normed[...] = (vhat * vecs[3:4, :] + vecs[4:5, :]).astype(BF16)


def place_kernel(ids_ref, *refs):
    blocks, out = refs[:-1], refs[-1]
    part = blocks[0].shape[0]
    for r, block in enumerate(blocks):
        out[at((ids_ref[0] ^ r) * part, part), :] = block[...]


def cut_mlp_kernel(ids_ref, w_up, w_down, up, down, buf, sems):
    c = ids_ref[1] * 2 + ids_ref[2]
    units = up.shape[1]
    one = pltpu.make_async_copy(w_up.at[:, at(c * units, units)], up, sems.at[0])
    two = pltpu.make_async_copy(w_down.at[at(c * units, units), :], buf, sems.at[1])
    one.start()
    two.start()
    two.wait()
    down[...] = buf[...].T
    one.wait()


def cot_kernel(chip_masks, t_count, ids_ref, *refs):
    both, pieces, cot = refs[:2], refs[2:-1], refs[-1]
    chips = len(chip_masks)
    own = cot.shape[0] // (2 * chips)
    for side in range(2):
        for k, mask in enumerate(chip_masks):
            to = (side * chips + k) * own
            y, t = mask // t_count, mask % t_count
            if y == 0:
                cot[to : to + own, :] = both[side][t * own : (t + 1) * own, :]
            else:
                cot[to : to + own, :] = pieces[((y - 1) * t_count + t) * 2 + side][...]


def hidden_kernel(ids_ref, normed_a, normed_b, up, bias_up, act_a, act_b, slope_a, slope_b):
    step = min(256, normed_a.shape[0])
    for normed, act, slope in ((normed_a, act_a, slope_a), (normed_b, act_b, slope_b)):

        def chunk(i, carry, normed=normed, act=act, slope=slope):
            rows = at(i * step, step)
            u = mm(normed[rows, :], up[...], NN) + bias_up[...]
            square = u * u
            th = jnp.tanh(0.7978845608028654 * (u + 0.044715 * square * u))
            act[rows, :] = (0.5 * u * (1.0 + th)).astype(BF16)
            slope[rows, :] = 0.5 * (1.0 + th) + 0.5 * u * (1.0 - th * th) * (
                0.7978845608028654 * (1.0 + 3.0 * 0.044715 * square)
            )
            return carry

        lax.fori_loop(0, normed.shape[0] // step, chunk, 0)


def hidden_back_kernel(side, ids_ref, slope, cot, down, up, d_up, d_norm, grad_bias):
    half = slope.shape[0]
    step = min(256, half)

    def chunk(i, total):
        rows = at(i * step, step)
        d_act = mm(cot[at(side * half + i * step, step), :], down[...], NN)
        g = (d_act * slope[rows, :]).astype(BF16)
        d_up[rows, :] = g
        d_norm[rows, :] = mm(g, up[...], NT).astype(BF16)
        return total + jnp.sum(g.astype(F32), axis=0, keepdims=True)

    grad_bias[...] = lax.fori_loop(0, half // step, chunk, jnp.zeros(grad_bias.shape, F32))


def down_kernel(ids_ref, act_a, act_b, down, keep, give):
    step = min(256, act_a.shape[0])
    for act, out in ((act_b, give), (act_a, keep)):

        def chunk(i, carry, act=act, out=out):
            rows = at(i * step, step)
            out[rows, :] = mm(act[rows, :], down[...], NT).astype(BF16)
            return carry

        lax.fori_loop(0, act.shape[0] // step, chunk, 0)


def join_kernel(ids_ref, keep, landed, *pieces):
    own = pieces[0].shape[0]
    for k, piece in enumerate(pieces):
        rows = slice(k * own, (k + 1) * own)
        piece[...] = (keep[rows, :].astype(F32) + landed[rows, :].astype(F32)).astype(BF16)


def down_grad_kernel(ids_ref, cot, act_a, act_b, *outs):
    half = act_a.shape[0]
    part = outs[0].shape[0]
    for r in range(len(outs) - 1, -1, -1):
        cols = at((ids_ref[0] ^ r) * part, part)
        total = mm(cot[:half, cols], act_a[...], TN) + mm(cot[half:, cols], act_b[...], TN)
        outs[r][...] = total.astype(BF16)


def up_grad_kernel(ids_ref, normed_a, normed_b, d_up_a, d_up_b, near_down, *outs):
    part = outs[0].shape[0]
    for r in range(len(outs) - 1, -1, -1):
        cols = at((ids_ref[0] ^ r) * part, part)
        total = mm(normed_a[:, cols], d_up_a[...], TN) + mm(normed_b[:, cols], d_up_b[...], TN)
        outs[r][:part, :] = total.astype(BF16)
    outs[1][part:, :] = near_down[...]


def add_kernel(ids_ref, a, b, out):
    out[...] = (a[...].astype(F32) + b[...].astype(F32)).astype(BF16)


def mlp_sums_kernel(ups, ids_ref, near, *refs):
    out = refs[-1]
    part = out.shape[0] // 2
    for base, terms in ((0, refs[:ups]), (part, refs[ups:-1])):
        total = near[base : base + part, :].astype(F32)
        for term in terms:
            total += term[...].astype(F32)
        out[base : base + part, :] = total.astype(BF16)


def sum_kernel(ids_ref, *refs):
    total = refs[0][...].astype(F32)
    for ref in refs[1:-1]:
        total += ref[...].astype(F32)
    refs[-1][...] = total.astype(BF16)


def second_back_kernel(cfg, ids_ref, *refs):
    chips = cfg
    landed, refs = refs[:chips], refs[chips:]
    residual, cot, vecs, w_mine, w_other, d_res, branch, grads = refs[:8]
    d_mix = refs[8:]
    own, width = residual.shape
    feats = w_mine.shape[1]
    d_norm = landed[0][...].astype(F32)
    for ref in landed[1:]:
        d_norm += ref[...].astype(F32)
    vhat, scale = normalise(residual[...])
    c = cot[...].astype(F32)
    d_residual = c + norm_grad(vhat, scale, vecs[3:4, :] * d_norm)
    d_res[...] = d_residual
    b = d_residual.astype(BF16)
    branch[...] = b
    for k, piece in enumerate(d_mix):
        rows = slice(k * width, (k + 1) * width)
        piece[:, :feats] = mm(b, w_mine[rows, :], NN).astype(BF16)
        piece[:, feats:] = mm(b, w_other[rows, :], NN).astype(BF16)
    grads[0:1, :] = jnp.sum(d_residual, axis=0, keepdims=True)
    grads[1:2, :] = jnp.sum(vhat * d_norm, axis=0, keepdims=True)
    grads[2:3, :] = jnp.sum(d_norm, axis=0, keepdims=True)
    grads[3:4, :] = jnp.sum(c, axis=0, keepdims=True)


def attend_back_kernel(cfg, ids_ref, qkv, seg_row, seg_col, *refs):
    chip_masks, t_count = cfg
    me = Ids(ids_ref, t_count)
    mixes, refs = refs[: len(chip_masks)], refs[len(chip_masks) :]
    landed, d_qkv, sums, k_heads, v_heads, q_heads, m_heads, dk, dv = refs
    length, feats = qkv.shape[0], dk.shape[1]
    own = mixes[0].shape[0]
    heads = feats // HD
    tile = min(256, length)
    scale = HD ** (-0.5)
    for h in range(heads):
        mask = head_mask(feats, h)
        for k, m in enumerate(chip_masks):
            piece = mixes[k][:, :feats]
            m_heads[h, me.rows(0, m, own), :] = jnp.where(mask, piece, jnp.zeros_like(piece))
            piece = landed[k * own : (k + 1) * own, :]
            m_heads[h, me.rows(1, m, own), :] = jnp.where(mask, piece, jnp.zeros_like(piece))

    def prepare(i, carry):
        rows = at(i * tile, tile)
        for h in range(heads):
            mask = head_mask(feats, h)
            for k, ref in ((0, q_heads), (1, k_heads), (2, v_heads)):
                piece = qkv[rows, k * feats : (k + 1) * feats]
                if k == 0:
                    piece = piece * BF16(scale)
                ref[h, rows, :] = jnp.where(mask, piece, jnp.zeros_like(piece))
        dk[rows, :] = jnp.zeros((tile, feats), F32)
        dv[rows, :] = jnp.zeros((tile, feats), F32)
        return carry

    lax.fori_loop(0, length // tile, prepare, 0)
    back = -(-DOC_MOST // tile)
    for i in range(length // tile):
        first = max(0, i - back) * tile
        keys = (i + 1) * tile - first
        rows = slice(i * tile, (i + 1) * tile)
        span = slice(first, first + keys)
        k_pos = first + lax.broadcasted_iota(jnp.int32, (keys, tile), 0)
        q_pos = i * tile + lax.broadcasted_iota(jnp.int32, (keys, tile), 1)
        allowed = (k_pos <= q_pos) & (seg_col[span, 0:1] == seg_row[:, rows])

        def head(h, dq):
            k, v, q, m = k_heads[h, span, :], v_heads[h, span, :], q_heads[h, rows, :], m_heads[h, rows, :]
            s = jnp.where(allowed, mm(k, q, NT), NEGATIVE)
            e = jnp.exp(s - jnp.max(s, axis=0, keepdims=True))
            p = e * (1.0 / jnp.sum(e, axis=0, keepdims=True))
            dp = mm(v, m, NT)
            row_dot = jnp.sum(p * dp, axis=0, keepdims=True)
            ds = (p * (dp - row_dot)).astype(BF16)
            dv[span, :] += mm(p.astype(BF16), m, NN)
            dk[span, :] += mm(ds, q, NN)
            return dq + mm(ds, k, TN)

        dq = lax.fori_loop(0, heads, head, jnp.zeros((tile, feats), F32))
        d_qkv[rows, :feats] = (dq * scale).astype(BF16)

    def finish(i, carry):
        rows = at(i * tile, tile)
        d_qkv[rows, feats : 2 * feats] = dk[rows, :].astype(BF16)
        d_qkv[rows, 2 * feats :] = dv[rows, :].astype(BF16)
        return carry + jnp.sum(d_qkv[rows, :].astype(F32), axis=0, keepdims=True)

    sums[...] = lax.fori_loop(0, length // tile, finish, jnp.zeros((1, 3 * feats), F32))


def first_back_kernel(cfg, ids_ref, d_qkv, weight, vhat, keep, give, grads):
    chip_masks, own, t_count = cfg
    me = Ids(ids_ref, t_count)
    gain = jnp.zeros((1, vhat.shape[1]), F32)
    bias = gain
    for out, side in ((give, 1), (keep, 0)):
        for k, mask in enumerate(chip_masks):
            rows = me.rows(side, mask, own)
            d = mm(d_qkv[rows, :], weight[...], NT)
            out[k * own : (k + 1) * own, :] = d.astype(BF16)
            gain += jnp.sum(vhat[rows, :] * d, axis=0, keepdims=True)
            bias += jnp.sum(d, axis=0, keepdims=True)
    grads[0:1, :] = gain
    grads[1:2, :] = bias


def attn_grad_kernel(cfg, ids_ref, normed, d_qkv, attn, branch_a, branch_b, small, small_other, *refs):
    chip_masks, t_count, z_count, vec = cfg
    me = Ids(ids_ref, t_count)
    outs, branch = refs[:-1], refs[-1]
    own = branch_a.shape[0] // len(chip_masks)
    for side, ref in ((0, branch_a), (1, branch_b)):
        for k, mask in enumerate(chip_masks):
            branch[me.rows(side, mask, own), :] = ref[k * own : (k + 1) * own, :]
    count = small.shape[0] // z_count
    feats = attn.shape[1]
    part = normed.shape[1] // z_count
    row = lax.broadcasted_iota(jnp.int32, (count, feats), 0)
    for r in range(z_count - 1, -1, -1):
        out = outs[r]
        cols = at((me.z ^ r) * part, part)
        g = mm(normed[:, cols], d_qkv[...], TN)
        for k in range(3):
            out[k * part : (k + 1) * part, :] = g[:, k * feats : (k + 1) * feats].astype(BF16)
        out[3 * part : 4 * part, :] = mm(branch[:, cols], attn[...], TN).astype(BF16)
        mine = small[r * count : (r + 1) * count, :].astype(F32)
        both = mine + small_other[r * count : (r + 1) * count, :].astype(F32)
        out[4 * part :, :] = jnp.where(row < vec, both, mine).astype(BF16)


def last_kernel(t_count, ids_ref, *refs):
    me = Ids(ids_ref, t_count)
    x, vecs, d_res, out = refs[-4:]
    own = out.shape[0]
    d_norm = refs[0][...].astype(F32)
    for ref in refs[1:-4]:
        d_norm += ref[...].astype(F32)
    vhat, scale = normalise(x[at(me.t * own, own), :].astype(F32))
    out[...] = (d_res[...] + norm_grad(vhat, scale, vecs[0:1, :] * d_norm)).astype(BF16)


def output_kernel(ids_ref, *refs):
    residual, vecs, out = refs[-3:]
    total = residual[...] + vecs[5:6, :]
    for ref in refs[:-3]:
        total += ref[...].astype(F32)
    out[...] = total.astype(BF16)


def pair_kernel(ids_ref, mine, other, out):
    own = mine.shape[0]
    out[at(ids_ref[3] * own, own), :] = mine[...]
    out[at((1 - ids_ref[3]) * own, own), :] = other[...]


def small_grad_kernel(cfg, ids_ref, one, two, sums, bup_a, bup_b, out):
    z_count, heads, rows_up, cols_up = cfg
    width = one.shape[1]
    part = width // z_count
    feats = sums.shape[1] // 3
    units = bup_a.shape[1]
    each = HD // z_count
    wide = out.shape[1]
    vec, q, q_rows, u, u_rows, total = small_rows(part, heads, z_count, rows_up, cols_up, wide)
    per = part // wide
    bqv = (sums[:, :feats].astype(BF16), sums[:, 2 * feats :].astype(BF16))
    bup = (bup_a[...] + bup_b[...]).astype(BF16)
    out[...] = jnp.zeros(out.shape, out.dtype)
    for r in range(z_count):
        z = ids_ref[0] ^ r
        base = r * total
        for i in range(6):
            ref, row = (one, i) if i < 2 else (two, i - 2)
            for j in range(per):
                k = base + i * per + j
                if wide % 128 == 0:
                    out[k : k + 1, :] = ref[row : row + 1, at(z * part + j * wide, wide)].astype(BF16)
                else:
                    lane = lax.broadcasted_iota(jnp.int32, (wide, width), 0)
                    goal = lax.broadcasted_iota(jnp.int32, (wide, width), 1)
                    move = jnp.where(goal == z * part + j * wide + lane, 1.0, 0.0).astype(BF16)
                    out[k : k + 1, :] = mm(ref[row : row + 1, :].astype(BF16), move, NT).astype(BF16)
        lane = lax.broadcasted_iota(jnp.int32, (wide, feats), 0)
        goal = lax.broadcasted_iota(jnp.int32, (wide, feats), 1)
        for i in range(q_rows):
            line = jnp.zeros((1, wide), F32)
            for k in range(2):
                place = lane + i * wide - k * heads * each
                move = (place >= 0) & (place < heads * each)
                move &= goal == (place // each) * HD + z * each + place % each
                line += mm(bqv[k], jnp.where(move, 1.0, 0.0).astype(BF16), NT)
            out[base + vec + i : base + vec + i + 1, :] = line.astype(BF16)
        lane = lax.broadcasted_iota(jnp.int32, (wide, units), 0)
        goal = lax.broadcasted_iota(jnp.int32, (wide, units), 1)
        for i in range(u_rows):
            place = lane + i * wide
            move = (place < u) & (goal == (place // cols_up) * 128 + z * cols_up + place % cols_up)
            row = base + vec + q_rows + i
            out[row : row + 1, :] = mm(bup, jnp.where(move, 1.0, 0.0).astype(BF16), NT).astype(BF16)


def mlp_place_kernel(c_masks, ids_ref, *refs):
    blocks, (up, down) = refs[:-2], refs[-2:]
    c = ids_ref[1] * 2 + ids_ref[2]
    units = blocks[0].shape[1]
    part = blocks[0].shape[0] // 2
    for r, mask in enumerate(c_masks):
        where = at((c ^ mask) * units, units)
        up[:, where] = blocks[r][:part, :].astype(F32)
        down[where, :] = blocks[r][part:, :].astype(F32).T


def attn_place_kernel(cfg, ids_ref, *refs):
    c_masks, heads, rows_up, vec, q_rows = cfg
    blocks = refs[: len(c_masks)]
    qkv, out, vecs, b_qv, b_up = refs[len(c_masks) :]
    c = ids_ref[1] * 2 + ids_ref[2]
    wide = blocks[0].shape[1]
    part = vecs.shape[1]
    each, cols_up = b_qv.shape[2], b_up.shape[1]
    aligned = wide % 128 == 0
    for r, mask in enumerate(c_masks):
        where = at((c ^ mask) * wide, wide)
        if aligned:
            for k in range(3):
                qkv[k, :, where] = blocks[r][k * part : (k + 1) * part, :].astype(F32)
        else:
            for k in range(3):
                qkv[c ^ mask, k] = blocks[r][k * part : (k + 1) * part, :].astype(F32)
        out[where, :] = blocks[r][3 * part : 4 * part, :].astype(F32).T
        base = 4 * part + vec
        for k in range(2):
            for h in range(heads):
                flat = (k * heads + h) * each
                row, lane = base + flat // wide, flat % wide
                b_qv[k, pl.ds((c ^ mask) * heads + h, 1), :] = blocks[r][
                    row : row + 1, lane : lane + each
                ].astype(F32)
        for i in range(rows_up):
            row, lane = base + q_rows + (i * cols_up) // wide, (i * cols_up) % wide
            b_up[pl.ds((c ^ mask) * rows_up + i, 1), :] = blocks[r][
                row : row + 1, lane : lane + cols_up
            ].astype(F32)
    total = blocks[0][4 * part : 4 * part + vec, :].astype(F32)
    for block in blocks[1:]:
        total += block[4 * part : 4 * part + vec, :].astype(F32)
    per = part // wide
    for i in range(6):
        for j in range(per):
            vecs[i : i + 1, j * wide : (j + 1) * wide] = total[i * per + j : i * per + j + 1, :]


def body(
    tokens,
    segments,
    ln1_gain,
    ln1_bias,
    w_qkv,
    b_qv,
    w_out,
    b_out,
    ln2_gain,
    ln2_bias,
    w_up,
    b_up,
    w_down,
    b_down,
    cotangent,
):
    z_count, t_count, y_count = (lax.axis_size(a) for a in ("fsdp", "tp", "y"))
    z_me, y_me, core, t_me = (lax.axis_index(a) for a in ("fsdp", "y", "core", "tp"))
    ids = jnp.stack([z_me, y_me, core, t_me]).astype(jnp.int32)
    c_me = y_me * 2 + core
    c_count = size_of(CTX)
    c_masks, chip_masks = masks_of(CTX), masks_of(CHIPS)
    chips = len(chip_masks)
    x_span, cot_span = tokens[0], cotangent[0]
    span, width = x_span.shape
    length = span * c_count
    half = length // 2
    own = span // t_count
    feats = w_qkv.shape[2] // c_count
    heads = feats // HD
    units = w_up.shape[1] // c_count
    part = width // z_count
    rows_up, cols_up = b_up.shape[0] // c_count, b_up.shape[1]
    vec, _, q_rows, _, _, small_count = small_rows(part, heads, z_count, rows_up, cols_up, feats)
    Z, TP = ("fsdp",), ("tp",)
    turned = jnp.swapaxes(w_qkv, 0, 1)
    raw = [ln1_gain, ln1_bias, b_out, ln2_gain, ln2_bias, b_down, b_qv, b_up]
    pack_cfg = (z_count, heads, rows_up, cols_up)
    z_all, c_all = range(z_count), range(c_count)
    known, open_nodes = {}, set()

    def get(ref):
        name, _, index = ref.partition(".")
        key = name if name in KERNELS else ref
        if key not in known:
            if key in open_nodes:
                raise ValueError(key)
            open_nodes.add(key)
            known[key] = NODES[name]() if not index or name in KERNELS else NODES[name](int(index))
        value = known[key]
        return value[int(index)] if index and name in KERNELS else value

    def waits(key):
        return [get(ref) for ref in ORDER.get(key, ())]

    def move(key, value, axes, bits):
        pins = waits(key)
        return swap(after(value, *pins) if pins else value, axes, bits)

    def run(key, kernel, outs, arrays, **more):
        name = key.split(".")[0]
        deps = waits(key)
        return kernel_call(kernel, outs, ids, arrays, deps=deps, cost=COST.get(name, 0.1), name=name, **more)

    def gathered(name, source, axes, r):
        low = r & -r
        if r == 0:
            return get(source)
        return move(f"{name}.{r}", get(f"{name}.{r ^ low}"), axes, low)

    def from_chip(name, source, k):
        return get(source) if k == 0 else move(f"{name}.{k}", get(source), CHIPS, chip_masks[k])

    def traded(name, kernel, k, first=0):
        piece = get(f"{kernel}.{first + k}")
        return piece if k == 0 else move(f"{name}.{k}", piece, CHIPS, chip_masks[k])

    def pack():
        out = [shape((4 * part + small_count, feats))]
        if feats % 128:
            cuts = [
                lax.dynamic_slice_in_dim(turned, c_me * feats, feats, 2),
                lax.dynamic_slice_in_dim(w_out, c_me * feats, feats, 0),
            ]
            return run("pack", functools.partial(pack_plain_kernel, pack_cfg), out, [*cuts, *raw])
        scratch = [pltpu.VMEM((feats, part), BF16), *[pltpu.VMEM(v.shape, BF16) for v in raw]]
        return run(
            "pack",
            functools.partial(pack_kernel, pack_cfg),
            out,
            [],
            anys=[turned, w_out, *raw],
            scratch=[*scratch, pltpu.SemaphoreType.DMA((12,))],
        )

    def rows():
        outs = [shape((span + 16, width)), shape((own, width)), shape((own, width)), shape((span, width))]
        return run(
            "rows",
            pack_rows_kernel,
            outs,
            [],
            anys=[x_span, segments, cot_span],
            scratch=[pltpu.VMEM((1, span), jnp.int32), pltpu.SemaphoreType.DMA((6,))],
        )

    def norm():
        return run(
            "norm",
            functools.partial(first_norm_kernel, (c_masks, t_count, span)),
            [shape((length, width), F32), shape((1, length), F32), shape((length, 128), F32)],
            [get(f"x.{r}") for r in c_all],
        )

    def cut():
        return run(
            "cut",
            cut_mlp_kernel,
            [shape((part, units))] * 2,
            [],
            anys=[w_up, w_down],
            scratch=[pltpu.VMEM((units, part), BF16), pltpu.SemaphoreType.DMA((2,))],
        )

    def unpack():
        return run(
            "unpack",
            functools.partial(unpack_kernel, pack_cfg),
            [
                shape((width, 3 * feats)),
                shape((width, feats)),
                shape((8, width), F32),
                shape((2, feats), F32),
                shape((1, units), F32),
            ],
            [get(f"attn.{r}") for r in z_all],
        )

    def attend():
        vhat, seg_row, seg_col = get("norm")
        qkv_full, _, vecs, bias_qv, _ = get("unpack")
        return run(
            "attend",
            functools.partial(attend_kernel, (chip_masks, t_count)),
            [
                shape((length, width)),
                shape((length, 3 * feats)),
                shape((length, feats)),
                shape((half, feats)),
                shape((half, feats)),
            ],
            [vhat, qkv_full, vecs, bias_qv, seg_row, seg_col],
            scratch=[pltpu.VMEM((heads, length, feats), BF16)] * 2,
        )

    def cat(key, blocks):
        size, cols = blocks[0].shape
        return run(key, cat_kernel, [shape((size * len(blocks), cols))], blocks)

    def wcat():
        return cat("wcat", [get(f"wout.{k}") for k in range(chips)])

    def beside():
        pieces = [shape((own, 2 * feats))] * chips
        return run("beside", beside_kernel, pieces, [get("attend.3"), get("give_mix")])

    def out_norm():
        return run(
            "out_norm",
            functools.partial(out_norm_kernel, t_count),
            [shape((own, width), F32), shape((own, width))],
            [*[get(f"mixed.{k}") for k in range(chips)], get("wcat.0"), get("w_other"), get("rows.0"), get("unpack.2")],
        )

    def ncat():
        return cat("ncat", [get(f"normed.{k}") for k in range(chips)])

    def cots():
        pieces = []
        for y in range(1, y_count):
            for name in ("cot_a", "cot_b"):
                pieces += [get(f"{name}.{y}"), get(f"{name}_core.{y}")]
        return run(
            "cots",
            functools.partial(cot_kernel, chip_masks, t_count),
            [shape((length, width))],
            [get("rows.3"), get("cot_core"), *pieces],
        )

    def up_full():
        return run("up_full", place_kernel, [shape((width, units))], [get(f"up.{r}") for r in z_all])

    def down_full():
        return run("down_full", place_kernel, [shape((width, units))], [get(f"down_w.{r}") for r in z_all])

    def hidden():
        return run(
            "hidden",
            hidden_kernel,
            [shape((half, units))] * 2 + [shape((half, units), F32)] * 2,
            [get("ncat.0"), get("normed_b"), get("up_full.0"), get("unpack.4")],
        )

    def back(key, side):
        return run(
            key,
            functools.partial(hidden_back_kernel, side),
            [shape((half, units)), shape((half, width)), shape((1, units), F32)],
            [get(f"hidden.{2 + side}"), get("cots.0"), get("down_full.0"), get("up_full.0")],
        )

    def join(key, keep, give):
        return run(key, join_kernel, [shape((own, width))] * chips, [get(keep), get(give)])

    def grad_down():
        return run(
            "grad_down",
            down_grad_kernel,
            [shape((part, units))] * z_count,
            [get("cots.0"), get("hidden.0"), get("hidden.1")],
        )

    def grad_up():
        return run(
            "grad_up",
            up_grad_kernel,
            [shape((part if r != 1 else 2 * part, units)) for r in z_all],
            [get("ncat.0"), get("normed_b"), get("back_a.0"), get("back_b.0"), get("grad_down.1")],
        )

    def down():
        return run(
            "down",
            down_kernel,
            [shape((half, width))] * 2,
            [get("hidden.0"), get("hidden.1"), get("down_full.0")],
        )

    def z_total(name, kernel, r):
        value = get(f"{kernel}.{r}")
        for low in (1, 2, 4):
            if low < (r & -r) and r | low < z_count:
                key = f"{name}_sum.{r}"
                (value,) = run(key, add_kernel, [shape(value.shape)], [value, get(f"{name}_in.{r | low}")])
        return value

    def z_in(name, kernel, r):
        return move(f"{name}_in.{r}", get(f"{name}_sum.{r}"), Z, r & -r)

    def z_ends(name):
        return [get(f"{name}_in.{r}") for r in z_all if r > 1 and r == r & -r]

    def mlp_sums():
        ups = [get("grad_up.0"), *z_ends("du")]
        downs = [get("grad_down.0"), *z_ends("dd")]
        near = get("near")
        return run(
            "mlp_sums",
            functools.partial(mlp_sums_kernel, len(ups)),
            [shape((2 * part, units))],
            [near, *ups, *downs],
        )

    def res_back():
        return run(
            "res_back",
            functools.partial(second_back_kernel, chips),
            [shape((own, width), F32), shape((own, width)), shape((4, width), F32)]
            + [shape((own, 2 * feats))] * chips,
            [
                *[get(f"two.{k}") for k in range(chips)],
                get("out_norm.0"),
                get("rows.1"),
                get("unpack.2"),
                get("wcat.0"),
                get("w_other"),
            ],
        )

    def apart():
        return run("apart", apart_kernel, [shape((half, feats))], [get(f"d_mix.{k}") for k in range(chips)])

    def attend_back():
        return run(
            "attend_back",
            functools.partial(attend_back_kernel, (chip_masks, t_count)),
            [shape((length, 3 * feats)), shape((1, 3 * feats), F32)],
            [
                get("attend.1"),
                get("norm.1"),
                get("norm.2"),
                *[get(f"d_mix.{k}") for k in range(chips)],
                get("d_mix_core"),
            ],
            scratch=[pltpu.VMEM((heads, length, feats), BF16)] * 4 + [pltpu.VMEM((length, feats), F32)] * 2,
        )

    def bcat():
        return cat("bcat", [get(f"branch.{k}") for k in range(chips)])

    def norm_back():
        return run(
            "norm_back",
            functools.partial(first_back_kernel, (chip_masks, own, t_count)),
            [shape((half, width)), shape((half, width)), shape((2, width), F32)],
            [get("attend_back.0"), get("unpack.0"), get("norm.0")],
        )

    def small():
        return run(
            "small",
            functools.partial(small_grad_kernel, (z_count, heads, rows_up, cols_up)),
            [shape((z_count * small_count, feats))],
            [get("norm_back.2"), get("res_back.2"), get("attend_back.1"), get("back_a.2"), get("back_b.2")],
        )

    def grad_attn():
        return run(
            "grad_attn",
            functools.partial(attn_grad_kernel, (chip_masks, t_count, z_count, vec)),
            [shape((4 * part + small_count, feats))] * z_count,
            [
                get("attend.0"),
                get("attend_back.0"),
                get("attend.2"),
                get("bcat.0"),
                get("branch_b"),
                get("small.0"),
                get("small_tp"),
            ],
            scratch=[pltpu.VMEM((length, width), BF16)],
        )

    def attn_sums():
        terms = [get("grad_attn.0"), get("da_in.1"), *z_ends("da")]
        return run("attn_sums", sum_kernel, [shape(terms[0].shape)], terms)

    def last():
        return run(
            "last",
            functools.partial(last_kernel, t_count),
            [shape((own, width))],
            [*[get(f"one.{k}") for k in range(chips)], get("rows.0"), get("unpack.2"), get("res_back.0")],
        )

    def out():
        arrays = [*[get(f"down_in.{k}") for k in range(chips)], get("out_norm.0"), get("unpack.2")]
        return run("out", output_kernel, [shape((own, width))], arrays)

    def pair(key, mine, other):
        return run(key, pair_kernel, [shape((span, width))], [get(mine), get(other)])

    def mlp_place():
        return run(
            "mlp_place",
            functools.partial(mlp_place_kernel, c_masks),
            [shape((part, c_count * units), F32), shape((c_count * units, part), F32)],
            [get(f"mlp_all.{r}") for r in c_all],
        )

    def attn_place():
        return run(
            "attn_place",
            functools.partial(attn_place_kernel, (c_masks, heads, rows_up, vec, q_rows)),
            [
                shape((3, part, c_count * feats) if feats % 128 == 0 else (c_count, 3, part, feats), F32),
                shape((c_count * feats, part), F32),
                shape((8, part), F32),
                shape(b_qv.shape, F32),
                shape(b_up.shape, F32),
            ],
            [get(f"attn_all.{r}") for r in c_all],
        )

    KERNELS = {
        f.__name__: f
        for f in (
            [pack, rows, norm, cut, unpack, attend, wcat, beside, out_norm, ncat, cots, up_full, down_full]
            + [hidden, grad_down, grad_up, down, mlp_sums, res_back, apart, attend_back, bcat, norm_back]
            + [small, grad_attn, attn_sums, last, out, mlp_place, attn_place]
        )
    }
    KERNELS |= {
        "back_a": lambda: back("back_a", 0),
        "back_b": lambda: back("back_b", 1),
        "join_two": lambda: join("join_two", "back_a.1", "give_two"),
        "join_down": lambda: join("join_down", "down.0", "give_down"),
        "join_one": lambda: join("join_one", "norm_back.0", "give_one"),
        "pair_out": lambda: pair("pair_out", "out.0", "out_tp"),
        "pair_tok": lambda: pair("pair_tok", "last.0", "last_tp"),
    }
    NODES = KERNELS | {
        "attn": lambda r: gathered("attn", "pack.0", Z, r),
        "x": lambda r: gathered("x", "rows.0", CTX, r),
        "up": lambda r: gathered("up", "cut.0", Z, r),
        "down_w": lambda r: gathered("down_w", "cut.1", Z, r),
        "cot_core": lambda: move("cot_core", get("rows.3"), CTX, 1),
        "cot_a": lambda y: move(f"cot_a.{y}", get("rows.1"), CTX, 2 * y),
        "cot_b": lambda y: move(f"cot_b.{y}", get("rows.2"), CTX, 2 * y),
        "cot_a_core": lambda y: move(f"cot_a_core.{y}", get(f"cot_a.{y}"), CTX, 1),
        "cot_b_core": lambda y: move(f"cot_b_core.{y}", get(f"cot_b.{y}"), CTX, 1),
        "wout": lambda k: from_chip("wout", "unpack.1", k),
        "w_other": lambda: move("w_other", get("wcat.0"), CTX, 1),
        "give_mix": lambda: move("give_mix", get("attend.4"), CTX, 1),
        "mixed": lambda k: traded("mixed", "beside", k),
        "normed": lambda k: from_chip("normed", "out_norm.1", k),
        "normed_b": lambda: move("normed_b", get("ncat.0"), CTX, 1),
        "give_two": lambda: move("give_two", get("back_b.1"), CTX, 1),
        "two": lambda k: traded("two", "join_two", k),
        "give_down": lambda: move("give_down", get("down.1"), CTX, 1),
        "down_in": lambda k: traded("down_in", "join_down", k),
        "give_one": lambda: move("give_one", get("norm_back.1"), CTX, 1),
        "one": lambda k: traded("one", "join_one", k),
        "d_mix": lambda k: traded("d_mix", "res_back", k, 3),
        "d_mix_core": lambda: move("d_mix_core", get("apart.0"), CTX, 1),
        "branch": lambda k: from_chip("branch", "res_back.1", k),
        "branch_b": lambda: move("branch_b", get("bcat.0"), CTX, 1),
        "small_tp": lambda: move("small_tp", get("small.0"), TP, 1),
        "near": lambda: move("near", get("grad_up.1"), Z, 1),
        "dd_sum": lambda r: z_total("dd", "grad_down", r),
        "dd_in": lambda r: z_in("dd", "grad_down", r),
        "du_sum": lambda r: z_total("du", "grad_up", r),
        "du_in": lambda r: z_in("du", "grad_up", r),
        "da_sum": lambda r: z_total("da", "grad_attn", r),
        "da_in": lambda r: z_in("da", "grad_attn", r),
        "out_tp": lambda: move("out_tp", get("out.0"), TP, 1),
        "last_tp": lambda: move("last_tp", get("last.0"), TP, 1),
        "mlp_all": lambda r: gathered("mlp_all", "mlp_sums.0", CTX, r),
        "attn_all": lambda r: gathered("attn_all", "attn_sums.0", CTX, r),
    }
    full_qkv, full_out, vec_sum, full_bqv, full_bup = get("attn_place")
    if feats % 128:
        full_qkv = full_qkv.transpose(1, 2, 0, 3).reshape(3, part, c_count * feats)
    full_up, full_down = get("mlp_place")
    return (
        get("pair_out.0")[None],
        get("pair_tok.0")[None],
        vec_sum[0],
        vec_sum[1],
        jnp.swapaxes(full_qkv, 0, 1),
        full_bqv,
        full_out,
        vec_sum[2],
        vec_sum[3],
        vec_sum[4],
        full_up,
        full_bup,
        full_down,
        vec_sum[5],
    )


def solution(mesh):
    fsdp, ctx, tp = (mesh.shape[a] for a in ("fsdp", "ctx", "tp"))
    split = Mesh(mesh.devices.reshape(fsdp, ctx // 2, 2, tp), ("fsdp", "y", "core", "tp"))
    rows = P("fsdp", CTX, None)
    shares = (
        P("fsdp"),
        P("fsdp"),
        P("fsdp", None, "tp"),
        P(None, "tp", "fsdp"),
        P("tp", "fsdp"),
        P("fsdp"),
        P("fsdp"),
        P("fsdp"),
        P("fsdp", "tp"),
        P("tp", "fsdp"),
        P("tp", "fsdp"),
        P("fsdp"),
    )
    return jax.shard_map(
        body,
        mesh=split,
        in_specs=(rows, P("fsdp", CTX), *shares, rows),
        out_specs=(rows, rows, *shares),
        check_vma=False,
    )
```

```python
from functools import partial

import jax
import jax.numpy as jnp
import numpy as np
from jax import lax
from jax.experimental import pallas as pl
from jax.experimental.pallas import tpu as pltpu
from jax.sharding import Mesh
from jax.sharding import PartitionSpec as P

HD = 64
DOC_MOST = 512
EPSILON = 1e-05
NEGATIVE = -1e30
F32 = jnp.float32
FLOPS_PER_US = 2e9
BF16 = jnp.bfloat16

CTX = ("y", "core")
CHIPS = ("y", "tp")


def size_of(axes):
    return int(np.prod([lax.axis_size(a) for a in axes]))


def swap(value, axes, bits):
    count = size_of(axes)
    return lax.ppermute(value, axes, [(i, i ^ bits) for i in range(count)])


def masks_of(axes):
    bits, at = [], 1
    for a in reversed(axes):
        mine = []
        while len(mine) < (lax.axis_size(a) - 1).bit_length():
            mine.append(at)
            at *= 2
        bits = mine + bits if a == "core" else bits + mine
    masks = [0]
    for r in range(1, size_of(axes)):
        low = r & -r
        masks.append(masks[r ^ low] | bits[low.bit_length() - 1])
    return masks


def after(value, *others):
    return lax.optimization_barrier((value, *others))[0]


def kernel_call(kernel, outs, ids, arrays, scratch=(), cost=1.0, name=None, vmem=12, deps=(), anys=()):
    deps = list(deps)
    extra = len(deps)

    def run(*refs):
        kernel(*refs[:1], *refs[1 + extra :])

    def place(space):
        return pl.BlockSpec(memory_space=space)

    return pl.pallas_call(
        run,
        out_shape=[jax.ShapeDtypeStruct(s.shape, s.dtype) for s in outs],
        in_specs=[place(pltpu.SMEM)]
        + [place(pl.ANY)] * extra
        + [place(pltpu.HBM)] * len(anys)
        + [place(pltpu.VMEM)] * len(arrays),
        out_specs=[place(pltpu.VMEM)] * len(outs),
        scratch_shapes=list(scratch),
        compiler_params=pltpu.CompilerParams(vmem_limit_bytes=vmem << 20),
        cost_estimate=pl.CostEstimate(
            flops=int(cost * FLOPS_PER_US), bytes_accessed=int(cost * 1e5), transcendentals=0
        ),
        name=name,
    )(ids, *deps, *[pltpu.with_memory_space_constraint(a, pltpu.HBM) for a in anys], *arrays)


def shape(dims, dtype=BF16):
    return jax.ShapeDtypeStruct(tuple(dims), dtype)


NN = (((1,), (0,)), ((), ()))
NT = (((1,), (1,)), ((), ()))
TN = (((0,), (0,)), ((), ()))


def mm(a, b, dims):
    return lax.dot_general(a, b, dims, preferred_element_type=F32)


def at(start, size, unit=None):
    return pl.ds(pl.multiple_of(start, unit or size), size)


def normalise(values):
    centred = values - jnp.mean(values, axis=-1, keepdims=True)
    variance = jnp.mean(centred * centred, axis=-1, keepdims=True)
    scale = lax.rsqrt(variance + EPSILON)
    return centred * scale, scale


def norm_grad(vhat, scale, weighted):
    return scale * (
        weighted
        - jnp.mean(weighted, axis=-1, keepdims=True)
        - vhat * jnp.mean(weighted * vhat, axis=-1, keepdims=True)
    )


class Ids:
    def __init__(self, ref, t_count):
        self.z, self.y, self.core, self.t = ref[0], ref[1], ref[2], ref[3]
        self.c = self.y * 2 + self.core
        self.p = self.c * t_count + self.t
        self.t_count = t_count

    def rows(self, side, mask, own):
        c = (self.y ^ (mask // self.t_count)) * 2 + (self.core ^ side)
        return at((c * self.t_count + (self.t ^ (mask % self.t_count))) * own, own)


def small_rows(part, heads, z_count, rows_up, cols_up, wide):
    vec = 6 * part // wide
    q = 2 * heads * (HD // z_count)
    u = rows_up * cols_up
    q_rows, u_rows = -(-q // wide), -(-u // wide)
    total = vec + q_rows + u_rows
    return vec, q, q_rows, u, u_rows, -(-total // 16) * 16


def pick(table, index):
    row = lax.broadcasted_iota(jnp.int32, table.shape, 0)
    return jnp.sum(jnp.where(row == index, table.astype(F32), 0.0), axis=0, keepdims=True).astype(BF16)


def lay_rows(out, first, pieces, wide):
    line, used = [], 0
    for piece in [*pieces, None]:
        if piece is None or used + piece.shape[1] > wide:
            if line:
                gap = wide - used
                if gap:
                    line.append(jnp.zeros((1, gap), line[0].dtype))
                out[first : first + 1, :] = jnp.concatenate(line, axis=1) if len(line) > 1 else line[0]
                first, line, used = first + 1, [], 0
        if piece is not None:
            line.append(piece)
            used += piece.shape[1]


def copy_in(pairs, sems):
    copies = [pltpu.make_async_copy(a, b, sems.at[i]) for i, (a, b) in enumerate(pairs)]
    for copy in copies:
        copy.start()
    return copies


def pack_kernel(cfg, ids_ref, w_qkv, w_out, *refs):
    params, out, buf, bufs, sems = refs[:8], refs[8], refs[9], refs[10:18], refs[18]
    c = ids_ref[1] * 2 + ids_ref[2]
    feats = out.shape[1]
    part = w_out.shape[1]
    pairs = [
        (w_qkv.at[k, :, at(c * feats, feats)], out.at[k * part : (k + 1) * part, :]) for k in range(3)
    ]
    pairs.append((w_out.at[at(c * feats, feats), :], buf))
    copies = copy_in(pairs + list(zip(params, bufs)), sems)
    for copy in copies[3:]:
        copy.wait()
    out[3 * part : 4 * part, :] = buf[...].T
    pack_small(cfg, c, bufs[:6], bufs[6], bufs[7], out, 4 * part)
    for copy in copies[:3]:
        copy.wait()


def pack_rows_kernel(ids_ref, x, seg, cot, rows, mine, other, both, seg_buf, sems):
    t = ids_ref[3]
    span, own = x.shape[0], mine.shape[0]
    near, far = cot.at[at(t * own, own), :], cot.at[at((1 - t) * own, own), :]
    pairs = [(seg, seg_buf), (x, rows.at[:span, :])]
    pairs += [(near, mine), (far, other), (near, both.at[:own, :]), (far, both.at[own:, :])]
    copies = copy_in(pairs, sems)
    rows[span:, :] = jnp.zeros((rows.shape[0] - span, rows.shape[1]), rows.dtype)
    copies[0].wait()
    rows[span : span + 1, :span] = seg_buf[...].astype(F32).astype(BF16)
    for copy in copies[1:]:
        copy.wait()


def pack_plain_kernel(cfg, ids_ref, w_qkv, w_out, *refs):
    z_count, heads, rows_up, cols_up = cfg
    vectors, (b_qv, b_up, out) = refs[:6], refs[6:]
    part = w_out.shape[1]
    for k in range(3):
        out[k * part : (k + 1) * part, :] = w_qkv[k]
    out[3 * part : 4 * part, :] = w_out[...].T
    pack_small(cfg, ids_ref[1] * 2 + ids_ref[2], vectors, b_qv, b_up, out, 4 * part)


def pack_small(cfg, c, vectors, b_qv, b_up, out, base):
    z_count, heads, rows_up, cols_up = cfg
    wide = out.shape[1]
    part = vectors[0].shape[-1]
    vec, q, q_rows, u, u_rows, total = small_rows(part, heads, z_count, rows_up, cols_up, wide)
    out[base : base + total, :] = jnp.zeros((total, wide), out.dtype)
    per = part // wide
    for i, ref in enumerate(vectors):
        line = ref[...].reshape(1, part)
        for j in range(per):
            row = base + i * per + j
            out[row : row + 1, :] = line[:, j * wide : (j + 1) * wide]
    q_lines = [pick(b_qv[k], c * heads + h) for k in range(2) for h in range(heads)]
    lay_rows(out, base + vec, q_lines, wide)
    lay_rows(out, base + vec + q_rows, [pick(b_up[...], c * rows_up + i) for i in range(rows_up)], wide)


def first_norm_kernel(cfg, ids_ref, *refs):
    c_masks, t_count, span = cfg
    me = Ids(ids_ref, t_count)
    x, (vhat_out, seg_row, seg_col) = refs[: len(c_masks)], refs[len(c_masks) :]
    for r, mask in enumerate(c_masks):
        seg_row[:, at((me.c ^ mask) * span, span)] = x[r][span : span + 1, :span].astype(F32)
    for i in range(seg_row.shape[1] // 128):
        block = jnp.broadcast_to(seg_row[:, i * 128 : (i + 1) * 128], (128, 128))
        seg_col[i * 128 : (i + 1) * 128, :] = block.T
    step = min(64, span)
    for r, mask in enumerate(c_masks):

        def chunk(i, carry, r=r, mask=mask):
            vhat, _ = normalise(x[r][at(i * step, step), :].astype(F32))
            vhat_out[at((me.c ^ mask) * span + i * step, step), :] = vhat
            return carry

        lax.fori_loop(0, span // step, chunk, 0, unroll=True)


def unpack_kernel(cfg, ids_ref, *refs):
    z_count, heads, rows_up, cols_up = cfg
    small, (weight, out_w, vecs, bias_qv, bias_up) = refs[:z_count], refs[z_count:]
    width = weight.shape[0]
    part = width // z_count
    feats = bias_qv.shape[1]
    units = bias_up.shape[1]
    each = HD // z_count
    wide = small[0].shape[1]
    vec, q, q_rows, u, u_rows, total = small_rows(part, heads, z_count, rows_up, cols_up, wide)
    base = 4 * part
    per = part // wide
    qv = [jnp.zeros((1, feats), F32), jnp.zeros((1, feats), F32)]
    ups = jnp.zeros((1, units), F32)
    if wide % 128:
        vecs[...] = jnp.zeros(vecs.shape, F32)
    for r in range(z_count):
        z = ids_ref[0] ^ r
        where = at(z * part, part)
        for k in range(3):
            weight[where, k * feats : (k + 1) * feats] = small[r][k * part : (k + 1) * part, :]
        out_w[where, :] = small[r][3 * part : 4 * part, :]
        for i in range(6):
            for j in range(per):
                row = base + i * per + j
                line = small[r][row : row + 1, :]
                if wide % 128 == 0:
                    vecs[i : i + 1, at(z * part + j * wide, wide)] = line.astype(F32)
                else:
                    lane = lax.broadcasted_iota(jnp.int32, (wide, width), 0)
                    goal = lax.broadcasted_iota(jnp.int32, (wide, width), 1)
                    move = jnp.where(goal == z * part + j * wide + lane, 1.0, 0.0).astype(BF16)
                    vecs[i : i + 1, :] += mm(line, move, NN)
        lane = lax.broadcasted_iota(jnp.int32, (wide, feats), 0)
        goal = lax.broadcasted_iota(jnp.int32, (wide, feats), 1)
        for k in range(2):
            for i in range(q_rows):
                place = lane + i * wide - k * heads * each
                move = (place >= 0) & (place < heads * each)
                move &= goal == (place // each) * HD + z * each + place % each
                row = base + vec + i
                qv[k] += mm(small[r][row : row + 1, :], jnp.where(move, 1.0, 0.0).astype(BF16), NN)
        lane = lax.broadcasted_iota(jnp.int32, (wide, units), 0)
        goal = lax.broadcasted_iota(jnp.int32, (wide, units), 1)
        for i in range(u_rows):
            place = lane + i * wide
            move = (place < u) & (goal == (place // cols_up) * 128 + z * cols_up + place % cols_up)
            row = base + vec + q_rows + i
            ups += mm(small[r][row : row + 1, :], jnp.where(move, 1.0, 0.0).astype(BF16), NN)
    for k in range(2):
        bias_qv[k : k + 1, :] = qv[k]
    bias_up[...] = ups


def head_mask(width, head):
    lane = lax.broadcasted_iota(jnp.int32, (1, width), 1)
    return (lane // HD) == head


def attend_kernel(
    cfg, ids_ref, vhat, weight, vecs, bias_qv, seg_row, seg_col, normed, qkv, attn, keep, give, k_heads, v_heads, mask
):
    chip_masks, t_count = cfg
    me = Ids(ids_ref, t_count)
    length, feats = attn.shape
    heads = feats // HD
    tile = min(256, length)

    def project(i, carry):
        rows = at(i * tile, tile)
        x = (vhat[rows, :] * vecs[0:1, :] + vecs[1:2, :]).astype(BF16)
        normed[rows, :] = x
        out = mm(x, weight[...], NN)
        q = (out[:, :feats] + bias_qv[0:1, :]).astype(BF16)
        k = out[:, feats : 2 * feats].astype(BF16)
        v = (out[:, 2 * feats :] + bias_qv[1:2, :]).astype(BF16)
        qkv[rows, :feats] = q
        qkv[rows, feats : 2 * feats] = k
        qkv[rows, 2 * feats :] = v
        for h in range(heads):
            lanes = head_mask(feats, h)
            k_heads[h, rows, :] = jnp.where(lanes, k, jnp.zeros_like(k))
            v_heads[h, rows, :] = jnp.where(lanes, v, jnp.zeros_like(v))
        return carry

    lax.fori_loop(0, length // tile, project, 0)
    back = -(-DOC_MOST // tile)
    for i in range(length // tile):
        first = max(0, i - back) * tile
        keys = (i + 1) * tile - first
        rows = slice(i * tile, (i + 1) * tile)
        q = qkv[rows, :feats] * BF16(HD ** (-0.5))
        same = seg_col[rows, 0:1] == seg_row[:, first : first + keys]
        q_pos = i * tile + lax.broadcasted_iota(jnp.int32, (tile, keys), 0)
        k_pos = first + lax.broadcasted_iota(jnp.int32, (tile, keys), 1)
        mask[:, :keys] = jnp.where(same & (k_pos <= q_pos), 0.0, NEGATIVE)
        total = jnp.zeros((tile, feats), F32)
        for h in range(heads):
            s = mm(q, k_heads[h, first : first + keys, :], NT) + mask[:, :keys]
            e = jnp.exp(s - jnp.max(s, axis=1, keepdims=True))
            scale = 1.0 / jnp.sum(e, axis=1, keepdims=True)
            total += mm((e * scale).astype(BF16), v_heads[h, first : first + keys, :], NN)
        attn[rows, :] = total.astype(BF16)
    own = keep.shape[0] // len(chip_masks)
    for side, out in ((1, give), (0, keep)):
        for k in range(len(chip_masks)):
            out[k * own : (k + 1) * own, :] = attn[me.rows(side, chip_masks[k], own), :]


def cat_kernel(ids_ref, *refs):
    rows = refs[0].shape[0]
    for k, ref in enumerate(refs[:-1]):
        refs[-1][k * rows : (k + 1) * rows, :] = ref[...]


def beside_kernel(ids_ref, keep, landed, *pieces):
    own, both = pieces[0].shape
    for k, piece in enumerate(pieces):
        rows = slice(k * own, (k + 1) * own)
        piece[:, : both // 2] = keep[rows, :]
        piece[:, both // 2 :] = landed[rows, :]


def apart_kernel(ids_ref, *refs):
    pieces, out = refs[:-1], refs[-1]
    own, feats = pieces[0].shape[0], out.shape[1]
    for k, piece in enumerate(pieces):
        out[k * own : (k + 1) * own, :] = piece[:, feats:]


def out_norm_kernel(t_count, ids_ref, *refs):
    me = Ids(ids_ref, t_count)
    w_mine, w_other, x, vecs, residual, normed = refs[-6:]
    own, width = residual.shape
    feats = w_mine.shape[1]
    total = x[at(me.t * own, own), :].astype(F32) + vecs[2:3, :]
    for k, piece in enumerate(refs[:-6]):
        rows = slice(k * width, (k + 1) * width)
        total += mm(piece[:, :feats], w_mine[rows, :], NT) + mm(piece[:, feats:], w_other[rows, :], NT)
    residual[...] = total
    vhat, _ = normalise(total)
    normed[...] = (vhat * vecs[3:4, :] + vecs[4:5, :]).astype(BF16)


def place_kernel(ids_ref, *refs):
    blocks, out = refs[:-1], refs[-1]
    part = blocks[0].shape[0]
    for r, block in enumerate(blocks):
        out[at((ids_ref[0] ^ r) * part, part), :] = block[...]


def cut_mlp_kernel(ids_ref, w_up, w_down, up, down, buf, sems):
    c = ids_ref[1] * 2 + ids_ref[2]
    units = up.shape[1]
    one = pltpu.make_async_copy(w_up.at[:, at(c * units, units)], up, sems.at[0])
    two = pltpu.make_async_copy(w_down.at[at(c * units, units), :], buf, sems.at[1])
    one.start()
    two.start()
    two.wait()
    down[...] = buf[...].T
    one.wait()


def cot_kernel(chip_masks, t_count, ids_ref, *refs):
    both, pieces, cot = refs[:2], refs[2:-1], refs[-1]
    chips = len(chip_masks)
    own = cot.shape[0] // (2 * chips)
    for side in range(2):
        for k, mask in enumerate(chip_masks):
            to = (side * chips + k) * own
            y, t = mask // t_count, mask % t_count
            if y == 0:
                cot[to : to + own, :] = both[side][t * own : (t + 1) * own, :]
            else:
                cot[to : to + own, :] = pieces[((y - 1) * t_count + t) * 2 + side][...]


def hidden_kernel(ids_ref, normed_a, normed_b, up, bias_up, act_a, act_b, slope_a, slope_b):
    step = min(512, normed_a.shape[0])
    for normed, act, slope in ((normed_a, act_a, slope_a), (normed_b, act_b, slope_b)):

        def chunk(i, carry, normed=normed, act=act, slope=slope):
            rows = at(i * step, step)
            u = mm(normed[rows, :], up[...], NN) + bias_up[...]
            square = u * u
            th = jnp.tanh(0.7978845608028654 * (u + 0.044715 * square * u))
            act[rows, :] = (0.5 * u * (1.0 + th)).astype(BF16)
            slope[rows, :] = 0.5 * (1.0 + th) + 0.5 * u * (1.0 - th * th) * (
                0.7978845608028654 * (1.0 + 3.0 * 0.044715 * square)
            )
            return carry

        lax.fori_loop(0, normed.shape[0] // step, chunk, 0, unroll=True)


def hidden_back_kernel(side, ids_ref, slope, cot, down, up, d_up, d_norm, grad_bias):
    half = slope.shape[0]
    step = min(512, half)

    def chunk(i, total):
        rows = at(i * step, step)
        d_act = mm(cot[at(side * half + i * step, step), :], down[...], NN)
        g = (d_act * slope[rows, :]).astype(BF16)
        d_up[rows, :] = g
        d_norm[rows, :] = mm(g, up[...], NT).astype(BF16)
        return total + jnp.sum(g.astype(F32), axis=0, keepdims=True)

    grad_bias[...] = lax.fori_loop(0, half // step, chunk, jnp.zeros(grad_bias.shape, F32), unroll=True)


def down_kernel(ids_ref, act_a, act_b, down, keep, give):
    step = min(512, act_a.shape[0])
    for act, out in ((act_b, give), (act_a, keep)):

        def chunk(i, carry, act=act, out=out):
            rows = at(i * step, step)
            out[rows, :] = mm(act[rows, :], down[...], NT).astype(BF16)
            return carry

        lax.fori_loop(0, act.shape[0] // step, chunk, 0, unroll=True)


def join_kernel(ids_ref, keep, landed, *pieces):
    own = pieces[0].shape[0]
    for k, piece in enumerate(pieces):
        rows = slice(k * own, (k + 1) * own)
        piece[...] = (keep[rows, :].astype(F32) + landed[rows, :].astype(F32)).astype(BF16)


def down_grad_kernel(ids_ref, cot, act_a, act_b, *outs):
    half = act_a.shape[0]
    part = outs[0].shape[0]
    for r in range(len(outs) - 1, -1, -1):
        cols = at((ids_ref[0] ^ r) * part, part)
        total = mm(cot[:half, cols], act_a[...], TN) + mm(cot[half:, cols], act_b[...], TN)
        outs[r][...] = total.astype(BF16)


def up_grad_kernel(ids_ref, normed_a, normed_b, d_up_a, d_up_b, near_down, *outs):
    part = outs[0].shape[0]
    for r in range(len(outs) - 1, -1, -1):
        cols = at((ids_ref[0] ^ r) * part, part)
        total = mm(normed_a[:, cols], d_up_a[...], TN) + mm(normed_b[:, cols], d_up_b[...], TN)
        outs[r][:part, :] = total.astype(BF16)
    outs[1][part:, :] = near_down[...]


def add_kernel(ids_ref, a, b, out):
    out[...] = (a[...].astype(F32) + b[...].astype(F32)).astype(BF16)


def mlp_sums_kernel(ups, ids_ref, near, *refs):
    out = refs[-1]
    part = out.shape[0] // 2
    for base, terms in ((0, refs[:ups]), (part, refs[ups:-1])):
        total = near[base : base + part, :].astype(F32)
        for term in terms:
            total += term[...].astype(F32)
        out[base : base + part, :] = total.astype(BF16)


def sum_kernel(ids_ref, *refs):
    total = refs[0][...].astype(F32)
    for ref in refs[1:-1]:
        total += ref[...].astype(F32)
    refs[-1][...] = total.astype(BF16)


def second_back_kernel(cfg, ids_ref, *refs):
    chips = cfg
    landed, refs = refs[:chips], refs[chips:]
    residual, cot, vecs, w_mine, w_other, d_res, branch, grads = refs[:8]
    d_mix = refs[8:]
    own, width = residual.shape
    feats = w_mine.shape[1]
    d_norm = landed[0][...].astype(F32)
    for ref in landed[1:]:
        d_norm += ref[...].astype(F32)
    vhat, scale = normalise(residual[...])
    c = cot[...].astype(F32)
    d_residual = c + norm_grad(vhat, scale, vecs[3:4, :] * d_norm)
    d_res[...] = d_residual
    b = d_residual.astype(BF16)
    branch[...] = b
    for k, piece in enumerate(d_mix):
        rows = slice(k * width, (k + 1) * width)
        piece[:, :feats] = mm(b, w_mine[rows, :], NN).astype(BF16)
        piece[:, feats:] = mm(b, w_other[rows, :], NN).astype(BF16)
    grads[0:1, :] = jnp.sum(d_residual, axis=0, keepdims=True)
    grads[1:2, :] = jnp.sum(vhat * d_norm, axis=0, keepdims=True)
    grads[2:3, :] = jnp.sum(d_norm, axis=0, keepdims=True)
    grads[3:4, :] = jnp.sum(c, axis=0, keepdims=True)


def attend_back_kernel(cfg, ids_ref, qkv, seg_row, seg_col, *refs):
    chip_masks, t_count = cfg
    me = Ids(ids_ref, t_count)
    mixes, refs = refs[: len(chip_masks)], refs[len(chip_masks) :]
    landed, d_qkv, sums, k_heads, v_heads, q_heads, m_heads, dk, dv, mask = refs
    length, feats = qkv.shape[0], dk.shape[1]
    own = mixes[0].shape[0]
    heads = feats // HD
    tile = min(256, length)
    scale = HD ** (-0.5)
    for h in range(heads):
        lanes = head_mask(feats, h)
        for k, m in enumerate(chip_masks):
            piece = mixes[k][:, :feats]
            m_heads[h, me.rows(0, m, own), :] = jnp.where(lanes, piece, jnp.zeros_like(piece))
            piece = landed[k * own : (k + 1) * own, :]
            m_heads[h, me.rows(1, m, own), :] = jnp.where(lanes, piece, jnp.zeros_like(piece))

    def prepare(i, carry):
        rows = at(i * tile, tile)
        for h in range(heads):
            lanes = head_mask(feats, h)
            for k, ref in ((0, q_heads), (1, k_heads), (2, v_heads)):
                piece = qkv[rows, k * feats : (k + 1) * feats]
                if k == 0:
                    piece = piece * BF16(scale)
                ref[h, rows, :] = jnp.where(lanes, piece, jnp.zeros_like(piece))
        dk[rows, :] = jnp.zeros((tile, feats), F32)
        dv[rows, :] = jnp.zeros((tile, feats), F32)
        return carry

    lax.fori_loop(0, length // tile, prepare, 0)
    back = -(-DOC_MOST // tile)
    for i in range(length // tile):
        first = max(0, i - back) * tile
        keys = (i + 1) * tile - first
        rows = slice(i * tile, (i + 1) * tile)
        span = slice(first, first + keys)
        same = seg_col[span, 0:1] == seg_row[:, rows]
        k_pos = first + lax.broadcasted_iota(jnp.int32, (keys, tile), 0)
        q_pos = i * tile + lax.broadcasted_iota(jnp.int32, (keys, tile), 1)
        mask[:keys, :] = jnp.where(same & (k_pos <= q_pos), 0.0, NEGATIVE)
        dq = jnp.zeros((tile, feats), F32)
        dvs = jnp.zeros((keys, feats), F32)
        dks = jnp.zeros((keys, feats), F32)
        for h in range(heads):
            k, v, q, m = k_heads[h, span, :], v_heads[h, span, :], q_heads[h, rows, :], m_heads[h, rows, :]
            s = mm(k, q, NT) + mask[:keys, :]
            e = jnp.exp(s - jnp.max(s, axis=0, keepdims=True))
            p = e * (1.0 / jnp.sum(e, axis=0, keepdims=True))
            dp = mm(v, m, NT)
            row_dot = jnp.sum(p * dp, axis=0, keepdims=True)
            ds = (p * (dp - row_dot)).astype(BF16)
            dvs += mm(p.astype(BF16), m, NN)
            dks += mm(ds, q, NN)
            dq += mm(ds, k, TN)
        dv[span, :] += dvs
        dk[span, :] += dks
        d_qkv[rows, :feats] = (dq * scale).astype(BF16)

    def finish(i, carry):
        rows = at(i * tile, tile)
        d_qkv[rows, feats : 2 * feats] = dk[rows, :].astype(BF16)
        d_qkv[rows, 2 * feats :] = dv[rows, :].astype(BF16)
        return carry + jnp.sum(d_qkv[rows, :].astype(F32), axis=0, keepdims=True)

    sums[...] = lax.fori_loop(0, length // tile, finish, jnp.zeros((1, 3 * feats), F32))


def first_back_kernel(cfg, ids_ref, d_qkv, weight, vhat, keep, give, grads):
    chip_masks, own, t_count = cfg
    me = Ids(ids_ref, t_count)
    span = own * t_count
    gain = jnp.zeros((1, vhat.shape[1]), F32)
    bias = gain
    for out, side in ((give, 1), (keep, 0)):
        for k, mask in enumerate(chip_masks[::t_count]):
            c = (me.y ^ (mask // t_count)) * 2 + (me.core ^ side)
            rows = at(c * span, span)
            d = mm(d_qkv[rows, :], weight[...], NT)
            for t in range(t_count):
                to = at(k * span + (t ^ me.t) * own, own)
                out[to, :] = d[t * own : (t + 1) * own, :].astype(BF16)
            gain += jnp.sum(vhat[rows, :] * d, axis=0, keepdims=True)
            bias += jnp.sum(d, axis=0, keepdims=True)
    grads[0:1, :] = gain
    grads[1:2, :] = bias


def attn_grad_kernel(cfg, ids_ref, normed, d_qkv, attn, branch_a, branch_b, small, small_other, *refs):
    chip_masks, t_count, z_count, vec = cfg
    me = Ids(ids_ref, t_count)
    outs, branch = refs[:-1], refs[-1]
    own = branch_a.shape[0] // len(chip_masks)
    for side, ref in ((0, branch_a), (1, branch_b)):
        for k, mask in enumerate(chip_masks):
            branch[me.rows(side, mask, own), :] = ref[k * own : (k + 1) * own, :]
    count = small.shape[0] // z_count
    feats = attn.shape[1]
    part = normed.shape[1] // z_count
    row = lax.broadcasted_iota(jnp.int32, (count, feats), 0)
    for r in range(z_count - 1, -1, -1):
        out = outs[r]
        cols = at((me.z ^ r) * part, part)
        g = mm(normed[:, cols], d_qkv[...], TN)
        for k in range(3):
            out[k * part : (k + 1) * part, :] = g[:, k * feats : (k + 1) * feats].astype(BF16)
        out[3 * part : 4 * part, :] = mm(branch[:, cols], attn[...], TN).astype(BF16)
        mine = small[r * count : (r + 1) * count, :].astype(F32)
        both = mine + small_other[r * count : (r + 1) * count, :].astype(F32)
        out[4 * part :, :] = jnp.where(row < vec, both, mine).astype(BF16)


def last_kernel(t_count, ids_ref, *refs):
    me = Ids(ids_ref, t_count)
    x, vecs, d_res, out = refs[-4:]
    own = out.shape[0]
    d_norm = refs[0][...].astype(F32)
    for ref in refs[1:-4]:
        d_norm += ref[...].astype(F32)
    vhat, scale = normalise(x[at(me.t * own, own), :].astype(F32))
    out[...] = (d_res[...] + norm_grad(vhat, scale, vecs[0:1, :] * d_norm)).astype(BF16)


def output_kernel(ids_ref, *refs):
    residual, vecs, out = refs[-3:]
    total = residual[...] + vecs[5:6, :]
    for ref in refs[:-3]:
        total += ref[...].astype(F32)
    out[...] = total.astype(BF16)


def pair_kernel(ids_ref, mine, other, out):
    own = mine.shape[0]
    out[at(ids_ref[3] * own, own), :] = mine[...]
    out[at((1 - ids_ref[3]) * own, own), :] = other[...]


def small_grad_kernel(cfg, ids_ref, one, two, sums, bup_a, bup_b, out):
    z_count, heads, rows_up, cols_up = cfg
    width = one.shape[1]
    part = width // z_count
    feats = sums.shape[1] // 3
    units = bup_a.shape[1]
    each = HD // z_count
    wide = out.shape[1]
    vec, q, q_rows, u, u_rows, total = small_rows(part, heads, z_count, rows_up, cols_up, wide)
    per = part // wide
    bqv = (sums[:, :feats].astype(BF16), sums[:, 2 * feats :].astype(BF16))
    bup = (bup_a[...] + bup_b[...]).astype(BF16)
    out[...] = jnp.zeros(out.shape, out.dtype)
    for r in range(z_count):
        z = ids_ref[0] ^ r
        base = r * total
        for i in range(6):
            ref, row = (one, i) if i < 2 else (two, i - 2)
            for j in range(per):
                k = base + i * per + j
                if wide % 128 == 0:
                    out[k : k + 1, :] = ref[row : row + 1, at(z * part + j * wide, wide)].astype(BF16)
                else:
                    lane = lax.broadcasted_iota(jnp.int32, (wide, width), 0)
                    goal = lax.broadcasted_iota(jnp.int32, (wide, width), 1)
                    move = jnp.where(goal == z * part + j * wide + lane, 1.0, 0.0).astype(BF16)
                    out[k : k + 1, :] = mm(ref[row : row + 1, :].astype(BF16), move, NT).astype(BF16)
        lane = lax.broadcasted_iota(jnp.int32, (wide, feats), 0)
        goal = lax.broadcasted_iota(jnp.int32, (wide, feats), 1)
        for i in range(q_rows):
            line = jnp.zeros((1, wide), F32)
            for k in range(2):
                place = lane + i * wide - k * heads * each
                move = (place >= 0) & (place < heads * each)
                move &= goal == (place // each) * HD + z * each + place % each
                line += mm(bqv[k], jnp.where(move, 1.0, 0.0).astype(BF16), NT)
            out[base + vec + i : base + vec + i + 1, :] = line.astype(BF16)
        lane = lax.broadcasted_iota(jnp.int32, (wide, units), 0)
        goal = lax.broadcasted_iota(jnp.int32, (wide, units), 1)
        for i in range(u_rows):
            place = lane + i * wide
            move = (place < u) & (goal == (place // cols_up) * 128 + z * cols_up + place % cols_up)
            row = base + vec + q_rows + i
            out[row : row + 1, :] = mm(bup, jnp.where(move, 1.0, 0.0).astype(BF16), NT).astype(BF16)


def mlp_place_kernel(c_masks, ids_ref, *refs):
    blocks, (up, down) = refs[:-2], refs[-2:]
    c = ids_ref[1] * 2 + ids_ref[2]
    units = blocks[0].shape[1]
    part = blocks[0].shape[0] // 2
    for r, mask in enumerate(c_masks):
        where = at((c ^ mask) * units, units)
        up[:, where] = blocks[r][:part, :].astype(F32)
        down[where, :] = blocks[r][part:, :].astype(F32).T


def attn_place_kernel(cfg, ids_ref, *refs):
    c_masks, heads, rows_up, vec, q_rows = cfg
    blocks = refs[: len(c_masks)]
    qkv, out, vecs, b_qv, b_up = refs[len(c_masks) :]
    c = ids_ref[1] * 2 + ids_ref[2]
    wide = blocks[0].shape[1]
    part = vecs.shape[1]
    each, cols_up = b_qv.shape[2], b_up.shape[1]
    aligned = wide % 128 == 0
    for r, mask in enumerate(c_masks):
        where = at((c ^ mask) * wide, wide)
        if aligned:
            for k in range(3):
                qkv[k, :, where] = blocks[r][k * part : (k + 1) * part, :].astype(F32)
        else:
            for k in range(3):
                qkv[c ^ mask, k] = blocks[r][k * part : (k + 1) * part, :].astype(F32)
        out[where, :] = blocks[r][3 * part : 4 * part, :].astype(F32).T
        base = 4 * part + vec
        for k in range(2):
            for h in range(heads):
                flat = (k * heads + h) * each
                row, lane = base + flat // wide, flat % wide
                b_qv[k, pl.ds((c ^ mask) * heads + h, 1), :] = blocks[r][
                    row : row + 1, lane : lane + each
                ].astype(F32)
        for i in range(rows_up):
            row, lane = base + q_rows + (i * cols_up) // wide, (i * cols_up) % wide
            b_up[pl.ds((c ^ mask) * rows_up + i, 1), :] = blocks[r][
                row : row + 1, lane : lane + cols_up
            ].astype(F32)
    total = blocks[0][4 * part : 4 * part + vec, :].astype(F32)
    for block in blocks[1:]:
        total += block[4 * part : 4 * part + vec, :].astype(F32)
    per = part // wide
    for i in range(6):
        for j in range(per):
            vecs[i : i + 1, j * wide : (j + 1) * wide] = total[i * per + j : i * per + j + 1, :]


def body(
    tokens,
    segments,
    ln1_gain,
    ln1_bias,
    w_qkv,
    b_qv,
    w_out,
    b_out,
    ln2_gain,
    ln2_bias,
    w_up,
    b_up,
    w_down,
    b_down,
    cotangent,
):
    z_count, t_count, y_count = (lax.axis_size(a) for a in ("fsdp", "tp", "y"))
    z_me, y_me, core, t_me = (lax.axis_index(a) for a in ("fsdp", "y", "core", "tp"))
    ids = jnp.stack([z_me, y_me, core, t_me]).astype(jnp.int32)
    c_me = y_me * 2 + core
    c_count = size_of(CTX)
    c_masks, chip_masks = masks_of(CTX), masks_of(CHIPS)
    chips = len(chip_masks)
    x_span, cot_span = tokens[0], cotangent[0]
    span, width = x_span.shape
    length = span * c_count
    half = length // 2
    own = span // t_count
    feats = w_qkv.shape[2] // c_count
    heads = feats // HD
    units = w_up.shape[1] // c_count
    part = width // z_count
    tile = min(256, length)
    keys = min(length, (-(-DOC_MOST // tile) + 1) * tile)
    rows_up, cols_up = b_up.shape[0] // c_count, b_up.shape[1]
    vec, _, q_rows, _, _, small_count = small_rows(part, heads, z_count, rows_up, cols_up, feats)
    Z, TP = ("fsdp",), ("tp",)
    turned = jnp.swapaxes(w_qkv, 0, 1)
    raw = [ln1_gain, ln1_bias, b_out, ln2_gain, ln2_bias, b_down, b_qv, b_up]
    pack_cfg = (z_count, heads, rows_up, cols_up)
    z_all, c_all = range(z_count), range(c_count)
    known, order, cost = {}, {}, {}

    def node(make):
        def value(*index):
            if (value, index) not in known:
                known[value, index] = make(*index)
            return known[value, index]

        value.title = make.__name__
        return value

    def waits(*key):
        return order[key]() if key in order else []

    def move(key, value, axes, bits):
        pins = waits(*key)
        return swap(after(value, *pins) if pins else value, axes, bits)

    def run(key, kernel, outs, arrays, index=(), **more):
        deps = waits(key, *index)
        declared = cost.get(key, 0.1)
        return kernel_call(kernel, outs, ids, arrays, deps=deps, cost=declared, name=key.title, **more)

    def gathered(key, source, axes, r):
        low = r & -r
        return move((key, r), key(r ^ low), axes, low) if r else source

    def from_chip(key, source, k):
        return move((key, k), source, CHIPS, chip_masks[k]) if k else source

    @node
    def pack():
        out = [shape((4 * part + small_count, feats))]
        if feats % 128:
            cuts = [
                lax.dynamic_slice_in_dim(turned, c_me * feats, feats, 2),
                lax.dynamic_slice_in_dim(w_out, c_me * feats, feats, 0),
            ]
            return run(pack, partial(pack_plain_kernel, pack_cfg), out, [*cuts, *raw])
        scratch = [pltpu.VMEM((feats, part), BF16), *[pltpu.VMEM(v.shape, BF16) for v in raw]]
        return run(
            pack,
            partial(pack_kernel, pack_cfg),
            out,
            [],
            anys=[turned, w_out, *raw],
            scratch=[*scratch, pltpu.SemaphoreType.DMA((12,))],
        )

    @node
    def rows():
        outs = [shape((span + 16, width)), shape((own, width)), shape((own, width)), shape((span, width))]
        return run(
            rows,
            pack_rows_kernel,
            outs,
            [],
            anys=[x_span, segments, cot_span],
            scratch=[pltpu.VMEM((1, span), jnp.int32), pltpu.SemaphoreType.DMA((6,))],
        )

    @node
    def norm():
        return run(
            norm,
            partial(first_norm_kernel, (c_masks, t_count, span)),
            [shape((length, width), F32), shape((1, length), F32), shape((length, 128), F32)],
            [x(r) for r in c_all],
        )

    @node
    def cut():
        return run(
            cut,
            cut_mlp_kernel,
            [shape((part, units))] * 2,
            [],
            anys=[w_up, w_down],
            scratch=[pltpu.VMEM((units, part), BF16), pltpu.SemaphoreType.DMA((2,))],
        )

    @node
    def unpack():
        return run(
            unpack,
            partial(unpack_kernel, pack_cfg),
            [
                shape((width, 3 * feats)),
                shape((width, feats)),
                shape((8, width), F32),
                shape((2, feats), F32),
                shape((1, units), F32),
            ],
            [attn(r) for r in z_all],
        )

    @node
    def attend():
        vhat, seg_row, seg_col = norm()
        qkv_full, _, vecs, bias_qv, _ = unpack()
        return run(
            attend,
            partial(attend_kernel, (chip_masks, t_count)),
            [
                shape((length, width)),
                shape((length, 3 * feats)),
                shape((length, feats)),
                shape((half, feats)),
                shape((half, feats)),
            ],
            [vhat, qkv_full, vecs, bias_qv, seg_row, seg_col],
            scratch=[pltpu.VMEM((heads, length, feats), BF16)] * 2 + [pltpu.VMEM((tile, keys), F32)],
        )

    def cat(key, blocks):
        size, cols = blocks[0].shape
        return run(key, cat_kernel, [shape((size * len(blocks), cols))], blocks)

    @node
    def wcat():
        return cat(wcat, [wout(k) for k in range(chips)])

    @node
    def beside():
        pieces = [shape((own, 2 * feats))] * chips
        return run(beside, beside_kernel, pieces, [attend()[3], give_mix()])

    @node
    def out_norm():
        return run(
            out_norm,
            partial(out_norm_kernel, t_count),
            [shape((own, width), F32), shape((own, width))],
            [*[mixed(k) for k in range(chips)], wcat()[0], w_other(), rows()[0], unpack()[2]],
        )

    @node
    def ncat():
        return cat(ncat, [normed(k) for k in range(chips)])

    @node
    def cots():
        pieces = []
        for y in range(1, y_count):
            pieces += [cot_a(y), cot_a_core(y), cot_b(y), cot_b_core(y)]
        return run(
            cots,
            partial(cot_kernel, chip_masks, t_count),
            [shape((length, width))],
            [rows()[3], cot_core(), *pieces],
        )

    @node
    def up_full():
        return run(up_full, place_kernel, [shape((width, units))], [up(r) for r in z_all])

    @node
    def down_full():
        return run(down_full, place_kernel, [shape((width, units))], [down_w(r) for r in z_all])

    @node
    def hidden():
        return run(
            hidden,
            hidden_kernel,
            [shape((half, units))] * 2 + [shape((half, units), F32)] * 2,
            [ncat()[0], normed_b(), up_full()[0], unpack()[4]],
        )

    def back(key, side):
        return run(
            key,
            partial(hidden_back_kernel, side),
            [shape((half, units)), shape((half, width)), shape((1, units), F32)],
            [hidden()[2 + side], cots()[0], down_full()[0], up_full()[0]],
        )

    def join(key, keep, give):
        return run(key, join_kernel, [shape((own, width))] * chips, [keep, give])

    @node
    def grad_down():
        return run(
            grad_down,
            down_grad_kernel,
            [shape((part, units))] * z_count,
            [cots()[0], hidden()[0], hidden()[1]],
        )

    @node
    def grad_up():
        return run(
            grad_up,
            up_grad_kernel,
            [shape((part if r != 1 else 2 * part, units)) for r in z_all],
            [ncat()[0], normed_b(), back_a()[0], back_b()[0], grad_down()[1]],
        )

    @node
    def down():
        return run(
            down,
            down_kernel,
            [shape((half, width))] * 2,
            [hidden()[0], hidden()[1], down_full()[0]],
        )

    def z_total(key, arrived, pieces, r):
        value = pieces[r]
        for low in (1, 2, 4):
            if low < (r & -r) and r | low < z_count:
                out = [shape(value.shape)]
                (value,) = run(key, add_kernel, out, [value, arrived(r | low)], index=(r,))
        return value

    def z_ends(arrived):
        return [arrived(r) for r in z_all if r > 1 and r == r & -r]

    @node
    def mlp_sums():
        ups = [grad_up()[0], *z_ends(du_in)]
        downs = [grad_down()[0], *z_ends(dd_in)]
        return run(
            mlp_sums,
            partial(mlp_sums_kernel, len(ups)),
            [shape((2 * part, units))],
            [near(), *ups, *downs],
        )

    @node
    def res_back():
        return run(
            res_back,
            partial(second_back_kernel, chips),
            [shape((own, width), F32), shape((own, width)), shape((4, width), F32)]
            + [shape((own, 2 * feats))] * chips,
            [
                *[two(k) for k in range(chips)],
                out_norm()[0],
                rows()[1],
                unpack()[2],
                wcat()[0],
                w_other(),
            ],
        )

    @node
    def apart():
        return run(apart, apart_kernel, [shape((half, feats))], [d_mix(k) for k in range(chips)])

    @node
    def attend_back():
        return run(
            attend_back,
            partial(attend_back_kernel, (chip_masks, t_count)),
            [shape((length, 3 * feats)), shape((1, 3 * feats), F32)],
            [
                attend()[1],
                norm()[1],
                norm()[2],
                *[d_mix(k) for k in range(chips)],
                d_mix_core(),
            ],
            scratch=[pltpu.VMEM((heads, length, feats), BF16)] * 4
            + [pltpu.VMEM((length, feats), F32)] * 2
            + [pltpu.VMEM((keys, tile), F32)],
        )

    @node
    def bcat():
        return cat(bcat, [branch(k) for k in range(chips)])

    @node
    def norm_back():
        return run(
            norm_back,
            partial(first_back_kernel, (chip_masks, own, t_count)),
            [shape((half, width)), shape((half, width)), shape((2, width), F32)],
            [attend_back()[0], unpack()[0], norm()[0]],
        )

    @node
    def small():
        return run(
            small,
            partial(small_grad_kernel, (z_count, heads, rows_up, cols_up)),
            [shape((z_count * small_count, feats))],
            [norm_back()[2], res_back()[2], attend_back()[1], back_a()[2], back_b()[2]],
        )

    @node
    def grad_attn():
        return run(
            grad_attn,
            partial(attn_grad_kernel, (chip_masks, t_count, z_count, vec)),
            [shape((4 * part + small_count, feats))] * z_count,
            [
                attend()[0],
                attend_back()[0],
                attend()[2],
                bcat()[0],
                branch_b(),
                small()[0],
                small_tp(),
            ],
            scratch=[pltpu.VMEM((length, width), BF16)],
        )

    @node
    def attn_sums():
        terms = [grad_attn()[0], da_in(1), *z_ends(da_in)]
        return run(attn_sums, sum_kernel, [shape(terms[0].shape)], terms)

    @node
    def last():
        return run(
            last,
            partial(last_kernel, t_count),
            [shape((own, width))],
            [*[one(k) for k in range(chips)], rows()[0], unpack()[2], res_back()[0]],
        )

    @node
    def out():
        arrays = [*[down_in(k) for k in range(chips)], out_norm()[0], unpack()[2]]
        return run(out, output_kernel, [shape((own, width))], arrays)

    def pair(key, mine, other):
        return run(key, pair_kernel, [shape((span, width))], [mine, other])

    @node
    def mlp_place():
        return run(
            mlp_place,
            partial(mlp_place_kernel, c_masks),
            [shape((part, c_count * units), F32), shape((c_count * units, part), F32)],
            [mlp_all(r) for r in c_all],
        )

    @node
    def attn_place():
        return run(
            attn_place,
            partial(attn_place_kernel, (c_masks, heads, rows_up, vec, q_rows)),
            [
                shape((3, part, c_count * feats) if feats % 128 == 0 else (c_count, 3, part, feats), F32),
                shape((c_count * feats, part), F32),
                shape((8, part), F32),
                shape(b_qv.shape, F32),
                shape(b_up.shape, F32),
            ],
            [attn_all(r) for r in c_all],
        )

    @node
    def back_a():
        return back(back_a, 0)

    @node
    def back_b():
        return back(back_b, 1)

    @node
    def join_two():
        return join(join_two, back_a()[1], give_two())

    @node
    def join_down():
        return join(join_down, down()[0], give_down())

    @node
    def join_one():
        return join(join_one, norm_back()[0], give_one())

    @node
    def pair_out():
        return pair(pair_out, out()[0], out_tp())

    @node
    def pair_tok():
        return pair(pair_tok, last()[0], last_tp())

    @node
    def dd_sum(r):
        return z_total(dd_sum, dd_in, grad_down(), r)

    @node
    def du_sum(r):
        return z_total(du_sum, du_in, grad_up(), r)

    @node
    def da_sum(r):
        return z_total(da_sum, da_in, grad_attn(), r)

    attn = node(lambda r: gathered(attn, pack()[0], Z, r))
    x = node(lambda r: gathered(x, rows()[0], CTX, r))
    up = node(lambda r: gathered(up, cut()[0], Z, r))
    down_w = node(lambda r: gathered(down_w, cut()[1], Z, r))
    cot_core = node(lambda: move((cot_core,), rows()[3], CTX, 1))
    cot_a = node(lambda y: move((cot_a, y), rows()[1], CTX, 2 * y))
    cot_b = node(lambda y: move((cot_b, y), rows()[2], CTX, 2 * y))
    cot_a_core = node(lambda y: move((cot_a_core, y), cot_a(y), CTX, 1))
    cot_b_core = node(lambda y: move((cot_b_core, y), cot_b(y), CTX, 1))
    wout = node(lambda k: from_chip(wout, unpack()[1], k))
    w_other = node(lambda: move((w_other,), wcat()[0], CTX, 1))
    give_mix = node(lambda: move((give_mix,), attend()[4], CTX, 1))
    mixed = node(lambda k: from_chip(mixed, beside()[k], k))
    normed = node(lambda k: from_chip(normed, out_norm()[1], k))
    normed_b = node(lambda: move((normed_b,), ncat()[0], CTX, 1))
    give_two = node(lambda: move((give_two,), back_b()[1], CTX, 1))
    two = node(lambda k: from_chip(two, join_two()[k], k))
    give_down = node(lambda: move((give_down,), down()[1], CTX, 1))
    down_in = node(lambda k: from_chip(down_in, join_down()[k], k))
    give_one = node(lambda: move((give_one,), norm_back()[1], CTX, 1))
    one = node(lambda k: from_chip(one, join_one()[k], k))
    d_mix = node(lambda k: from_chip(d_mix, res_back()[3 + k], k))
    d_mix_core = node(lambda: move((d_mix_core,), apart()[0], CTX, 1))
    branch = node(lambda k: from_chip(branch, res_back()[1], k))
    branch_b = node(lambda: move((branch_b,), bcat()[0], CTX, 1))
    small_tp = node(lambda: move((small_tp,), small()[0], TP, 1))
    near = node(lambda: move((near,), grad_up()[1], Z, 1))
    dd_in = node(lambda r: move((dd_in, r), dd_sum(r), Z, r & -r))
    du_in = node(lambda r: move((du_in, r), du_sum(r), Z, r & -r))
    da_in = node(lambda r: move((da_in, r), da_sum(r), Z, r & -r))
    out_tp = node(lambda: move((out_tp,), out()[0], TP, 1))
    last_tp = node(lambda: move((last_tp,), last()[0], TP, 1))
    mlp_all = node(lambda r: gathered(mlp_all, mlp_sums()[0], CTX, r))
    attn_all = node(lambda r: gathered(attn_all, attn_sums()[0], CTX, r))

    order |= {
        (x, 3): lambda: [attn(1), attn(2)],
        (cut,): lambda: [norm()[1]],
        (unpack,): lambda: [norm()[1], cut()[0], cot_a(1)],
        (attend,): lambda: [up(1), attn(3)],
        (wcat,): lambda: [attend()[4], up(1), up(2)],
        (beside,): lambda: [wcat()[0]],
        (out_norm,): lambda: [up(3)],
        (ncat,): lambda: [down_w(1), down_w(2)],
        (cots,): lambda: [ncat()[0]],
        (up_full,): lambda: [cots()[0]],
        (down_full,): lambda: [hidden()[0]],
        (grad_down,): lambda: [up_full()[0]],
        (grad_up,): lambda: [join_two()[0], dd_in(3)],
        (dd_sum, 2): lambda: [down()[0]],
        (res_back,): lambda: [down()[0]],
        (apart,): lambda: [du_sum(2)],
        (branch, 1): lambda: [res_back()[3]],
        (branch, 2): lambda: [res_back()[0], du_sum(2)],
        (branch, 3): lambda: [apart()[0]],
        (attend_back,): lambda: [dd_in(2), d_mix(3)],
        (mlp_sums,): lambda: [attend_back()[0], d_mix(3)],
        (bcat,): lambda: [mlp_sums()[0]],
        (join_one,): lambda: [grad_attn()[0], give_one(), mlp_all(1)],
        (mlp_all, 3): lambda: [join_one()[0]],
        (da_sum, 2): lambda: [join_one()[0], small()[0]],
        (join_down,): lambda: [join_one()[0]],
        (last,): lambda: [da_sum(2), mlp_all(1), mlp_all(2), down_in(1)],
        (dd_in, 3): lambda: [down_w(3)],
        (small,): lambda: [branch(2), bcat()[0]],
        (normed_b,): lambda: [mixed(2)],
        (near,): lambda: [du_in(3)],
        (last_tp,): lambda: [da_in(2), down_in(2)],
        (da_in, 3): lambda: [small_tp()],
        (two, 3): lambda: [normed_b()],
        (give_two,): lambda: [grad_down()[0]],
        (down_in, 1): lambda: [grad_attn()[0]],
        (two, 2): lambda: [normed(2)],
        (mixed, 2): lambda: [wout(1)],
        (give_one,): lambda: [branch(3)],
        (cot_a_core, 1): lambda: [wout(3)],
    }
    cost |= {
        pack: 2,
        norm: 8,
        cut: 1,
        unpack: 1,
        attend: 9,
        out_norm: 8,
        cots: 4,
        up_full: 0.5,
        down_full: 8,
        hidden: 0.3,
        grad_down: 8,
        back_a: 1,
        back_b: 2,
        grad_up: 1.5,
        down: 2.5,
        res_back: 0.01,
        attend_back: 8,
        small: 8,
        grad_attn: 2.5,
        last: 1,
        out: 1,
        pair_out: 1,
        pair_tok: 1,
        mlp_place: 1,
        attn_place: 1,
        beside: 8,
        ncat: 16,
        attn_sums: 4,
        da_sum: 1,
        bcat: 1,
    }
    full_qkv, full_out, vec_sum, full_bqv, full_bup = attn_place()
    if feats % 128:
        full_qkv = full_qkv.transpose(1, 2, 0, 3).reshape(3, part, c_count * feats)
    full_up, full_down = mlp_place()
    return (
        pair_out()[0][None],
        pair_tok()[0][None],
        vec_sum[0],
        vec_sum[1],
        jnp.swapaxes(full_qkv, 0, 1),
        full_bqv,
        full_out,
        vec_sum[2],
        vec_sum[3],
        vec_sum[4],
        full_up,
        full_bup,
        full_down,
        vec_sum[5],
    )


def solution(mesh):
    fsdp, ctx, tp = (mesh.shape[a] for a in ("fsdp", "ctx", "tp"))
    split = Mesh(mesh.devices.reshape(fsdp, ctx // 2, 2, tp), ("fsdp", "y", "core", "tp"))
    rows = P("fsdp", CTX, None)
    shares = (
        P("fsdp"),
        P("fsdp"),
        P("fsdp", None, "tp"),
        P(None, "tp", "fsdp"),
        P("tp", "fsdp"),
        P("fsdp"),
        P("fsdp"),
        P("fsdp"),
        P("fsdp", "tp"),
        P("tp", "fsdp"),
        P("tp", "fsdp"),
        P("fsdp"),
    )
    return jax.shard_map(
        body,
        mesh=split,
        in_specs=(rows, P("fsdp", CTX), *shares, rows),
        out_specs=(rows, rows, *shares),
        check_vma=False,
    )
```

```python
from functools import partial

import jax
import jax.numpy as jnp
import numpy as np
from jax import lax
from jax.experimental import pallas as pl
from jax.experimental.pallas import tpu as pltpu
from jax.sharding import Mesh
from jax.sharding import PartitionSpec as P

HD = 64
DOC_MOST = 512
EPSILON = 1e-05
NEGATIVE = -1e30
F32 = jnp.float32
FLOPS_PER_US = 2e9
BF16 = jnp.bfloat16

CTX = ("y", "core")
CHIPS = ("y", "tp")


def size_of(axes):
    return int(np.prod([lax.axis_size(a) for a in axes]))


def swap(value, axes, bits):
    count = size_of(axes)
    return lax.ppermute(value, axes, [(i, i ^ bits) for i in range(count)])


def masks_of(axes):
    bits, at = [], 1
    for a in reversed(axes):
        mine = []
        while len(mine) < (lax.axis_size(a) - 1).bit_length():
            mine.append(at)
            at *= 2
        bits = mine + bits if a == "core" else bits + mine
    masks = [0]
    for r in range(1, size_of(axes)):
        low = r & -r
        masks.append(masks[r ^ low] | bits[low.bit_length() - 1])
    return masks


def after(value, *others):
    return lax.optimization_barrier((value, *others))[0]


def kernel_call(kernel, outs, ids, arrays, scratch=(), cost=1.0, name=None, vmem=12, deps=(), anys=()):
    deps = list(deps)
    extra = len(deps)

    def run(*refs):
        kernel(*refs[:1], *refs[1 + extra :])

    def place(space):
        return pl.BlockSpec(memory_space=space)

    return pl.pallas_call(
        run,
        out_shape=[jax.ShapeDtypeStruct(s.shape, s.dtype) for s in outs],
        in_specs=[place(pltpu.SMEM)]
        + [place(pl.ANY)] * extra
        + [place(pltpu.HBM)] * len(anys)
        + [place(pltpu.VMEM)] * len(arrays),
        out_specs=[place(pltpu.VMEM)] * len(outs),
        scratch_shapes=list(scratch),
        compiler_params=pltpu.CompilerParams(vmem_limit_bytes=vmem << 20),
        cost_estimate=pl.CostEstimate(
            flops=int(cost * FLOPS_PER_US), bytes_accessed=int(cost * 1e5), transcendentals=0
        ),
        name=name,
    )(ids, *deps, *[pltpu.with_memory_space_constraint(a, pltpu.HBM) for a in anys], *arrays)


def shape(dims, dtype=BF16):
    return jax.ShapeDtypeStruct(tuple(dims), dtype)


NN = (((1,), (0,)), ((), ()))
NT = (((1,), (1,)), ((), ()))
TN = (((0,), (0,)), ((), ()))


def mm(a, b, dims):
    return lax.dot_general(a, b, dims, preferred_element_type=F32)


def at(start, size, unit=None):
    return pl.ds(pl.multiple_of(start, unit or size), size)


def normalise(values):
    centred = values - jnp.mean(values, axis=-1, keepdims=True)
    variance = jnp.mean(centred * centred, axis=-1, keepdims=True)
    scale = lax.rsqrt(variance + EPSILON)
    return centred * scale, scale


def norm_grad(vhat, scale, weighted):
    return scale * (
        weighted
        - jnp.mean(weighted, axis=-1, keepdims=True)
        - vhat * jnp.mean(weighted * vhat, axis=-1, keepdims=True)
    )


class Ids:
    def __init__(self, ref, t_count):
        self.z, self.y, self.core, self.t = ref[0], ref[1], ref[2], ref[3]
        self.c = self.y * 2 + self.core
        self.p = self.c * t_count + self.t
        self.t_count = t_count

    def rows(self, side, mask, own):
        c = (self.y ^ (mask // self.t_count)) * 2 + (self.core ^ side)
        return at((c * self.t_count + (self.t ^ (mask % self.t_count))) * own, own)


def small_rows(part, heads, z_count, rows_up, cols_up, wide):
    vec = 6 * part // wide
    q = 2 * heads * (HD // z_count)
    u = rows_up * cols_up
    q_rows, u_rows = -(-q // wide), -(-u // wide)
    total = vec + q_rows + u_rows
    return vec, q, q_rows, u, u_rows, -(-total // 16) * 16


def pick(table, index):
    row = lax.broadcasted_iota(jnp.int32, table.shape, 0)
    return jnp.sum(jnp.where(row == index, table.astype(F32), 0.0), axis=0, keepdims=True).astype(BF16)


def lay_rows(out, first, pieces, wide):
    line, used = [], 0
    for piece in [*pieces, None]:
        if piece is None or used + piece.shape[1] > wide:
            if line:
                gap = wide - used
                if gap:
                    line.append(jnp.zeros((1, gap), line[0].dtype))
                out[first : first + 1, :] = jnp.concatenate(line, axis=1) if len(line) > 1 else line[0]
                first, line, used = first + 1, [], 0
        if piece is not None:
            line.append(piece)
            used += piece.shape[1]


def copy_in(pairs, sems):
    copies = [pltpu.make_async_copy(a, b, sems.at[i]) for i, (a, b) in enumerate(pairs)]
    for copy in copies:
        copy.start()
    return copies


def pack_kernel(cfg, ids_ref, w_qkv, w_out, *refs):
    params, out, buf, bufs, sems = refs[:8], refs[8], refs[9], refs[10:18], refs[18]
    c = ids_ref[1] * 2 + ids_ref[2]
    feats = out.shape[1]
    part = w_out.shape[1]
    pairs = [
        (w_qkv.at[k, :, at(c * feats, feats)], out.at[k * part : (k + 1) * part, :]) for k in range(3)
    ]
    pairs.append((w_out.at[at(c * feats, feats), :], buf))
    copies = copy_in(pairs + list(zip(params, bufs)), sems)
    for copy in copies[3:]:
        copy.wait()
    out[3 * part : 4 * part, :] = buf[...].T
    pack_small(cfg, c, bufs[:6], bufs[6], bufs[7], out, 4 * part)
    for copy in copies[:3]:
        copy.wait()


def pack_rows_kernel(ids_ref, cot, mine, other, both, sems):
    t = ids_ref[3]
    own = mine.shape[0]
    near, far = cot.at[at(t * own, own), :], cot.at[at((1 - t) * own, own), :]
    pairs = [(near, mine), (far, other), (near, both.at[:own, :]), (far, both.at[own:, :])]
    for copy in copy_in(pairs, sems):
        copy.wait()


def pack_plain_kernel(cfg, ids_ref, w_qkv, w_out, *refs):
    z_count, heads, rows_up, cols_up = cfg
    vectors, (b_qv, b_up, out) = refs[:6], refs[6:]
    part = w_out.shape[1]
    for k in range(3):
        out[k * part : (k + 1) * part, :] = w_qkv[k]
    out[3 * part : 4 * part, :] = w_out[...].T
    pack_small(cfg, ids_ref[1] * 2 + ids_ref[2], vectors, b_qv, b_up, out, 4 * part)


def pack_small(cfg, c, vectors, b_qv, b_up, out, base):
    z_count, heads, rows_up, cols_up = cfg
    wide = out.shape[1]
    part = vectors[0].shape[-1]
    vec, q, q_rows, u, u_rows, total = small_rows(part, heads, z_count, rows_up, cols_up, wide)
    out[base : base + total, :] = jnp.zeros((total, wide), out.dtype)
    per = part // wide
    for i, ref in enumerate(vectors):
        line = ref[...].reshape(1, part)
        for j in range(per):
            row = base + i * per + j
            out[row : row + 1, :] = line[:, j * wide : (j + 1) * wide]
    q_lines = [pick(b_qv[k], c * heads + h) for k in range(2) for h in range(heads)]
    lay_rows(out, base + vec, q_lines, wide)
    lay_rows(out, base + vec + q_rows, [pick(b_up[...], c * rows_up + i) for i in range(rows_up)], wide)


def first_norm_kernel(cfg, ids_ref, *refs):
    c_masks, t_count = cfg
    me = Ids(ids_ref, t_count)
    count = len(c_masks)
    x, seg, (vhat_out, seg_row, seg_col) = refs[:count], refs[count : 2 * count], refs[2 * count :]
    span = x[0].shape[0]
    for r, mask in enumerate(c_masks):
        seg_row[:, at((me.c ^ mask) * span, span)] = seg[r][...].astype(F32)
    for i in range(seg_row.shape[1] // 128):
        block = jnp.broadcast_to(seg_row[:, i * 128 : (i + 1) * 128], (128, 128))
        seg_col[i * 128 : (i + 1) * 128, :] = block.T
    step = min(64, span)
    for r, mask in enumerate(c_masks):

        def chunk(i, carry, r=r, mask=mask):
            vhat, _ = normalise(x[r][at(i * step, step), :].astype(F32))
            vhat_out[at((me.c ^ mask) * span + i * step, step), :] = vhat
            return carry

        lax.fori_loop(0, span // step, chunk, 0, unroll=True)


def unpack_kernel(cfg, ids_ref, *refs):
    z_count, heads, rows_up, cols_up = cfg
    small, (weight, out_w, vecs, bias_qv, bias_up) = refs[:z_count], refs[z_count:]
    width = weight.shape[0]
    part = width // z_count
    feats = bias_qv.shape[1]
    units = bias_up.shape[1]
    each = HD // z_count
    wide = small[0].shape[1]
    vec, q, q_rows, u, u_rows, total = small_rows(part, heads, z_count, rows_up, cols_up, wide)
    base = 4 * part
    per = part // wide
    qv = [jnp.zeros((1, feats), F32), jnp.zeros((1, feats), F32)]
    ups = jnp.zeros((1, units), F32)
    if wide % 128:
        vecs[...] = jnp.zeros(vecs.shape, F32)
    for r in range(z_count):
        z = ids_ref[0] ^ r
        where = at(z * part, part)
        for k in range(3):
            weight[where, k * feats : (k + 1) * feats] = small[r][k * part : (k + 1) * part, :]
        out_w[where, :] = small[r][3 * part : 4 * part, :]
        for i in range(6):
            for j in range(per):
                row = base + i * per + j
                line = small[r][row : row + 1, :]
                if wide % 128 == 0:
                    vecs[i : i + 1, at(z * part + j * wide, wide)] = line.astype(F32)
                else:
                    lane = lax.broadcasted_iota(jnp.int32, (wide, width), 0)
                    goal = lax.broadcasted_iota(jnp.int32, (wide, width), 1)
                    move = jnp.where(goal == z * part + j * wide + lane, 1.0, 0.0).astype(BF16)
                    vecs[i : i + 1, :] += mm(line, move, NN)
        lane = lax.broadcasted_iota(jnp.int32, (wide, feats), 0)
        goal = lax.broadcasted_iota(jnp.int32, (wide, feats), 1)
        for k in range(2):
            for i in range(q_rows):
                place = lane + i * wide - k * heads * each
                move = (place >= 0) & (place < heads * each)
                move &= goal == (place // each) * HD + z * each + place % each
                row = base + vec + i
                qv[k] += mm(small[r][row : row + 1, :], jnp.where(move, 1.0, 0.0).astype(BF16), NN)
        lane = lax.broadcasted_iota(jnp.int32, (wide, units), 0)
        goal = lax.broadcasted_iota(jnp.int32, (wide, units), 1)
        for i in range(u_rows):
            place = lane + i * wide
            move = (place < u) & (goal == (place // cols_up) * 128 + z * cols_up + place % cols_up)
            row = base + vec + q_rows + i
            ups += mm(small[r][row : row + 1, :], jnp.where(move, 1.0, 0.0).astype(BF16), NN)
    for k in range(2):
        bias_qv[k : k + 1, :] = qv[k]
    bias_up[...] = ups


def head_mask(width, head):
    lane = lax.broadcasted_iota(jnp.int32, (1, width), 1)
    return (lane // HD) == head


def attend_kernel(
    cfg, ids_ref, vhat, weight, vecs, bias_qv, seg_row, seg_col, normed, qkv, attn, keep, give, k_heads, v_heads, mask
):
    chip_masks, t_count = cfg
    me = Ids(ids_ref, t_count)
    length, feats = attn.shape
    heads = feats // HD
    tile = min(256, length)

    def project(i, carry):
        rows = at(i * tile, tile)
        x = (vhat[rows, :] * vecs[0:1, :] + vecs[1:2, :]).astype(BF16)
        normed[rows, :] = x
        out = mm(x, weight[...], NN)
        q = (out[:, :feats] + bias_qv[0:1, :]).astype(BF16)
        k = out[:, feats : 2 * feats].astype(BF16)
        v = (out[:, 2 * feats :] + bias_qv[1:2, :]).astype(BF16)
        qkv[rows, :feats] = q
        qkv[rows, feats : 2 * feats] = k
        qkv[rows, 2 * feats :] = v
        for h in range(heads):
            lanes = head_mask(feats, h)
            k_heads[h, rows, :] = jnp.where(lanes, k, jnp.zeros_like(k))
            v_heads[h, rows, :] = jnp.where(lanes, v, jnp.zeros_like(v))
        return carry

    lax.fori_loop(0, length // tile, project, 0)
    back = -(-DOC_MOST // tile)
    for i in range(length // tile):
        first = max(0, i - back) * tile
        keys = (i + 1) * tile - first
        rows = slice(i * tile, (i + 1) * tile)
        q = qkv[rows, :feats] * BF16(HD ** (-0.5))
        same = seg_col[rows, 0:1] == seg_row[:, first : first + keys]
        q_pos = i * tile + lax.broadcasted_iota(jnp.int32, (tile, keys), 0)
        k_pos = first + lax.broadcasted_iota(jnp.int32, (tile, keys), 1)
        mask[:, :keys] = jnp.where(same & (k_pos <= q_pos), 0.0, NEGATIVE)
        total = jnp.zeros((tile, feats), F32)
        for h in range(heads):
            s = mm(q, k_heads[h, first : first + keys, :], NT) + mask[:, :keys]
            e = jnp.exp(s - jnp.max(s, axis=1, keepdims=True))
            scale = 1.0 / jnp.sum(e, axis=1, keepdims=True)
            total += mm((e * scale).astype(BF16), v_heads[h, first : first + keys, :], NN)
        attn[rows, :] = total.astype(BF16)
    own = keep.shape[0] // len(chip_masks)
    for side, out in ((1, give), (0, keep)):
        for k in range(len(chip_masks)):
            out[k * own : (k + 1) * own, :] = attn[me.rows(side, chip_masks[k], own), :]


def cat_kernel(ids_ref, *refs):
    rows = refs[0].shape[0]
    for k, ref in enumerate(refs[:-1]):
        refs[-1][k * rows : (k + 1) * rows, :] = ref[...]


def beside_kernel(ids_ref, keep, landed, *pieces):
    own, both = pieces[0].shape
    for k, piece in enumerate(pieces):
        rows = slice(k * own, (k + 1) * own)
        piece[:, : both // 2] = keep[rows, :]
        piece[:, both // 2 :] = landed[rows, :]


def apart_kernel(ids_ref, *refs):
    pieces, out = refs[:-1], refs[-1]
    own, feats = pieces[0].shape[0], out.shape[1]
    for k, piece in enumerate(pieces):
        out[k * own : (k + 1) * own, :] = piece[:, feats:]


def out_norm_kernel(t_count, ids_ref, *refs):
    me = Ids(ids_ref, t_count)
    w_mine, w_other, x, vecs, residual, normed = refs[-6:]
    own, width = residual.shape
    feats = w_mine.shape[1]
    total = x[at(me.t * own, own), :].astype(F32) + vecs[2:3, :]
    for k, piece in enumerate(refs[:-6]):
        rows = slice(k * width, (k + 1) * width)
        total += mm(piece[:, :feats], w_mine[rows, :], NT) + mm(piece[:, feats:], w_other[rows, :], NT)
    residual[...] = total
    vhat, _ = normalise(total)
    normed[...] = (vhat * vecs[3:4, :] + vecs[4:5, :]).astype(BF16)


def place_kernel(ids_ref, *refs):
    blocks, out = refs[:-1], refs[-1]
    part = blocks[0].shape[0]
    for r, block in enumerate(blocks):
        out[at((ids_ref[0] ^ r) * part, part), :] = block[...]


def cut_mlp_kernel(ids_ref, w_up, w_down, up, down, buf, sems):
    c = ids_ref[1] * 2 + ids_ref[2]
    units = up.shape[1]
    one = pltpu.make_async_copy(w_up.at[:, at(c * units, units)], up, sems.at[0])
    two = pltpu.make_async_copy(w_down.at[at(c * units, units), :], buf, sems.at[1])
    one.start()
    two.start()
    two.wait()
    down[...] = buf[...].T
    one.wait()


def cot_kernel(chip_masks, t_count, ids_ref, *refs):
    both, pieces, cot = refs[:2], refs[2:-1], refs[-1]
    chips = len(chip_masks)
    own = cot.shape[0] // (2 * chips)
    for side in range(2):
        for k, mask in enumerate(chip_masks):
            to = (side * chips + k) * own
            y, t = mask // t_count, mask % t_count
            if y == 0:
                cot[to : to + own, :] = both[side][t * own : (t + 1) * own, :]
            else:
                cot[to : to + own, :] = pieces[((y - 1) * t_count + t) * 2 + side][...]


def hidden_kernel(ids_ref, normed_a, normed_b, up, bias_up, act_a, act_b, slope_a, slope_b):
    step = min(512, normed_a.shape[0])
    for normed, act, slope in ((normed_a, act_a, slope_a), (normed_b, act_b, slope_b)):

        def chunk(i, carry, normed=normed, act=act, slope=slope):
            rows = at(i * step, step)
            u = mm(normed[rows, :], up[...], NN) + bias_up[...]
            square = u * u
            th = jnp.tanh(0.7978845608028654 * (u + 0.044715 * square * u))
            act[rows, :] = (0.5 * u * (1.0 + th)).astype(BF16)
            slope[rows, :] = 0.5 * (1.0 + th) + 0.5 * u * (1.0 - th * th) * (
                0.7978845608028654 * (1.0 + 3.0 * 0.044715 * square)
            )
            return carry

        lax.fori_loop(0, normed.shape[0] // step, chunk, 0, unroll=True)


def hidden_back_kernel(side, ids_ref, slope, cot, down, up, d_up, d_norm, grad_bias):
    half = slope.shape[0]
    step = min(512, half)

    def chunk(i, total):
        rows = at(i * step, step)
        d_act = mm(cot[at(side * half + i * step, step), :], down[...], NN)
        g = (d_act * slope[rows, :]).astype(BF16)
        d_up[rows, :] = g
        d_norm[rows, :] = mm(g, up[...], NT).astype(BF16)
        return total + jnp.sum(g.astype(F32), axis=0, keepdims=True)

    grad_bias[...] = lax.fori_loop(0, half // step, chunk, jnp.zeros(grad_bias.shape, F32), unroll=True)


def down_kernel(ids_ref, act_a, act_b, down, keep, give):
    step = min(512, act_a.shape[0])
    for act, out in ((act_b, give), (act_a, keep)):

        def chunk(i, carry, act=act, out=out):
            rows = at(i * step, step)
            out[rows, :] = mm(act[rows, :], down[...], NT).astype(BF16)
            return carry

        lax.fori_loop(0, act.shape[0] // step, chunk, 0, unroll=True)


def join_kernel(ids_ref, keep, landed, *pieces):
    own = pieces[0].shape[0]
    for k, piece in enumerate(pieces):
        rows = slice(k * own, (k + 1) * own)
        piece[...] = (keep[rows, :].astype(F32) + landed[rows, :].astype(F32)).astype(BF16)


def down_grad_kernel(ids_ref, cot, act_a, act_b, *outs):
    half = act_a.shape[0]
    part = outs[0].shape[0]
    for r in range(len(outs) - 1, -1, -1):
        cols = at((ids_ref[0] ^ r) * part, part)
        total = mm(cot[:half, cols], act_a[...], TN) + mm(cot[half:, cols], act_b[...], TN)
        outs[r][...] = total.astype(BF16)


def up_grad_kernel(ids_ref, normed_a, normed_b, d_up_a, d_up_b, near_down, *outs):
    part = outs[0].shape[0]
    for r in range(len(outs) - 1, -1, -1):
        cols = at((ids_ref[0] ^ r) * part, part)
        total = mm(normed_a[:, cols], d_up_a[...], TN) + mm(normed_b[:, cols], d_up_b[...], TN)
        outs[r][:part, :] = total.astype(BF16)
    outs[1][part:, :] = near_down[...]


def join_far_kernel(chips, ids_ref, keep, landed, near, far):
    own = keep.shape[0] // chips
    for k in range(chips):
        rows, to = slice(k * own, (k + 1) * own), slice(k // 2 * own, (k // 2 + 1) * own)
        total = keep[rows, :].astype(F32) + landed[rows, :].astype(F32)
        (far if k % 2 else near)[to, :] = total.astype(BF16)


def fold_kernel(ids_ref, near, landed, *pieces):
    own = pieces[0].shape[0]
    for k, piece in enumerate(pieces):
        rows = slice(k * own, (k + 1) * own)
        piece[...] = (near[rows, :].astype(F32) + landed[rows, :].astype(F32)).astype(BF16)


def add_kernel(ids_ref, a, b, out):
    out[...] = (a[...].astype(F32) + b[...].astype(F32)).astype(BF16)


def mlp_sums_kernel(ups, ids_ref, near, *refs):
    out = refs[-1]
    part = out.shape[0] // 2
    for base, terms in ((0, refs[:ups]), (part, refs[ups:-1])):
        total = near[base : base + part, :].astype(F32)
        for term in terms:
            total += term[...].astype(F32)
        out[base : base + part, :] = total.astype(BF16)


def sum_kernel(ids_ref, *refs):
    total = refs[0][...].astype(F32)
    for ref in refs[1:-1]:
        total += ref[...].astype(F32)
    refs[-1][...] = total.astype(BF16)


def second_back_kernel(cfg, ids_ref, *refs):
    chips = cfg
    landed, refs = refs[:chips], refs[chips:]
    residual, cot, vecs, w_mine, w_other, d_res, branch, grads = refs[:8]
    d_mix = refs[8:]
    own, width = residual.shape
    feats = w_mine.shape[1]
    d_norm = landed[0][...].astype(F32)
    for ref in landed[1:]:
        d_norm += ref[...].astype(F32)
    vhat, scale = normalise(residual[...])
    c = cot[...].astype(F32)
    d_residual = c + norm_grad(vhat, scale, vecs[3:4, :] * d_norm)
    d_res[...] = d_residual
    b = d_residual.astype(BF16)
    branch[...] = b
    for k, piece in enumerate(d_mix):
        rows = slice(k * width, (k + 1) * width)
        piece[:, :feats] = mm(b, w_mine[rows, :], NN).astype(BF16)
        piece[:, feats:] = mm(b, w_other[rows, :], NN).astype(BF16)
    grads[0:1, :] = jnp.sum(d_residual, axis=0, keepdims=True)
    grads[1:2, :] = jnp.sum(vhat * d_norm, axis=0, keepdims=True)
    grads[2:3, :] = jnp.sum(d_norm, axis=0, keepdims=True)
    grads[3:4, :] = jnp.sum(c, axis=0, keepdims=True)


def attend_back_kernel(cfg, ids_ref, qkv, seg_row, seg_col, *refs):
    chip_masks, t_count = cfg
    me = Ids(ids_ref, t_count)
    mixes, refs = refs[: len(chip_masks)], refs[len(chip_masks) :]
    landed, d_qkv, sums, k_heads, v_heads, q_heads, m_heads, dk, dv, mask = refs
    length, feats = qkv.shape[0], dk.shape[1]
    own = mixes[0].shape[0]
    heads = feats // HD
    tile = min(256, length)
    scale = HD ** (-0.5)
    for h in range(heads):
        lanes = head_mask(feats, h)
        for k, m in enumerate(chip_masks):
            piece = mixes[k][:, :feats]
            m_heads[h, me.rows(0, m, own), :] = jnp.where(lanes, piece, jnp.zeros_like(piece))
            piece = landed[k * own : (k + 1) * own, :]
            m_heads[h, me.rows(1, m, own), :] = jnp.where(lanes, piece, jnp.zeros_like(piece))

    def prepare(i, carry):
        rows = at(i * tile, tile)
        for h in range(heads):
            lanes = head_mask(feats, h)
            for k, ref in ((0, q_heads), (1, k_heads), (2, v_heads)):
                piece = qkv[rows, k * feats : (k + 1) * feats]
                if k == 0:
                    piece = piece * BF16(scale)
                ref[h, rows, :] = jnp.where(lanes, piece, jnp.zeros_like(piece))
        dk[rows, :] = jnp.zeros((tile, feats), F32)
        dv[rows, :] = jnp.zeros((tile, feats), F32)
        return carry

    lax.fori_loop(0, length // tile, prepare, 0)
    back = -(-DOC_MOST // tile)
    for i in range(length // tile):
        first = max(0, i - back) * tile
        keys = (i + 1) * tile - first
        rows = slice(i * tile, (i + 1) * tile)
        span = slice(first, first + keys)
        same = seg_col[span, 0:1] == seg_row[:, rows]
        k_pos = first + lax.broadcasted_iota(jnp.int32, (keys, tile), 0)
        q_pos = i * tile + lax.broadcasted_iota(jnp.int32, (keys, tile), 1)
        mask[:keys, :] = jnp.where(same & (k_pos <= q_pos), 0.0, NEGATIVE)
        dq = jnp.zeros((tile, feats), F32)
        dvs = jnp.zeros((keys, feats), F32)
        dks = jnp.zeros((keys, feats), F32)
        for h in range(heads):
            k, v, q, m = k_heads[h, span, :], v_heads[h, span, :], q_heads[h, rows, :], m_heads[h, rows, :]
            s = mm(k, q, NT) + mask[:keys, :]
            e = jnp.exp(s - jnp.max(s, axis=0, keepdims=True))
            p = e * (1.0 / jnp.sum(e, axis=0, keepdims=True))
            dp = mm(v, m, NT)
            row_dot = jnp.sum(p * dp, axis=0, keepdims=True)
            ds = (p * (dp - row_dot)).astype(BF16)
            dvs += mm(p.astype(BF16), m, NN)
            dks += mm(ds, q, NN)
            dq += mm(ds, k, TN)
        dv[span, :] += dvs
        dk[span, :] += dks
        d_qkv[rows, :feats] = (dq * scale).astype(BF16)

    def finish(i, carry):
        rows = at(i * tile, tile)
        d_qkv[rows, feats : 2 * feats] = dk[rows, :].astype(BF16)
        d_qkv[rows, 2 * feats :] = dv[rows, :].astype(BF16)
        return carry + jnp.sum(d_qkv[rows, :].astype(F32), axis=0, keepdims=True)

    sums[...] = lax.fori_loop(0, length // tile, finish, jnp.zeros((1, 3 * feats), F32))


def first_back_kernel(cfg, ids_ref, d_qkv, weight, vhat, keep, give, grads):
    chip_masks, own, t_count = cfg
    me = Ids(ids_ref, t_count)
    span = own * t_count
    gain = jnp.zeros((1, vhat.shape[1]), F32)
    bias = gain
    for out, side in ((give, 1), (keep, 0)):
        for k, mask in enumerate(chip_masks[::t_count]):
            c = (me.y ^ (mask // t_count)) * 2 + (me.core ^ side)
            rows = at(c * span, span)
            d = mm(d_qkv[rows, :], weight[...], NT)
            for t in range(t_count):
                to = at(k * span + (t ^ me.t) * own, own)
                out[to, :] = d[t * own : (t + 1) * own, :].astype(BF16)
            gain += jnp.sum(vhat[rows, :] * d, axis=0, keepdims=True)
            bias += jnp.sum(d, axis=0, keepdims=True)
    grads[0:1, :] = gain
    grads[1:2, :] = bias


def attn_grad_kernel(cfg, ids_ref, normed, d_qkv, attn, branch_a, branch_b, small, small_other, *refs):
    chip_masks, t_count, z_count, vec = cfg
    me = Ids(ids_ref, t_count)
    outs, branch = refs[:-1], refs[-1]
    own = branch_a.shape[0] // len(chip_masks)
    for side, ref in ((0, branch_a), (1, branch_b)):
        for k, mask in enumerate(chip_masks):
            branch[me.rows(side, mask, own), :] = ref[k * own : (k + 1) * own, :]
    count = small.shape[0] // z_count
    feats = attn.shape[1]
    part = normed.shape[1] // z_count
    row = lax.broadcasted_iota(jnp.int32, (count, feats), 0)
    for r in range(z_count - 1, -1, -1):
        out = outs[r]
        cols = at((me.z ^ r) * part, part)
        g = mm(normed[:, cols], d_qkv[...], TN)
        for k in range(3):
            out[k * part : (k + 1) * part, :] = g[:, k * feats : (k + 1) * feats].astype(BF16)
        out[3 * part : 4 * part, :] = mm(branch[:, cols], attn[...], TN).astype(BF16)
        mine = small[r * count : (r + 1) * count, :].astype(F32)
        both = mine + small_other[r * count : (r + 1) * count, :].astype(F32)
        out[4 * part :, :] = jnp.where(row < vec, both, mine).astype(BF16)


def last_kernel(t_count, ids_ref, *refs):
    me = Ids(ids_ref, t_count)
    x, vecs, d_res, out = refs[-4:]
    own = out.shape[0]
    d_norm = refs[0][...].astype(F32)
    for ref in refs[1:-4]:
        d_norm += ref[...].astype(F32)
    vhat, scale = normalise(x[at(me.t * own, own), :].astype(F32))
    out[...] = (d_res[...] + norm_grad(vhat, scale, vecs[0:1, :] * d_norm)).astype(BF16)


def output_kernel(ids_ref, *refs):
    residual, vecs, out = refs[-3:]
    total = residual[...] + vecs[5:6, :]
    for ref in refs[:-3]:
        total += ref[...].astype(F32)
    out[...] = total.astype(BF16)


def pair_kernel(ids_ref, mine, other, out):
    own = mine.shape[0]
    out[at(ids_ref[3] * own, own), :] = mine[...]
    out[at((1 - ids_ref[3]) * own, own), :] = other[...]


def small_grad_kernel(cfg, ids_ref, one, two, sums, bup_a, bup_b, out):
    z_count, heads, rows_up, cols_up = cfg
    width = one.shape[1]
    part = width // z_count
    feats = sums.shape[1] // 3
    units = bup_a.shape[1]
    each = HD // z_count
    wide = out.shape[1]
    vec, q, q_rows, u, u_rows, total = small_rows(part, heads, z_count, rows_up, cols_up, wide)
    per = part // wide
    bqv = (sums[:, :feats].astype(BF16), sums[:, 2 * feats :].astype(BF16))
    bup = (bup_a[...] + bup_b[...]).astype(BF16)
    out[...] = jnp.zeros(out.shape, out.dtype)
    for r in range(z_count):
        z = ids_ref[0] ^ r
        base = r * total
        for i in range(6):
            ref, row = (one, i) if i < 2 else (two, i - 2)
            for j in range(per):
                k = base + i * per + j
                if wide % 128 == 0:
                    out[k : k + 1, :] = ref[row : row + 1, at(z * part + j * wide, wide)].astype(BF16)
                else:
                    lane = lax.broadcasted_iota(jnp.int32, (wide, width), 0)
                    goal = lax.broadcasted_iota(jnp.int32, (wide, width), 1)
                    move = jnp.where(goal == z * part + j * wide + lane, 1.0, 0.0).astype(BF16)
                    out[k : k + 1, :] = mm(ref[row : row + 1, :].astype(BF16), move, NT).astype(BF16)
        lane = lax.broadcasted_iota(jnp.int32, (wide, feats), 0)
        goal = lax.broadcasted_iota(jnp.int32, (wide, feats), 1)
        for i in range(q_rows):
            line = jnp.zeros((1, wide), F32)
            for k in range(2):
                place = lane + i * wide - k * heads * each
                move = (place >= 0) & (place < heads * each)
                move &= goal == (place // each) * HD + z * each + place % each
                line += mm(bqv[k], jnp.where(move, 1.0, 0.0).astype(BF16), NT)
            out[base + vec + i : base + vec + i + 1, :] = line.astype(BF16)
        lane = lax.broadcasted_iota(jnp.int32, (wide, units), 0)
        goal = lax.broadcasted_iota(jnp.int32, (wide, units), 1)
        for i in range(u_rows):
            place = lane + i * wide
            move = (place < u) & (goal == (place // cols_up) * 128 + z * cols_up + place % cols_up)
            row = base + vec + q_rows + i
            out[row : row + 1, :] = mm(bup, jnp.where(move, 1.0, 0.0).astype(BF16), NT).astype(BF16)


def mlp_place_kernel(c_masks, ids_ref, *refs):
    blocks, (up, down) = refs[:-2], refs[-2:]
    c = ids_ref[1] * 2 + ids_ref[2]
    units = blocks[0].shape[1]
    part = blocks[0].shape[0] // 2
    for r, mask in enumerate(c_masks):
        where = at((c ^ mask) * units, units)
        up[:, where] = blocks[r][:part, :].astype(F32)
        down[where, :] = blocks[r][part:, :].astype(F32).T


def attn_place_kernel(cfg, ids_ref, *refs):
    c_masks, heads, rows_up, vec, q_rows = cfg
    blocks = refs[: len(c_masks)]
    qkv, out, *vecs, b_qv, b_up = refs[len(c_masks) :]
    c = ids_ref[1] * 2 + ids_ref[2]
    wide = blocks[0].shape[1]
    part = vecs[0].shape[0]
    each, cols_up = b_qv.shape[2], b_up.shape[1]
    aligned = wide % 128 == 0
    for r, mask in enumerate(c_masks):
        where = at((c ^ mask) * wide, wide)
        if aligned:
            for k in range(3):
                qkv[k, :, where] = blocks[r][k * part : (k + 1) * part, :].astype(F32)
        else:
            for k in range(3):
                qkv[c ^ mask, k] = blocks[r][k * part : (k + 1) * part, :].astype(F32)
        out[where, :] = blocks[r][3 * part : 4 * part, :].astype(F32).T
        base = 4 * part + vec
        for k in range(2):
            for h in range(heads):
                flat = (k * heads + h) * each
                row, lane = base + flat // wide, flat % wide
                b_qv[k, pl.ds((c ^ mask) * heads + h, 1), :] = blocks[r][
                    row : row + 1, lane : lane + each
                ].astype(F32)
        for i in range(rows_up):
            row, lane = base + q_rows + (i * cols_up) // wide, (i * cols_up) % wide
            b_up[pl.ds((c ^ mask) * rows_up + i, 1), :] = blocks[r][
                row : row + 1, lane : lane + cols_up
            ].astype(F32)
    total = blocks[0][4 * part : 4 * part + vec, :].astype(F32)
    for block in blocks[1:]:
        total += block[4 * part : 4 * part + vec, :].astype(F32)
    per = part // wide
    for i, ref in enumerate(vecs):
        lines = [total[i * per + j : i * per + j + 1, :] for j in range(per)]
        ref[...] = (jnp.concatenate(lines, axis=1) if per > 1 else lines[0]).reshape(part)


def body(
    tokens,
    segments,
    ln1_gain,
    ln1_bias,
    w_qkv,
    b_qv,
    w_out,
    b_out,
    ln2_gain,
    ln2_bias,
    w_up,
    b_up,
    w_down,
    b_down,
    cotangent,
):
    z_count, t_count, y_count = (lax.axis_size(a) for a in ("fsdp", "tp", "y"))
    z_me, y_me, core, t_me = (lax.axis_index(a) for a in ("fsdp", "y", "core", "tp"))
    ids = jnp.stack([z_me, y_me, core, t_me]).astype(jnp.int32)
    c_me = y_me * 2 + core
    c_count = size_of(CTX)
    c_masks, chip_masks = masks_of(CTX), masks_of(CHIPS)
    chips = len(chip_masks)
    x_span, cot_span = tokens[0], cotangent[0]
    span, width = x_span.shape
    length = span * c_count
    half = length // 2
    own = span // t_count
    feats = w_qkv.shape[2] // c_count
    heads = feats // HD
    units = w_up.shape[1] // c_count
    part = width // z_count
    tile = min(256, length)
    keys = min(length, (-(-DOC_MOST // tile) + 1) * tile)
    rows_up, cols_up = b_up.shape[0] // c_count, b_up.shape[1]
    vec, _, q_rows, _, _, small_count = small_rows(part, heads, z_count, rows_up, cols_up, feats)
    Z, TP = ("fsdp",), ("tp",)
    turned = jnp.swapaxes(w_qkv, 0, 1)
    raw = [ln1_gain, ln1_bias, b_out, ln2_gain, ln2_bias, b_down, b_qv, b_up]
    pack_cfg = (z_count, heads, rows_up, cols_up)
    z_all, c_all = range(z_count), range(c_count)
    known, order, cost = {}, {}, {}

    def node(make):
        def value(*index):
            if (value, index) not in known:
                known[value, index] = make(*index)
            return known[value, index]

        value.title = make.__name__
        return value

    def waits(*key):
        return order[key]() if key in order else []

    def move(key, value, axes, bits):
        pins = waits(*key)
        return swap(after(value, *pins) if pins else value, axes, bits)

    def run(key, kernel, outs, arrays, index=(), **more):
        deps = waits(key, *index)
        declared = cost.get(key, 0.1)
        return kernel_call(kernel, outs, ids, arrays, deps=deps, cost=declared, name=key.title, **more)

    def gathered(key, source, axes, r):
        low = r & -r
        return move((key, r), key(r ^ low), axes, low) if r else source

    def from_chip(key, source, k):
        return move((key, k), source, CHIPS, chip_masks[k]) if k else source

    @node
    def pack():
        out = [shape((4 * part + small_count, feats))]
        if feats % 128:
            cuts = [
                lax.dynamic_slice_in_dim(turned, c_me * feats, feats, 2),
                lax.dynamic_slice_in_dim(w_out, c_me * feats, feats, 0),
            ]
            return run(pack, partial(pack_plain_kernel, pack_cfg), out, [*cuts, *raw])
        scratch = [pltpu.VMEM((feats, part), BF16), *[pltpu.VMEM(v.shape, BF16) for v in raw]]
        return run(
            pack,
            partial(pack_kernel, pack_cfg),
            out,
            [],
            anys=[turned, w_out, *raw],
            scratch=[*scratch, pltpu.SemaphoreType.DMA((12,))],
        )

    @node
    def rows():
        return run(
            rows,
            pack_rows_kernel,
            [shape((own, width)), shape((own, width)), shape((span, width))],
            [],
            anys=[cot_span],
            scratch=[pltpu.SemaphoreType.DMA((4,))],
        )

    @node
    def norm():
        return run(
            norm,
            partial(first_norm_kernel, (c_masks, t_count)),
            [shape((length, width), F32), shape((1, length), F32), shape((length, 128), F32)],
            [x(r) for r in c_all] + [seg(r) for r in c_all],
        )

    @node
    def cut():
        return run(
            cut,
            cut_mlp_kernel,
            [shape((part, units))] * 2,
            [],
            anys=[w_up, w_down],
            scratch=[pltpu.VMEM((units, part), BF16), pltpu.SemaphoreType.DMA((2,))],
        )

    @node
    def unpack():
        return run(
            unpack,
            partial(unpack_kernel, pack_cfg),
            [
                shape((width, 3 * feats)),
                shape((width, feats)),
                shape((8, width), F32),
                shape((2, feats), F32),
                shape((1, units), F32),
            ],
            [attn(r) for r in z_all],
        )

    @node
    def attend():
        vhat, seg_row, seg_col = norm()
        qkv_full, _, vecs, bias_qv, _ = unpack()
        return run(
            attend,
            partial(attend_kernel, (chip_masks, t_count)),
            [
                shape((length, width)),
                shape((length, 3 * feats)),
                shape((length, feats)),
                shape((half, feats)),
                shape((half, feats)),
            ],
            [vhat, qkv_full, vecs, bias_qv, seg_row, seg_col],
            scratch=[pltpu.VMEM((heads, length, feats), BF16)] * 2 + [pltpu.VMEM((tile, keys), F32)],
        )

    def cat(key, blocks):
        size, cols = blocks[0].shape
        return run(key, cat_kernel, [shape((size * len(blocks), cols))], blocks)

    @node
    def wcat():
        return cat(wcat, [wout(k) for k in range(chips)])

    @node
    def beside():
        pieces = [shape((own, 2 * feats))] * chips
        return run(beside, beside_kernel, pieces, [attend()[3], give_mix()])

    @node
    def out_norm():
        return run(
            out_norm,
            partial(out_norm_kernel, t_count),
            [shape((own, width), F32), shape((own, width))],
            [*[mixed(k) for k in range(chips)], wcat()[0], w_other(), x_span, unpack()[2]],
        )

    @node
    def ncat():
        return cat(ncat, [normed(k) for k in range(chips)])

    @node
    def cots():
        pieces = []
        for y in range(1, y_count):
            pieces += [cot_a(y), cot_a_core(y), cot_b(y), cot_b_core(y)]
        return run(
            cots,
            partial(cot_kernel, chip_masks, t_count),
            [shape((length, width))],
            [rows()[2], cot_core(), *pieces],
        )

    @node
    def up_full():
        return run(up_full, place_kernel, [shape((width, units))], [up(r) for r in z_all])

    @node
    def down_full():
        return run(down_full, place_kernel, [shape((width, units))], [down_w(r) for r in z_all])

    @node
    def hidden():
        return run(
            hidden,
            hidden_kernel,
            [shape((half, units))] * 2 + [shape((half, units), F32)] * 2,
            [ncat()[0], normed_b(), up_full()[0], unpack()[4]],
        )

    def back(key, side):
        return run(
            key,
            partial(hidden_back_kernel, side),
            [shape((half, units)), shape((half, width)), shape((1, units), F32)],
            [hidden()[2 + side], cots()[0], down_full()[0], up_full()[0]],
        )

    def join(key, keep, give):
        return run(key, join_kernel, [shape((own, width))] * chips, [keep, give])

    def join_far(key, keep, give):
        outs = [shape((y_count * own, width))] * 2
        return run(key, partial(join_far_kernel, chips), outs, [keep, give])

    def fold(key, near, landed):
        return run(key, fold_kernel, [shape((own, width))] * y_count, [near, landed])

    @node
    def grad_down():
        return run(
            grad_down,
            down_grad_kernel,
            [shape((part, units))] * z_count,
            [cots()[0], hidden()[0], hidden()[1]],
        )

    @node
    def grad_up():
        return run(
            grad_up,
            up_grad_kernel,
            [shape((part if r != 1 else 2 * part, units)) for r in z_all],
            [ncat()[0], normed_b(), back_a()[0], back_b()[0], grad_down()[1]],
        )

    @node
    def down():
        return run(
            down,
            down_kernel,
            [shape((half, width))] * 2,
            [hidden()[0], hidden()[1], down_full()[0]],
        )

    def z_total(key, arrived, pieces, r):
        value = pieces[r]
        for low in (1, 2, 4):
            if low < (r & -r) and r | low < z_count:
                out = [shape(value.shape)]
                (value,) = run(key, add_kernel, out, [value, arrived(r | low)], index=(r,))
        return value

    def z_ends(arrived):
        return [arrived(r) for r in z_all if r > 1 and r == r & -r]

    @node
    def mlp_sums():
        ups = [grad_up()[0], *z_ends(du_in)]
        downs = [grad_down()[0], *z_ends(dd_in)]
        return run(
            mlp_sums,
            partial(mlp_sums_kernel, len(ups)),
            [shape((2 * part, units))],
            [near(), *ups, *downs],
        )

    @node
    def res_back():
        return run(
            res_back,
            partial(second_back_kernel, chips),
            [shape((own, width), F32), shape((own, width)), shape((4, width), F32)]
            + [shape((own, 2 * feats))] * chips,
            [
                *[two(k) for k in range(chips)],
                out_norm()[0],
                rows()[0],
                unpack()[2],
                wcat()[0],
                w_other(),
            ],
        )

    @node
    def apart():
        return run(apart, apart_kernel, [shape((half, feats))], [d_mix(k) for k in range(chips)])

    @node
    def attend_back():
        return run(
            attend_back,
            partial(attend_back_kernel, (chip_masks, t_count)),
            [shape((length, 3 * feats)), shape((1, 3 * feats), F32)],
            [
                attend()[1],
                norm()[1],
                norm()[2],
                *[d_mix(k) for k in range(chips)],
                d_mix_core(),
            ],
            scratch=[pltpu.VMEM((heads, length, feats), BF16)] * 4
            + [pltpu.VMEM((length, feats), F32)] * 2
            + [pltpu.VMEM((keys, tile), F32)],
        )

    @node
    def bcat():
        return cat(bcat, [branch(k) for k in range(chips)])

    @node
    def norm_back():
        return run(
            norm_back,
            partial(first_back_kernel, (chip_masks, own, t_count)),
            [shape((half, width)), shape((half, width)), shape((2, width), F32)],
            [attend_back()[0], unpack()[0], norm()[0]],
        )

    @node
    def small():
        return run(
            small,
            partial(small_grad_kernel, (z_count, heads, rows_up, cols_up)),
            [shape((z_count * small_count, feats))],
            [norm_back()[2], res_back()[2], attend_back()[1], back_a()[2], back_b()[2]],
        )

    @node
    def grad_attn():
        return run(
            grad_attn,
            partial(attn_grad_kernel, (chip_masks, t_count, z_count, vec)),
            [shape((4 * part + small_count, feats))] * z_count,
            [
                attend()[0],
                attend_back()[0],
                attend()[2],
                bcat()[0],
                branch_b(),
                small()[0],
                small_tp(),
            ],
            scratch=[pltpu.VMEM((length, width), BF16)],
        )

    @node
    def attn_sums():
        terms = [grad_attn()[0], da_in(1), *z_ends(da_in)]
        return run(attn_sums, sum_kernel, [shape(terms[0].shape)], terms)

    @node
    def last():
        return run(
            last,
            partial(last_kernel, t_count),
            [shape((own, width))],
            [fold_one()[0], *[one(y) for y in range(1, y_count)], x_span, unpack()[2], res_back()[0]],
        )

    @node
    def out():
        sums = [fold_down()[0], *[down_in(y) for y in range(1, y_count)]]
        arrays = [*sums, out_norm()[0], unpack()[2]]
        return run(out, output_kernel, [shape((own, width))], arrays)

    def pair(key, mine, other):
        return run(key, pair_kernel, [shape((span, width))], [mine, other])

    @node
    def mlp_place():
        return run(
            mlp_place,
            partial(mlp_place_kernel, c_masks),
            [shape((part, c_count * units), F32), shape((c_count * units, part), F32)],
            [mlp_all(r) for r in c_all],
        )

    @node
    def attn_place():
        return run(
            attn_place,
            partial(attn_place_kernel, (c_masks, heads, rows_up, vec, q_rows)),
            [
                shape((3, part, c_count * feats) if feats % 128 == 0 else (c_count, 3, part, feats), F32),
                shape((c_count * feats, part), F32),
                *[shape((part,), F32)] * 6,
                shape(b_qv.shape, F32),
                shape(b_up.shape, F32),
            ],
            [attn_all(r) for r in c_all],
        )

    @node
    def back_a():
        return back(back_a, 0)

    @node
    def back_b():
        return back(back_b, 1)

    @node
    def join_two():
        return join(join_two, back_a()[1], give_two())

    @node
    def join_down():
        return join_far(join_down, down()[0], give_down())

    @node
    def fold_down():
        return fold(fold_down, join_down()[0], down_x())

    @node
    def join_one():
        return join_far(join_one, norm_back()[0], give_one())

    @node
    def fold_one():
        return fold(fold_one, join_one()[0], one_x())

    @node
    def pair_out():
        return pair(pair_out, out()[0], out_tp())

    @node
    def pair_tok():
        return pair(pair_tok, last()[0], last_tp())

    @node
    def dd_sum(r):
        return z_total(dd_sum, dd_in, grad_down(), r)

    @node
    def du_sum(r):
        return z_total(du_sum, du_in, grad_up(), r)

    @node
    def da_sum(r):
        return z_total(da_sum, da_in, grad_attn(), r)

    attn = node(lambda r: gathered(attn, pack()[0], Z, r))
    x = node(lambda r: gathered(x, x_span, CTX, r))
    seg = node(lambda r: gathered(seg, segments, CTX, r))
    up = node(lambda r: gathered(up, cut()[0], Z, r))
    down_w = node(lambda r: gathered(down_w, cut()[1], Z, r))
    cot_core = node(lambda: move((cot_core,), rows()[2], CTX, 1))
    cot_a = node(lambda y: move((cot_a, y), rows()[0], CTX, 2 * y))
    cot_b = node(lambda y: move((cot_b, y), rows()[1], CTX, 2 * y))
    cot_a_core = node(lambda y: move((cot_a_core, y), cot_a(y), CTX, 1))
    cot_b_core = node(lambda y: move((cot_b_core, y), cot_b(y), CTX, 1))
    wout = node(lambda k: from_chip(wout, unpack()[1], k))
    w_other = node(lambda: move((w_other,), wcat()[0], CTX, 1))
    give_mix = node(lambda: move((give_mix,), attend()[4], CTX, 1))
    mixed = node(lambda k: from_chip(mixed, beside()[k], k))
    normed = node(lambda k: from_chip(normed, out_norm()[1], k))
    normed_b = node(lambda: move((normed_b,), ncat()[0], CTX, 1))
    give_two = node(lambda: move((give_two,), back_b()[1], CTX, 1))
    two = node(lambda k: from_chip(two, join_two()[k], k))
    give_down = node(lambda: move((give_down,), down()[1], CTX, 1))
    down_x = node(lambda: move((down_x,), join_down()[1], TP, 1))
    down_in = node(lambda y: move((down_in, y), fold_down()[y], CTX, 2 * y))
    give_one = node(lambda: move((give_one,), norm_back()[1], CTX, 1))
    one_x = node(lambda: move((one_x,), join_one()[1], TP, 1))
    one = node(lambda y: move((one, y), fold_one()[y], CTX, 2 * y))
    d_mix = node(lambda k: from_chip(d_mix, res_back()[3 + k], k))
    d_mix_core = node(lambda: move((d_mix_core,), apart()[0], CTX, 1))
    branch = node(lambda k: from_chip(branch, res_back()[1], k))
    branch_b = node(lambda: move((branch_b,), bcat()[0], CTX, 1))
    small_tp = node(lambda: move((small_tp,), small()[0], TP, 1))
    near = node(lambda: move((near,), grad_up()[1], Z, 1))
    dd_in = node(lambda r: move((dd_in, r), dd_sum(r), Z, r & -r))
    du_in = node(lambda r: move((du_in, r), du_sum(r), Z, r & -r))
    da_in = node(lambda r: move((da_in, r), da_sum(r), Z, r & -r))
    out_tp = node(lambda: move((out_tp,), out()[0], TP, 1))
    last_tp = node(lambda: move((last_tp,), last()[0], TP, 1))
    mlp_all = node(lambda r: gathered(mlp_all, mlp_sums()[0], CTX, r))
    attn_all = node(lambda r: gathered(attn_all, attn_sums()[0], CTX, r))

    order |= {
        (x, 3): lambda: [attn(1), attn(2), seg(1)],
        (cut,): lambda: [norm()[1]],
        (unpack,): lambda: [norm()[1], cut()[0], cot_a(1)],
        (attend,): lambda: [attn(3)],
        (wcat,): lambda: [up(1)],
        (out_norm,): lambda: [up(3)],
        (ncat,): lambda: [down_w(1), down_w(2)],
        (cots,): lambda: [ncat()[0]],
        (up_full,): lambda: [cots()[0]],
        (down_full,): lambda: [hidden()[0], normed(3)],
        (grad_up,): lambda: [join_two()[0], dd_in(3)],
        (dd_sum, 2): lambda: [down()[0]],
        (branch, 2): lambda: [du_sum(2)],
        (branch, 3): lambda: [apart()[0], du_sum(2)],
        (attend_back,): lambda: [dd_in(2), d_mix(3)],
        (join_one,): lambda: [grad_attn()[0], mlp_all(1), branch(3)],
        (mlp_all, 3): lambda: [mlp_all(1), small_tp()],
        (da_sum, 2): lambda: [join_one()[0], small()[0]],
        (last,): lambda: [da_sum(2), mlp_all(1)],
        (small,): lambda: [branch(2)],
        (normed_b,): lambda: [mixed(2)],
        (two, 3): lambda: [normed_b()],
        (two, 2): lambda: [normed(2)],
        (mixed, 2): lambda: [w_other()],
        (cot_a_core, 1): lambda: [wout(3)],
        (rows,): lambda: [pack()[0]],
        (dd_in, 2): lambda: [grad_up()[0]],
        (branch_b,): lambda: [d_mix_core(), mlp_sums()[0]],
        (cot_a, 1): lambda: [cot_core()],
        (norm_back,): lambda: [branch(2)],
        (mlp_all, 1): lambda: [branch(2)],
        (down_w, 3): lambda: [normed(3)],
        (grad_attn,): lambda: [give_one()],
        (attn_place,): lambda: [attn_sums()[0]],
        (mixed, 3): lambda: [up(2)],
        (du_in, 2): lambda: [res_back()[0]],
        (one_x,): lambda: [join_one()[0]],
        (cot_core,): lambda: [seg(3)],
        (da_in, 2): lambda: [small_tp()],
        (attn_sums,): lambda: [give_one()],
        (down_w, 1): lambda: [mixed(3)],
        (back_a,): lambda: [back_b()[0], normed_b()],
    }
    cost |= {
        pack: 8,
        rows: 0.01,
        norm: 8,
        cut: 1,
        unpack: 1,
        attend: 8,
        out_norm: 1,
        cots: 4,
        up_full: 2,
        down_full: 8,
        hidden: 0.3,
        back_b: 2,
        grad_up: 1.5,
        down: 1,
        res_back: 0.3,
        small: 8,
        grad_attn: 4,
        last: 1,
        out: 1,
        pair_out: 1,
        pair_tok: 16,
        mlp_place: 1,
        apart: 2,
        beside: 8,
        ncat: 16,
        attn_sums: 4,
        da_sum: 0.01,
        bcat: 1,
        dd_sum: 0.01,
        norm_back: 1,
        join_one: 1,
        du_sum: 8,
    }
    full_qkv, full_out, *vec_sum, full_bqv, full_bup = attn_place()
    if feats % 128:
        full_qkv = full_qkv.transpose(1, 2, 0, 3).reshape(3, part, c_count * feats)
    full_up, full_down = mlp_place()
    return (
        pair_out()[0][None],
        pair_tok()[0][None],
        vec_sum[0],
        vec_sum[1],
        jnp.swapaxes(full_qkv, 0, 1),
        full_bqv,
        full_out,
        vec_sum[2],
        vec_sum[3],
        vec_sum[4],
        full_up,
        full_bup,
        full_down,
        vec_sum[5],
    )


def solution(mesh):
    fsdp, ctx, tp = (mesh.shape[a] for a in ("fsdp", "ctx", "tp"))
    split = Mesh(mesh.devices.reshape(fsdp, ctx // 2, 2, tp), ("fsdp", "y", "core", "tp"))
    rows = P("fsdp", CTX, None)
    shares = (
        P("fsdp"),
        P("fsdp"),
        P("fsdp", None, "tp"),
        P(None, "tp", "fsdp"),
        P("tp", "fsdp"),
        P("fsdp"),
        P("fsdp"),
        P("fsdp"),
        P("fsdp", "tp"),
        P("tp", "fsdp"),
        P("tp", "fsdp"),
        P("fsdp"),
    )
    return jax.shard_map(
        body,
        mesh=split,
        in_specs=(rows, P("fsdp", CTX), *shares, rows),
        out_specs=(rows, rows, *shares),
        check_vma=False,
    )
```

```python
from functools import partial

import jax
import jax.numpy as jnp
import numpy as np
from jax import lax
from jax.experimental import pallas as pl
from jax.experimental.pallas import tpu as pltpu
from jax.sharding import Mesh
from jax.sharding import PartitionSpec as P

HD = 64
DOC_MOST = 512
EPSILON = 1e-05
NEGATIVE = -1e30
F32 = jnp.float32
FLOPS_PER_US = 2e9
BF16 = jnp.bfloat16

CTX = ("y", "core")
CHIPS = ("y", "tp")


def size_of(axes):
    return int(np.prod([lax.axis_size(a) for a in axes]))


def swap(value, axes, bits):
    count = size_of(axes)
    return lax.ppermute(value, axes, [(i, i ^ bits) for i in range(count)])


def masks_of(axes):
    bits, at = [], 1
    for a in reversed(axes):
        mine = []
        while len(mine) < (lax.axis_size(a) - 1).bit_length():
            mine.append(at)
            at *= 2
        bits = mine + bits if a == "core" else bits + mine
    masks = [0]
    for r in range(1, size_of(axes)):
        low = r & -r
        masks.append(masks[r ^ low] | bits[low.bit_length() - 1])
    return masks


def after(value, *others):
    return lax.optimization_barrier((value, *others))[0]


class Place:
    def __getitem__(self, axis):
        return lax.axis_index(("fsdp", "y", "core", "tp")[axis])


def kernel_call(kernel, outs, arrays, scratch=(), cost=1.0, name=None, vmem=12, deps=(), anys=()):
    deps = list(deps)
    extra = len(deps)

    def run(*refs):
        kernel(Place(), *refs[extra:])

    def place(space):
        return pl.BlockSpec(memory_space=space)

    return pl.pallas_call(
        run,
        out_shape=[jax.ShapeDtypeStruct(s.shape, s.dtype) for s in outs],
        in_specs=[place(pl.ANY)] * extra
        + [place(pltpu.HBM)] * len(anys)
        + [place(pltpu.VMEM)] * len(arrays),
        out_specs=[place(pltpu.VMEM)] * len(outs),
        scratch_shapes=list(scratch),
        compiler_params=pltpu.CompilerParams(vmem_limit_bytes=vmem << 20),
        cost_estimate=pl.CostEstimate(
            flops=int(cost * FLOPS_PER_US), bytes_accessed=int(cost * 1e5), transcendentals=0
        ),
        name=name,
    )(*deps, *[pltpu.with_memory_space_constraint(a, pltpu.HBM) for a in anys], *arrays)


def shape(dims, dtype=BF16):
    return jax.ShapeDtypeStruct(tuple(dims), dtype)


NN = (((1,), (0,)), ((), ()))
NT = (((1,), (1,)), ((), ()))
TN = (((0,), (0,)), ((), ()))


def mm(a, b, dims):
    return lax.dot_general(a, b, dims, preferred_element_type=F32)


def at(start, size, unit=None):
    return pl.ds(pl.multiple_of(start, unit or size), size)


def normalise(values):
    centred = values - jnp.mean(values, axis=-1, keepdims=True)
    variance = jnp.mean(centred * centred, axis=-1, keepdims=True)
    scale = lax.rsqrt(variance + EPSILON)
    return centred * scale, scale


def norm_grad(vhat, scale, weighted):
    return scale * (
        weighted
        - jnp.mean(weighted, axis=-1, keepdims=True)
        - vhat * jnp.mean(weighted * vhat, axis=-1, keepdims=True)
    )


class Ids:
    def __init__(self, ref, t_count):
        self.z, self.y, self.core, self.t = ref[0], ref[1], ref[2], ref[3]
        self.c = self.y * 2 + self.core
        self.p = self.c * t_count + self.t
        self.t_count = t_count

    def rows(self, side, mask, own):
        c = (self.y ^ (mask // self.t_count)) * 2 + (self.core ^ side)
        return at((c * self.t_count + (self.t ^ (mask % self.t_count))) * own, own)


def small_rows(part, heads, z_count, rows_up, cols_up, wide):
    vec = 6 * part // wide
    q = 2 * heads * (HD // z_count)
    u = rows_up * cols_up
    q_rows, u_rows = -(-q // wide), -(-u // wide)
    total = vec + q_rows + u_rows
    return vec, q, q_rows, u, u_rows, -(-total // 16) * 16


def pick(table, index):
    row = lax.broadcasted_iota(jnp.int32, table.shape, 0)
    return jnp.sum(jnp.where(row == index, table.astype(F32), 0.0), axis=0, keepdims=True).astype(BF16)


def lay_rows(out, first, pieces, wide):
    line, used = [], 0
    for piece in [*pieces, None]:
        if piece is None or used + piece.shape[1] > wide:
            if line:
                gap = wide - used
                if gap:
                    line.append(jnp.zeros((1, gap), line[0].dtype))
                out[first : first + 1, :] = jnp.concatenate(line, axis=1) if len(line) > 1 else line[0]
                first, line, used = first + 1, [], 0
        if piece is not None:
            line.append(piece)
            used += piece.shape[1]


def copy_in(pairs, sems):
    copies = [pltpu.make_async_copy(a, b, sems.at[i]) for i, (a, b) in enumerate(pairs)]
    for copy in copies:
        copy.start()
    return copies


def pack_kernel(cfg, ids_ref, w_qkv, w_out, *refs):
    params, out, buf, bufs, sems = refs[:8], refs[8], refs[9], refs[10:18], refs[18]
    c = ids_ref[1] * 2 + ids_ref[2]
    feats = out.shape[1]
    part = w_out.shape[1]
    pairs = [
        (w_qkv.at[k, :, at(c * feats, feats)], out.at[k * part : (k + 1) * part, :]) for k in range(3)
    ]
    pairs.append((w_out.at[at(c * feats, feats), :], buf))
    copies = copy_in(pairs + list(zip(params, bufs)), sems)
    for copy in copies[3:]:
        copy.wait()
    out[3 * part : 4 * part, :] = buf[...].T
    pack_small(cfg, c, bufs[:6], bufs[6], bufs[7], out, 4 * part)
    for copy in copies[:3]:
        copy.wait()


def pack_rows_kernel(ids_ref, cot, mine, other, both, sems):
    t = ids_ref[3]
    own = mine.shape[0]
    near, far = cot.at[at(t * own, own), :], cot.at[at((1 - t) * own, own), :]
    pairs = [(near, mine), (far, other), (near, both.at[:own, :]), (far, both.at[own:, :])]
    for copy in copy_in(pairs, sems):
        copy.wait()


def pack_plain_kernel(cfg, ids_ref, w_qkv, w_out, *refs):
    z_count, heads, rows_up, cols_up = cfg
    vectors, (b_qv, b_up, out) = refs[:6], refs[6:]
    part = w_out.shape[1]
    for k in range(3):
        out[k * part : (k + 1) * part, :] = w_qkv[k]
    out[3 * part : 4 * part, :] = w_out[...].T
    pack_small(cfg, ids_ref[1] * 2 + ids_ref[2], vectors, b_qv, b_up, out, 4 * part)


def pack_small(cfg, c, vectors, b_qv, b_up, out, base):
    z_count, heads, rows_up, cols_up = cfg
    wide = out.shape[1]
    part = vectors[0].shape[-1]
    vec, q, q_rows, u, u_rows, total = small_rows(part, heads, z_count, rows_up, cols_up, wide)
    out[base : base + total, :] = jnp.zeros((total, wide), out.dtype)
    per = part // wide
    for i, ref in enumerate(vectors):
        line = ref[...].reshape(1, part)
        for j in range(per):
            row = base + i * per + j
            out[row : row + 1, :] = line[:, j * wide : (j + 1) * wide]
    q_lines = [pick(b_qv[k], c * heads + h) for k in range(2) for h in range(heads)]
    lay_rows(out, base + vec, q_lines, wide)
    lay_rows(out, base + vec + q_rows, [pick(b_up[...], c * rows_up + i) for i in range(rows_up)], wide)


def first_norm_kernel(cfg, ids_ref, *refs):
    c_masks, t_count = cfg
    me = Ids(ids_ref, t_count)
    count = len(c_masks)
    x, seg, (vhat_out, seg_row, seg_col) = refs[:count], refs[count : 2 * count], refs[2 * count :]
    span = x[0].shape[0]
    for r, mask in enumerate(c_masks):
        seg_row[:, at((me.c ^ mask) * span, span)] = seg[r][...].astype(F32)
    for i in range(seg_row.shape[1] // 128):
        block = jnp.broadcast_to(seg_row[:, i * 128 : (i + 1) * 128], (128, 128))
        seg_col[i * 128 : (i + 1) * 128, :] = block.T
    step = min(64, span)
    for r, mask in enumerate(c_masks):

        def chunk(i, carry, r=r, mask=mask):
            vhat, _ = normalise(x[r][at(i * step, step), :].astype(F32))
            vhat_out[at((me.c ^ mask) * span + i * step, step), :] = vhat
            return carry

        lax.fori_loop(0, span // step, chunk, 0, unroll=True)


def unpack_kernel(cfg, ids_ref, *refs):
    z_count, heads, rows_up, cols_up = cfg
    small, (weight, out_w, vecs, bias_qv, bias_up) = refs[:z_count], refs[z_count:]
    width = weight.shape[0]
    part = width // z_count
    feats = bias_qv.shape[1]
    units = bias_up.shape[1]
    each = HD // z_count
    wide = small[0].shape[1]
    vec, q, q_rows, u, u_rows, total = small_rows(part, heads, z_count, rows_up, cols_up, wide)
    base = 4 * part
    per = part // wide
    qv = [jnp.zeros((1, feats), F32), jnp.zeros((1, feats), F32)]
    ups = jnp.zeros((1, units), F32)
    if wide % 128:
        vecs[...] = jnp.zeros(vecs.shape, F32)
    for r in range(z_count):
        z = ids_ref[0] ^ r
        where = at(z * part, part)
        for k in range(3):
            weight[where, k * feats : (k + 1) * feats] = small[r][k * part : (k + 1) * part, :]
        out_w[where, :] = small[r][3 * part : 4 * part, :]
        for i in range(6):
            for j in range(per):
                row = base + i * per + j
                line = small[r][row : row + 1, :]
                if wide % 128 == 0:
                    vecs[i : i + 1, at(z * part + j * wide, wide)] = line.astype(F32)
                else:
                    lane = lax.broadcasted_iota(jnp.int32, (wide, width), 0)
                    goal = lax.broadcasted_iota(jnp.int32, (wide, width), 1)
                    move = jnp.where(goal == z * part + j * wide + lane, 1.0, 0.0).astype(BF16)
                    vecs[i : i + 1, :] += mm(line, move, NN)
        lane = lax.broadcasted_iota(jnp.int32, (wide, feats), 0)
        goal = lax.broadcasted_iota(jnp.int32, (wide, feats), 1)
        for k in range(2):
            for i in range(q_rows):
                place = lane + i * wide - k * heads * each
                move = (place >= 0) & (place < heads * each)
                move &= goal == (place // each) * HD + z * each + place % each
                row = base + vec + i
                qv[k] += mm(small[r][row : row + 1, :], jnp.where(move, 1.0, 0.0).astype(BF16), NN)
        lane = lax.broadcasted_iota(jnp.int32, (wide, units), 0)
        goal = lax.broadcasted_iota(jnp.int32, (wide, units), 1)
        for i in range(u_rows):
            place = lane + i * wide
            move = (place < u) & (goal == (place // cols_up) * 128 + z * cols_up + place % cols_up)
            row = base + vec + q_rows + i
            ups += mm(small[r][row : row + 1, :], jnp.where(move, 1.0, 0.0).astype(BF16), NN)
    for k in range(2):
        bias_qv[k : k + 1, :] = qv[k]
    bias_up[...] = ups


def head_mask(width, head):
    lane = lax.broadcasted_iota(jnp.int32, (1, width), 1)
    return (lane // HD) == head


def attend_kernel(
    cfg, ids_ref, vhat, weight, vecs, bias_qv, seg_row, seg_col, normed, qkv, attn, keep, give, k_heads, v_heads, mask
):
    chip_masks, t_count = cfg
    me = Ids(ids_ref, t_count)
    length, feats = attn.shape
    heads = feats // HD
    tile = min(256, length)

    def project(i, carry):
        rows = at(i * tile, tile)
        x = (vhat[rows, :] * vecs[0:1, :] + vecs[1:2, :]).astype(BF16)
        normed[rows, :] = x
        out = mm(x, weight[...], NN)
        q = (out[:, :feats] + bias_qv[0:1, :]).astype(BF16)
        k = out[:, feats : 2 * feats].astype(BF16)
        v = (out[:, 2 * feats :] + bias_qv[1:2, :]).astype(BF16)
        qkv[rows, :feats] = q
        qkv[rows, feats : 2 * feats] = k
        qkv[rows, 2 * feats :] = v
        for h in range(heads):
            lanes = head_mask(feats, h)
            k_heads[h, rows, :] = jnp.where(lanes, k, jnp.zeros_like(k))
            v_heads[h, rows, :] = jnp.where(lanes, v, jnp.zeros_like(v))
        return carry

    lax.fori_loop(0, length // tile, project, 0)
    back = -(-DOC_MOST // tile)
    for i in range(length // tile):
        first = max(0, i - back) * tile
        keys = (i + 1) * tile - first
        rows = slice(i * tile, (i + 1) * tile)
        q = qkv[rows, :feats] * BF16(HD ** (-0.5))
        same = seg_col[rows, 0:1] == seg_row[:, first : first + keys]
        q_pos = i * tile + lax.broadcasted_iota(jnp.int32, (tile, keys), 0)
        k_pos = first + lax.broadcasted_iota(jnp.int32, (tile, keys), 1)
        mask[:, :keys] = jnp.where(same & (k_pos <= q_pos), 0.0, NEGATIVE)
        total = jnp.zeros((tile, feats), F32)
        for h in range(heads):
            s = mm(q, k_heads[h, first : first + keys, :], NT) + mask[:, :keys]
            e = jnp.exp(s - jnp.max(s, axis=1, keepdims=True))
            scale = 1.0 / jnp.sum(e, axis=1, keepdims=True)
            total += mm((e * scale).astype(BF16), v_heads[h, first : first + keys, :], NN)
        attn[rows, :] = total.astype(BF16)
    own = keep.shape[0] // len(chip_masks)
    for side, out in ((1, give), (0, keep)):
        for k in range(len(chip_masks)):
            out[k * own : (k + 1) * own, :] = attn[me.rows(side, chip_masks[k], own), :]


def cat_kernel(ids_ref, *refs):
    rows = refs[0].shape[0]
    for k, ref in enumerate(refs[:-1]):
        refs[-1][k * rows : (k + 1) * rows, :] = ref[...]


def beside_kernel(ids_ref, keep, landed, *pieces):
    own, both = pieces[0].shape
    for k, piece in enumerate(pieces):
        rows = slice(k * own, (k + 1) * own)
        piece[:, : both // 2] = keep[rows, :]
        piece[:, both // 2 :] = landed[rows, :]


def apart_kernel(ids_ref, *refs):
    pieces, out = refs[:-1], refs[-1]
    own, feats = pieces[0].shape[0], out.shape[1]
    for k, piece in enumerate(pieces):
        out[k * own : (k + 1) * own, :] = piece[:, feats:]


def out_norm_kernel(t_count, ids_ref, *refs):
    me = Ids(ids_ref, t_count)
    w_mine, w_other, x, vecs, residual, normed = refs[-6:]
    own, width = residual.shape
    feats = w_mine.shape[1]
    total = x[at(me.t * own, own), :].astype(F32) + vecs[2:3, :]
    for k, piece in enumerate(refs[:-6]):
        rows = slice(k * width, (k + 1) * width)
        total += mm(piece[:, :feats], w_mine[rows, :], NT) + mm(piece[:, feats:], w_other[rows, :], NT)
    residual[...] = total
    vhat, _ = normalise(total)
    normed[...] = (vhat * vecs[3:4, :] + vecs[4:5, :]).astype(BF16)


def place_kernel(ids_ref, *refs):
    blocks, out = refs[:-1], refs[-1]
    part = blocks[0].shape[0]
    for r, block in enumerate(blocks):
        out[at((ids_ref[0] ^ r) * part, part), :] = block[...]


def cut_mlp_kernel(ids_ref, w_up, w_down, up, down, buf, sems):
    c = ids_ref[1] * 2 + ids_ref[2]
    units = up.shape[1]
    one = pltpu.make_async_copy(w_up.at[:, at(c * units, units)], up, sems.at[0])
    two = pltpu.make_async_copy(w_down.at[at(c * units, units), :], buf, sems.at[1])
    one.start()
    two.start()
    two.wait()
    down[...] = buf[...].T
    one.wait()


def cot_kernel(chip_masks, t_count, ids_ref, *refs):
    both, pieces, cot = refs[:2], refs[2:-1], refs[-1]
    chips = len(chip_masks)
    own = cot.shape[0] // (2 * chips)
    for side in range(2):
        for k, mask in enumerate(chip_masks):
            to = (side * chips + k) * own
            y, t = mask // t_count, mask % t_count
            if y == 0:
                cot[to : to + own, :] = both[side][t * own : (t + 1) * own, :]
            else:
                cot[to : to + own, :] = pieces[((y - 1) * t_count + t) * 2 + side][...]


def hidden_kernel(ids_ref, normed_a, normed_b, up, bias_up, act_a, act_b, slope_a, slope_b):
    step = min(512, normed_a.shape[0])
    for normed, act, slope in ((normed_a, act_a, slope_a), (normed_b, act_b, slope_b)):

        def chunk(i, carry, normed=normed, act=act, slope=slope):
            rows = at(i * step, step)
            u = mm(normed[rows, :], up[...], NN) + bias_up[...]
            square = u * u
            th = jnp.tanh(0.7978845608028654 * (u + 0.044715 * square * u))
            act[rows, :] = (0.5 * u * (1.0 + th)).astype(BF16)
            slope[rows, :] = 0.5 * (1.0 + th) + 0.5 * u * (1.0 - th * th) * (
                0.7978845608028654 * (1.0 + 3.0 * 0.044715 * square)
            )
            return carry

        lax.fori_loop(0, normed.shape[0] // step, chunk, 0, unroll=True)


def hidden_back_kernel(side, ids_ref, slope, cot, down, up, d_up, d_norm, grad_bias):
    half = slope.shape[0]
    step = min(512, half)

    def chunk(i, total):
        rows = at(i * step, step)
        d_act = mm(cot[at(side * half + i * step, step), :], down[...], NN)
        g = (d_act * slope[rows, :]).astype(BF16)
        d_up[rows, :] = g
        d_norm[rows, :] = mm(g, up[...], NT).astype(BF16)
        return total + jnp.sum(g.astype(F32), axis=0, keepdims=True)

    grad_bias[...] = lax.fori_loop(0, half // step, chunk, jnp.zeros(grad_bias.shape, F32), unroll=True)


def down_kernel(ids_ref, act_a, act_b, down, keep, give):
    step = min(512, act_a.shape[0])
    for act, out in ((act_b, give), (act_a, keep)):

        def chunk(i, carry, act=act, out=out):
            rows = at(i * step, step)
            out[rows, :] = mm(act[rows, :], down[...], NT).astype(BF16)
            return carry

        lax.fori_loop(0, act.shape[0] // step, chunk, 0, unroll=True)


def join_kernel(ids_ref, keep, landed, *pieces):
    own = pieces[0].shape[0]
    for k, piece in enumerate(pieces):
        rows = slice(k * own, (k + 1) * own)
        piece[...] = (keep[rows, :].astype(F32) + landed[rows, :].astype(F32)).astype(BF16)


def down_grad_kernel(ids_ref, cot, act_a, act_b, *outs):
    half = act_a.shape[0]
    part = outs[0].shape[0]
    for r in range(len(outs) - 1, -1, -1):
        cols = at((ids_ref[0] ^ r) * part, part)
        total = mm(cot[:half, cols], act_a[...], TN) + mm(cot[half:, cols], act_b[...], TN)
        outs[r][...] = total.astype(BF16)


def up_grad_kernel(ids_ref, normed_a, normed_b, d_up_a, d_up_b, near_down, *outs):
    part = outs[0].shape[0]
    for r in range(len(outs) - 1, -1, -1):
        cols = at((ids_ref[0] ^ r) * part, part)
        total = mm(normed_a[:, cols], d_up_a[...], TN) + mm(normed_b[:, cols], d_up_b[...], TN)
        outs[r][:part, :] = total.astype(BF16)
    outs[1][part:, :] = near_down[...]


def join_far_kernel(chips, ids_ref, keep, landed, near, far):
    own = keep.shape[0] // chips
    for k in range(chips):
        rows, to = slice(k * own, (k + 1) * own), slice(k // 2 * own, (k // 2 + 1) * own)
        total = keep[rows, :].astype(F32) + landed[rows, :].astype(F32)
        (far if k % 2 else near)[to, :] = total.astype(BF16)


def fold_kernel(ids_ref, near, landed, *pieces):
    own = pieces[0].shape[0]
    for k, piece in enumerate(pieces):
        rows = slice(k * own, (k + 1) * own)
        piece[...] = (near[rows, :].astype(F32) + landed[rows, :].astype(F32)).astype(BF16)


def add_kernel(ids_ref, a, b, out):
    out[...] = (a[...].astype(F32) + b[...].astype(F32)).astype(BF16)


def mlp_sums_kernel(ups, ids_ref, near, *refs):
    out = refs[-1]
    part = out.shape[0] // 2
    for base, terms in ((0, refs[:ups]), (part, refs[ups:-1])):
        total = near[base : base + part, :].astype(F32)
        for term in terms:
            total += term[...].astype(F32)
        out[base : base + part, :] = total.astype(BF16)


def sum_kernel(ids_ref, *refs):
    total = refs[0][...].astype(F32)
    for ref in refs[1:-1]:
        total += ref[...].astype(F32)
    refs[-1][...] = total.astype(BF16)


def second_back_kernel(cfg, ids_ref, *refs):
    chips = cfg
    landed, refs = refs[:chips], refs[chips:]
    residual, cot, vecs, w_mine, w_other, d_res, branch, grads = refs[:8]
    d_mix = refs[8:]
    own, width = residual.shape
    feats = w_mine.shape[1]
    d_norm = landed[0][...].astype(F32)
    for ref in landed[1:]:
        d_norm += ref[...].astype(F32)
    vhat, scale = normalise(residual[...])
    c = cot[...].astype(F32)
    d_residual = c + norm_grad(vhat, scale, vecs[3:4, :] * d_norm)
    d_res[...] = d_residual
    b = d_residual.astype(BF16)
    branch[...] = b
    for k, piece in enumerate(d_mix):
        rows = slice(k * width, (k + 1) * width)
        piece[:, :feats] = mm(b, w_mine[rows, :], NN).astype(BF16)
        piece[:, feats:] = mm(b, w_other[rows, :], NN).astype(BF16)
    grads[0:1, :] = jnp.sum(d_residual, axis=0, keepdims=True)
    grads[1:2, :] = jnp.sum(vhat * d_norm, axis=0, keepdims=True)
    grads[2:3, :] = jnp.sum(d_norm, axis=0, keepdims=True)
    grads[3:4, :] = jnp.sum(c, axis=0, keepdims=True)


def attend_back_kernel(cfg, ids_ref, qkv, seg_row, seg_col, *refs):
    chip_masks, t_count = cfg
    me = Ids(ids_ref, t_count)
    mixes, refs = refs[: len(chip_masks)], refs[len(chip_masks) :]
    landed, d_qkv, sums, k_heads, v_heads, q_heads, m_heads, dk, dv, mask = refs
    length, feats = qkv.shape[0], dk.shape[1]
    own = mixes[0].shape[0]
    heads = feats // HD
    tile = min(256, length)
    scale = HD ** (-0.5)
    for h in range(heads):
        lanes = head_mask(feats, h)
        for k, m in enumerate(chip_masks):
            piece = mixes[k][:, :feats]
            m_heads[h, me.rows(0, m, own), :] = jnp.where(lanes, piece, jnp.zeros_like(piece))
            piece = landed[k * own : (k + 1) * own, :]
            m_heads[h, me.rows(1, m, own), :] = jnp.where(lanes, piece, jnp.zeros_like(piece))

    def prepare(i, carry):
        rows = at(i * tile, tile)
        for h in range(heads):
            lanes = head_mask(feats, h)
            for k, ref in ((0, q_heads), (1, k_heads), (2, v_heads)):
                piece = qkv[rows, k * feats : (k + 1) * feats]
                if k == 0:
                    piece = piece * BF16(scale)
                ref[h, rows, :] = jnp.where(lanes, piece, jnp.zeros_like(piece))
        dk[rows, :] = jnp.zeros((tile, feats), F32)
        dv[rows, :] = jnp.zeros((tile, feats), F32)
        return carry

    lax.fori_loop(0, length // tile, prepare, 0)
    back = -(-DOC_MOST // tile)
    for i in range(length // tile):
        first = max(0, i - back) * tile
        keys = (i + 1) * tile - first
        rows = slice(i * tile, (i + 1) * tile)
        span = slice(first, first + keys)
        same = seg_col[span, 0:1] == seg_row[:, rows]
        k_pos = first + lax.broadcasted_iota(jnp.int32, (keys, tile), 0)
        q_pos = i * tile + lax.broadcasted_iota(jnp.int32, (keys, tile), 1)
        mask[:keys, :] = jnp.where(same & (k_pos <= q_pos), 0.0, NEGATIVE)
        dq = jnp.zeros((tile, feats), F32)
        dvs = jnp.zeros((keys, feats), F32)
        dks = jnp.zeros((keys, feats), F32)
        for h in range(heads):
            k, v, q, m = k_heads[h, span, :], v_heads[h, span, :], q_heads[h, rows, :], m_heads[h, rows, :]
            s = mm(k, q, NT) + mask[:keys, :]
            e = jnp.exp(s - jnp.max(s, axis=0, keepdims=True))
            p = e * (1.0 / jnp.sum(e, axis=0, keepdims=True))
            dp = mm(v, m, NT)
            row_dot = jnp.sum(p * dp, axis=0, keepdims=True)
            ds = (p * (dp - row_dot)).astype(BF16)
            dvs += mm(p.astype(BF16), m, NN)
            dks += mm(ds, q, NN)
            dq += mm(ds, k, TN)
        dv[span, :] += dvs
        dk[span, :] += dks
        d_qkv[rows, :feats] = (dq * scale).astype(BF16)

    def finish(i, carry):
        rows = at(i * tile, tile)
        d_qkv[rows, feats : 2 * feats] = dk[rows, :].astype(BF16)
        d_qkv[rows, 2 * feats :] = dv[rows, :].astype(BF16)
        return carry + jnp.sum(d_qkv[rows, :].astype(F32), axis=0, keepdims=True)

    sums[...] = lax.fori_loop(0, length // tile, finish, jnp.zeros((1, 3 * feats), F32))


def first_back_kernel(cfg, ids_ref, d_qkv, weight, vhat, keep, give, grads):
    chip_masks, own, t_count = cfg
    me = Ids(ids_ref, t_count)
    span = own * t_count
    gain = jnp.zeros((1, vhat.shape[1]), F32)
    bias = gain
    for out, side in ((give, 1), (keep, 0)):
        for k, mask in enumerate(chip_masks[::t_count]):
            c = (me.y ^ (mask // t_count)) * 2 + (me.core ^ side)
            rows = at(c * span, span)
            d = mm(d_qkv[rows, :], weight[...], NT)
            for t in range(t_count):
                to = at(k * span + (t ^ me.t) * own, own)
                out[to, :] = d[t * own : (t + 1) * own, :].astype(BF16)
            gain += jnp.sum(vhat[rows, :] * d, axis=0, keepdims=True)
            bias += jnp.sum(d, axis=0, keepdims=True)
    grads[0:1, :] = gain
    grads[1:2, :] = bias


def attn_grad_kernel(cfg, ids_ref, normed, d_qkv, attn, branch_a, branch_b, small, small_other, *refs):
    chip_masks, t_count, z_count, vec = cfg
    me = Ids(ids_ref, t_count)
    outs, branch = refs[:-1], refs[-1]
    own = branch_a.shape[0] // len(chip_masks)
    for side, ref in ((0, branch_a), (1, branch_b)):
        for k, mask in enumerate(chip_masks):
            branch[me.rows(side, mask, own), :] = ref[k * own : (k + 1) * own, :]
    count = small.shape[0] // z_count
    feats = attn.shape[1]
    part = normed.shape[1] // z_count
    row = lax.broadcasted_iota(jnp.int32, (count, feats), 0)
    for r in range(z_count - 1, -1, -1):
        out = outs[r]
        cols = at((me.z ^ r) * part, part)
        g = mm(normed[:, cols], d_qkv[...], TN)
        for k in range(3):
            out[k * part : (k + 1) * part, :] = g[:, k * feats : (k + 1) * feats].astype(BF16)
        out[3 * part : 4 * part, :] = mm(branch[:, cols], attn[...], TN).astype(BF16)
        mine = small[r * count : (r + 1) * count, :].astype(F32)
        both = mine + small_other[r * count : (r + 1) * count, :].astype(F32)
        out[4 * part :, :] = jnp.where(row < vec, both, mine).astype(BF16)


def last_kernel(t_count, ids_ref, *refs):
    me = Ids(ids_ref, t_count)
    x, vecs, d_res, out = refs[-4:]
    own = out.shape[0]
    d_norm = refs[0][...].astype(F32)
    for ref in refs[1:-4]:
        d_norm += ref[...].astype(F32)
    vhat, scale = normalise(x[at(me.t * own, own), :].astype(F32))
    out[...] = (d_res[...] + norm_grad(vhat, scale, vecs[0:1, :] * d_norm)).astype(BF16)


def output_kernel(ids_ref, *refs):
    residual, vecs, out = refs[-3:]
    total = residual[...] + vecs[5:6, :]
    for ref in refs[:-3]:
        total += ref[...].astype(F32)
    out[...] = total.astype(BF16)


def pair_kernel(ids_ref, mine, other, out):
    own = mine.shape[0]
    out[at(ids_ref[3] * own, own), :] = mine[...]
    out[at((1 - ids_ref[3]) * own, own), :] = other[...]


def small_grad_kernel(cfg, ids_ref, one, two, sums, bup_a, bup_b, out):
    z_count, heads, rows_up, cols_up = cfg
    width = one.shape[1]
    part = width // z_count
    feats = sums.shape[1] // 3
    units = bup_a.shape[1]
    each = HD // z_count
    wide = out.shape[1]
    vec, q, q_rows, u, u_rows, total = small_rows(part, heads, z_count, rows_up, cols_up, wide)
    per = part // wide
    bqv = (sums[:, :feats].astype(BF16), sums[:, 2 * feats :].astype(BF16))
    bup = (bup_a[...] + bup_b[...]).astype(BF16)
    out[...] = jnp.zeros(out.shape, out.dtype)
    for r in range(z_count):
        z = ids_ref[0] ^ r
        base = r * total
        for i in range(6):
            ref, row = (one, i) if i < 2 else (two, i - 2)
            for j in range(per):
                k = base + i * per + j
                if wide % 128 == 0:
                    out[k : k + 1, :] = ref[row : row + 1, at(z * part + j * wide, wide)].astype(BF16)
                else:
                    lane = lax.broadcasted_iota(jnp.int32, (wide, width), 0)
                    goal = lax.broadcasted_iota(jnp.int32, (wide, width), 1)
                    move = jnp.where(goal == z * part + j * wide + lane, 1.0, 0.0).astype(BF16)
                    out[k : k + 1, :] = mm(ref[row : row + 1, :].astype(BF16), move, NT).astype(BF16)
        lane = lax.broadcasted_iota(jnp.int32, (wide, feats), 0)
        goal = lax.broadcasted_iota(jnp.int32, (wide, feats), 1)
        for i in range(q_rows):
            line = jnp.zeros((1, wide), F32)
            for k in range(2):
                place = lane + i * wide - k * heads * each
                move = (place >= 0) & (place < heads * each)
                move &= goal == (place // each) * HD + z * each + place % each
                line += mm(bqv[k], jnp.where(move, 1.0, 0.0).astype(BF16), NT)
            out[base + vec + i : base + vec + i + 1, :] = line.astype(BF16)
        lane = lax.broadcasted_iota(jnp.int32, (wide, units), 0)
        goal = lax.broadcasted_iota(jnp.int32, (wide, units), 1)
        for i in range(u_rows):
            place = lane + i * wide
            move = (place < u) & (goal == (place // cols_up) * 128 + z * cols_up + place % cols_up)
            row = base + vec + q_rows + i
            out[row : row + 1, :] = mm(bup, jnp.where(move, 1.0, 0.0).astype(BF16), NT).astype(BF16)


def mlp_place_kernel(c_masks, ids_ref, *refs):
    blocks, (up, down) = refs[:-2], refs[-2:]
    c = ids_ref[1] * 2 + ids_ref[2]
    units = blocks[0].shape[1]
    part = blocks[0].shape[0] // 2
    for r, mask in enumerate(c_masks):
        where = at((c ^ mask) * units, units)
        up[:, where] = blocks[r][:part, :].astype(F32)
        down[where, :] = blocks[r][part:, :].astype(F32).T


def attn_place_kernel(cfg, ids_ref, *refs):
    c_masks, heads, rows_up, vec, q_rows = cfg
    blocks = refs[: len(c_masks)]
    qkv, out, *vecs, b_qv, b_up = refs[len(c_masks) :]
    c = ids_ref[1] * 2 + ids_ref[2]
    wide = blocks[0].shape[1]
    part = vecs[0].shape[0]
    each, cols_up = b_qv.shape[2], b_up.shape[1]
    aligned = wide % 128 == 0
    for r, mask in enumerate(c_masks):
        where = at((c ^ mask) * wide, wide)
        if aligned:
            for k in range(3):
                qkv[k, :, where] = blocks[r][k * part : (k + 1) * part, :].astype(F32)
        else:
            for k in range(3):
                qkv[c ^ mask, k] = blocks[r][k * part : (k + 1) * part, :].astype(F32)
        out[where, :] = blocks[r][3 * part : 4 * part, :].astype(F32).T
        base = 4 * part + vec
        for k in range(2):
            for h in range(heads):
                flat = (k * heads + h) * each
                row, lane = base + flat // wide, flat % wide
                b_qv[k, pl.ds((c ^ mask) * heads + h, 1), :] = blocks[r][
                    row : row + 1, lane : lane + each
                ].astype(F32)
        for i in range(rows_up):
            row, lane = base + q_rows + (i * cols_up) // wide, (i * cols_up) % wide
            b_up[pl.ds((c ^ mask) * rows_up + i, 1), :] = blocks[r][
                row : row + 1, lane : lane + cols_up
            ].astype(F32)
    total = blocks[0][4 * part : 4 * part + vec, :].astype(F32)
    for block in blocks[1:]:
        total += block[4 * part : 4 * part + vec, :].astype(F32)
    per = part // wide
    for i, ref in enumerate(vecs):
        lines = [total[i * per + j : i * per + j + 1, :] for j in range(per)]
        ref[...] = (jnp.concatenate(lines, axis=1) if per > 1 else lines[0]).reshape(part)


def body(
    tokens,
    segments,
    ln1_gain,
    ln1_bias,
    w_qkv,
    b_qv,
    w_out,
    b_out,
    ln2_gain,
    ln2_bias,
    w_up,
    b_up,
    w_down,
    b_down,
    cotangent,
):
    z_count, t_count, y_count = (lax.axis_size(a) for a in ("fsdp", "tp", "y"))
    z_me, y_me, core, t_me = (lax.axis_index(a) for a in ("fsdp", "y", "core", "tp"))
    c_me = y_me * 2 + core
    c_count = size_of(CTX)
    c_masks, chip_masks = masks_of(CTX), masks_of(CHIPS)
    chips = len(chip_masks)
    x_span, cot_span = tokens[0], cotangent[0]
    span, width = x_span.shape
    length = span * c_count
    half = length // 2
    own = span // t_count
    feats = w_qkv.shape[2] // c_count
    heads = feats // HD
    units = w_up.shape[1] // c_count
    part = width // z_count
    tile = min(256, length)
    keys = min(length, (-(-DOC_MOST // tile) + 1) * tile)
    rows_up, cols_up = b_up.shape[0] // c_count, b_up.shape[1]
    vec, _, q_rows, _, _, small_count = small_rows(part, heads, z_count, rows_up, cols_up, feats)
    Z, TP = ("fsdp",), ("tp",)
    turned = jnp.swapaxes(w_qkv, 0, 1)
    raw = [ln1_gain, ln1_bias, b_out, ln2_gain, ln2_bias, b_down, b_qv, b_up]
    pack_cfg = (z_count, heads, rows_up, cols_up)
    z_all, c_all = range(z_count), range(c_count)
    known, order, cost = {}, {}, {}

    def node(make):
        def value(*index):
            if (value, index) not in known:
                known[value, index] = make(*index)
            return known[value, index]

        value.title = make.__name__
        return value

    def waits(*key):
        return order[key]() if key in order else []

    def move(key, value, axes, bits):
        pins = waits(*key)
        return swap(after(value, *pins) if pins else value, axes, bits)

    def run(key, kernel, outs, arrays, index=(), **more):
        deps = waits(key, *index)
        declared = cost.get(key, 0.1)
        return kernel_call(kernel, outs, arrays, deps=deps, cost=declared, name=key.title, **more)

    def gathered(key, source, axes, r):
        low = r & -r
        return move((key, r), key(r ^ low), axes, low) if r else source

    def from_chip(key, source, k):
        return move((key, k), source, CHIPS, chip_masks[k]) if k else source

    @node
    def pack():
        out = [shape((4 * part + small_count, feats))]
        if feats % 128:
            cuts = [
                lax.dynamic_slice_in_dim(turned, c_me * feats, feats, 2),
                lax.dynamic_slice_in_dim(w_out, c_me * feats, feats, 0),
            ]
            return run(pack, partial(pack_plain_kernel, pack_cfg), out, [*cuts, *raw])
        scratch = [pltpu.VMEM((feats, part), BF16), *[pltpu.VMEM(v.shape, BF16) for v in raw]]
        return run(
            pack,
            partial(pack_kernel, pack_cfg),
            out,
            [],
            anys=[turned, w_out, *raw],
            scratch=[*scratch, pltpu.SemaphoreType.DMA((12,))],
        )

    @node
    def rows():
        return run(
            rows,
            pack_rows_kernel,
            [shape((own, width)), shape((own, width)), shape((span, width))],
            [],
            anys=[cot_span],
            scratch=[pltpu.SemaphoreType.DMA((4,))],
        )

    @node
    def norm():
        return run(
            norm,
            partial(first_norm_kernel, (c_masks, t_count)),
            [shape((length, width), F32), shape((1, length), F32), shape((length, 128), F32)],
            [x(r) for r in c_all] + [seg(r) for r in c_all],
        )

    @node
    def cut():
        return run(
            cut,
            cut_mlp_kernel,
            [shape((part, units))] * 2,
            [],
            anys=[w_up, w_down],
            scratch=[pltpu.VMEM((units, part), BF16), pltpu.SemaphoreType.DMA((2,))],
        )

    @node
    def unpack():
        return run(
            unpack,
            partial(unpack_kernel, pack_cfg),
            [
                shape((width, 3 * feats)),
                shape((width, feats)),
                shape((8, width), F32),
                shape((2, feats), F32),
                shape((1, units), F32),
            ],
            [attn(r) for r in z_all],
        )

    @node
    def attend():
        vhat, seg_row, seg_col = norm()
        qkv_full, _, vecs, bias_qv, _ = unpack()
        return run(
            attend,
            partial(attend_kernel, (chip_masks, t_count)),
            [
                shape((length, width)),
                shape((length, 3 * feats)),
                shape((length, feats)),
                shape((half, feats)),
                shape((half, feats)),
            ],
            [vhat, qkv_full, vecs, bias_qv, seg_row, seg_col],
            scratch=[pltpu.VMEM((heads, length, feats), BF16)] * 2 + [pltpu.VMEM((tile, keys), F32)],
        )

    def cat(key, blocks):
        size, cols = blocks[0].shape
        return run(key, cat_kernel, [shape((size * len(blocks), cols))], blocks)

    @node
    def wcat():
        return cat(wcat, [wout(k) for k in range(chips)])

    @node
    def beside():
        pieces = [shape((own, 2 * feats))] * chips
        return run(beside, beside_kernel, pieces, [attend()[3], give_mix()])

    @node
    def out_norm():
        return run(
            out_norm,
            partial(out_norm_kernel, t_count),
            [shape((own, width), F32), shape((own, width))],
            [*[mixed(k) for k in range(chips)], wcat()[0], w_other(), x_span, unpack()[2]],
        )

    @node
    def ncat():
        return cat(ncat, [normed(k) for k in range(chips)])

    @node
    def cots():
        pieces = []
        for y in range(1, y_count):
            pieces += [cot_a(y), cot_a_core(y), cot_b(y), cot_b_core(y)]
        return run(
            cots,
            partial(cot_kernel, chip_masks, t_count),
            [shape((length, width))],
            [rows()[2], cot_core(), *pieces],
        )

    @node
    def up_full():
        return run(up_full, place_kernel, [shape((width, units))], [up(r) for r in z_all])

    @node
    def down_full():
        return run(down_full, place_kernel, [shape((width, units))], [down_w(r) for r in z_all])

    @node
    def hidden():
        return run(
            hidden,
            hidden_kernel,
            [shape((half, units))] * 2 + [shape((half, units), F32)] * 2,
            [ncat()[0], normed_b(), up_full()[0], unpack()[4]],
        )

    def back(key, side):
        return run(
            key,
            partial(hidden_back_kernel, side),
            [shape((half, units)), shape((half, width)), shape((1, units), F32)],
            [hidden()[2 + side], cots()[0], down_full()[0], up_full()[0]],
        )

    def join(key, keep, give):
        return run(key, join_kernel, [shape((own, width))] * chips, [keep, give])

    def join_far(key, keep, give):
        outs = [shape((y_count * own, width))] * 2
        return run(key, partial(join_far_kernel, chips), outs, [keep, give])

    def fold(key, near, landed):
        return run(key, fold_kernel, [shape((own, width))] * y_count, [near, landed])

    @node
    def grad_down():
        return run(
            grad_down,
            down_grad_kernel,
            [shape((part, units))] * z_count,
            [cots()[0], hidden()[0], hidden()[1]],
        )

    @node
    def grad_up():
        return run(
            grad_up,
            up_grad_kernel,
            [shape((part if r != 1 else 2 * part, units)) for r in z_all],
            [ncat()[0], normed_b(), back_a()[0], back_b()[0], grad_down()[1]],
        )

    @node
    def down():
        return run(
            down,
            down_kernel,
            [shape((half, width))] * 2,
            [hidden()[0], hidden()[1], down_full()[0]],
        )

    def z_total(key, arrived, pieces, r):
        value = pieces[r]
        for low in (1, 2, 4):
            if low < (r & -r) and r | low < z_count:
                out = [shape(value.shape)]
                (value,) = run(key, add_kernel, out, [value, arrived(r | low)], index=(r,))
        return value

    def z_ends(arrived):
        return [arrived(r) for r in z_all if r > 1 and r == r & -r]

    @node
    def mlp_sums():
        ups = [grad_up()[0], *z_ends(du_in)]
        downs = [grad_down()[0], *z_ends(dd_in)]
        return run(
            mlp_sums,
            partial(mlp_sums_kernel, len(ups)),
            [shape((2 * part, units))],
            [near(), *ups, *downs],
        )

    @node
    def res_back():
        return run(
            res_back,
            partial(second_back_kernel, chips),
            [shape((own, width), F32), shape((own, width)), shape((4, width), F32)]
            + [shape((own, 2 * feats))] * chips,
            [
                *[two(k) for k in range(chips)],
                out_norm()[0],
                rows()[0],
                unpack()[2],
                wcat()[0],
                w_other(),
            ],
        )

    @node
    def apart():
        return run(apart, apart_kernel, [shape((half, feats))], [d_mix(k) for k in range(chips)])

    @node
    def attend_back():
        return run(
            attend_back,
            partial(attend_back_kernel, (chip_masks, t_count)),
            [shape((length, 3 * feats)), shape((1, 3 * feats), F32)],
            [
                attend()[1],
                norm()[1],
                norm()[2],
                *[d_mix(k) for k in range(chips)],
                d_mix_core(),
            ],
            scratch=[pltpu.VMEM((heads, length, feats), BF16)] * 4
            + [pltpu.VMEM((length, feats), F32)] * 2
            + [pltpu.VMEM((keys, tile), F32)],
        )

    @node
    def bcat():
        return cat(bcat, [branch(k) for k in range(chips)])

    @node
    def norm_back():
        return run(
            norm_back,
            partial(first_back_kernel, (chip_masks, own, t_count)),
            [shape((half, width)), shape((half, width)), shape((2, width), F32)],
            [attend_back()[0], unpack()[0], norm()[0]],
        )

    @node
    def small():
        return run(
            small,
            partial(small_grad_kernel, (z_count, heads, rows_up, cols_up)),
            [shape((z_count * small_count, feats))],
            [norm_back()[2], res_back()[2], attend_back()[1], back_a()[2], back_b()[2]],
        )

    @node
    def grad_attn():
        return run(
            grad_attn,
            partial(attn_grad_kernel, (chip_masks, t_count, z_count, vec)),
            [shape((4 * part + small_count, feats))] * z_count,
            [
                attend()[0],
                attend_back()[0],
                attend()[2],
                bcat()[0],
                branch_b(),
                small()[0],
                small_tp(),
            ],
            scratch=[pltpu.VMEM((length, width), BF16)],
        )

    @node
    def attn_sums():
        terms = [grad_attn()[0], da_in(1), *z_ends(da_in)]
        return run(attn_sums, sum_kernel, [shape(terms[0].shape)], terms)

    @node
    def last():
        return run(
            last,
            partial(last_kernel, t_count),
            [shape((own, width))],
            [fold_one()[0], *[one(y) for y in range(1, y_count)], x_span, unpack()[2], res_back()[0]],
        )

    @node
    def out():
        sums = [fold_down()[0], *[down_in(y) for y in range(1, y_count)]]
        arrays = [*sums, out_norm()[0], unpack()[2]]
        return run(out, output_kernel, [shape((own, width))], arrays)

    def pair(key, mine, other):
        return run(key, pair_kernel, [shape((span, width))], [mine, other])

    @node
    def mlp_place():
        return run(
            mlp_place,
            partial(mlp_place_kernel, c_masks),
            [shape((part, c_count * units), F32), shape((c_count * units, part), F32)],
            [mlp_all(r) for r in c_all],
        )

    @node
    def attn_place():
        return run(
            attn_place,
            partial(attn_place_kernel, (c_masks, heads, rows_up, vec, q_rows)),
            [
                shape((3, part, c_count * feats) if feats % 128 == 0 else (c_count, 3, part, feats), F32),
                shape((c_count * feats, part), F32),
                *[shape((part,), F32)] * 6,
                shape(b_qv.shape, F32),
                shape(b_up.shape, F32),
            ],
            [attn_all(r) for r in c_all],
        )

    @node
    def back_a():
        return back(back_a, 0)

    @node
    def back_b():
        return back(back_b, 1)

    @node
    def join_two():
        return join(join_two, back_a()[1], give_two())

    @node
    def join_down():
        return join_far(join_down, down()[0], give_down())

    @node
    def fold_down():
        return fold(fold_down, join_down()[0], down_x())

    @node
    def join_one():
        return join_far(join_one, norm_back()[0], give_one())

    @node
    def fold_one():
        return fold(fold_one, join_one()[0], one_x())

    @node
    def pair_out():
        return pair(pair_out, out()[0], out_tp())

    @node
    def pair_tok():
        return pair(pair_tok, last()[0], last_tp())

    @node
    def dd_sum(r):
        return z_total(dd_sum, dd_in, grad_down(), r)

    @node
    def du_sum(r):
        return z_total(du_sum, du_in, grad_up(), r)

    @node
    def da_sum(r):
        return z_total(da_sum, da_in, grad_attn(), r)

    attn = node(lambda r: gathered(attn, pack()[0], Z, r))
    x = node(lambda r: gathered(x, x_span, CTX, r))
    seg = node(lambda r: gathered(seg, segments, CTX, r))
    up = node(lambda r: gathered(up, cut()[0], Z, r))
    down_w = node(lambda r: gathered(down_w, cut()[1], Z, r))
    cot_core = node(lambda: move((cot_core,), rows()[2], CTX, 1))
    cot_a = node(lambda y: move((cot_a, y), rows()[0], CTX, 2 * y))
    cot_b = node(lambda y: move((cot_b, y), rows()[1], CTX, 2 * y))
    cot_a_core = node(lambda y: move((cot_a_core, y), cot_a(y), CTX, 1))
    cot_b_core = node(lambda y: move((cot_b_core, y), cot_b(y), CTX, 1))
    wout = node(lambda k: from_chip(wout, unpack()[1], k))
    w_other = node(lambda: move((w_other,), wcat()[0], CTX, 1))
    give_mix = node(lambda: move((give_mix,), attend()[4], CTX, 1))
    mixed = node(lambda k: from_chip(mixed, beside()[k], k))
    normed = node(lambda k: from_chip(normed, out_norm()[1], k))
    normed_b = node(lambda: move((normed_b,), ncat()[0], CTX, 1))
    give_two = node(lambda: move((give_two,), back_b()[1], CTX, 1))
    two = node(lambda k: from_chip(two, join_two()[k], k))
    give_down = node(lambda: move((give_down,), down()[1], CTX, 1))
    down_x = node(lambda: move((down_x,), join_down()[1], TP, 1))
    down_in = node(lambda y: move((down_in, y), fold_down()[y], CTX, 2 * y))
    give_one = node(lambda: move((give_one,), norm_back()[1], CTX, 1))
    one_x = node(lambda: move((one_x,), join_one()[1], TP, 1))
    one = node(lambda y: move((one, y), fold_one()[y], CTX, 2 * y))
    d_mix = node(lambda k: from_chip(d_mix, res_back()[3 + k], k))
    d_mix_core = node(lambda: move((d_mix_core,), apart()[0], CTX, 1))
    branch = node(lambda k: from_chip(branch, res_back()[1], k))
    branch_b = node(lambda: move((branch_b,), bcat()[0], CTX, 1))
    small_tp = node(lambda: move((small_tp,), small()[0], TP, 1))
    near = node(lambda: move((near,), grad_up()[1], Z, 1))
    dd_in = node(lambda r: move((dd_in, r), dd_sum(r), Z, r & -r))
    du_in = node(lambda r: move((du_in, r), du_sum(r), Z, r & -r))
    da_in = node(lambda r: move((da_in, r), da_sum(r), Z, r & -r))
    out_tp = node(lambda: move((out_tp,), out()[0], TP, 1))
    last_tp = node(lambda: move((last_tp,), last()[0], TP, 1))
    mlp_all = node(lambda r: gathered(mlp_all, mlp_sums()[0], CTX, r))
    attn_all = node(lambda r: gathered(attn_all, attn_sums()[0], CTX, r))

    order |= {
        (x, 3): lambda: [attn(1), attn(2), seg(1)],
        (cut,): lambda: [norm()[1]],
        (unpack,): lambda: [norm()[1], cut()[0], cot_a(1)],
        (attend,): lambda: [attn(3)],
        (wcat,): lambda: [up(1)],
        (out_norm,): lambda: [up(3)],
        (ncat,): lambda: [down_w(1), down_w(2)],
        (cots,): lambda: [ncat()[0]],
        (up_full,): lambda: [cots()[0]],
        (down_full,): lambda: [hidden()[0], normed(3)],
        (grad_up,): lambda: [join_two()[0], dd_in(3)],
        (dd_sum, 2): lambda: [down()[0]],
        (branch, 2): lambda: [du_sum(2)],
        (branch, 3): lambda: [apart()[0], du_sum(2)],
        (attend_back,): lambda: [dd_in(2), d_mix(3)],
        (join_one,): lambda: [grad_attn()[0], mlp_all(1), branch(3)],
        (mlp_all, 3): lambda: [mlp_all(1), small_tp()],
        (da_sum, 2): lambda: [join_one()[0], small()[0]],
        (last,): lambda: [da_sum(2), mlp_all(1)],
        (small,): lambda: [branch(2)],
        (normed_b,): lambda: [mixed(2)],
        (two, 3): lambda: [normed_b()],
        (two, 2): lambda: [normed(2)],
        (mixed, 2): lambda: [w_other()],
        (cot_a_core, 1): lambda: [wout(3)],
        (rows,): lambda: [pack()[0]],
        (dd_in, 2): lambda: [grad_up()[0]],
        (branch_b,): lambda: [d_mix_core(), mlp_sums()[0]],
        (cot_a, 1): lambda: [cot_core()],
        (norm_back,): lambda: [branch(2)],
        (mlp_all, 1): lambda: [branch(2)],
        (down_w, 3): lambda: [normed(3)],
        (grad_attn,): lambda: [give_one()],
        (attn_place,): lambda: [attn_sums()[0]],
        (mixed, 3): lambda: [up(2)],
        (du_in, 2): lambda: [res_back()[0]],
        (one_x,): lambda: [join_one()[0]],
        (cot_core,): lambda: [seg(3)],
        (da_in, 2): lambda: [small_tp()],
        (attn_sums,): lambda: [give_one()],
        (down_w, 1): lambda: [mixed(3)],
        (back_a,): lambda: [back_b()[0], normed_b()],
    }
    cost |= {
        pack: 8,
        rows: 0.01,
        norm: 8,
        cut: 1,
        unpack: 1,
        attend: 8,
        out_norm: 1,
        cots: 4,
        up_full: 2,
        down_full: 8,
        hidden: 0.3,
        back_b: 2,
        grad_up: 1.5,
        down: 1,
        res_back: 0.3,
        small: 8,
        grad_attn: 4,
        last: 1,
        out: 1,
        pair_out: 1,
        pair_tok: 16,
        mlp_place: 1,
        apart: 2,
        beside: 8,
        ncat: 16,
        attn_sums: 4,
        da_sum: 0.01,
        bcat: 1,
        dd_sum: 0.01,
        norm_back: 1,
        join_one: 1,
        du_sum: 8,
    }
    full_qkv, full_out, *vec_sum, full_bqv, full_bup = attn_place()
    if feats % 128:
        full_qkv = full_qkv.transpose(1, 2, 0, 3).reshape(3, part, c_count * feats)
    full_up, full_down = mlp_place()
    return (
        pair_out()[0][None],
        pair_tok()[0][None],
        vec_sum[0],
        vec_sum[1],
        jnp.swapaxes(full_qkv, 0, 1),
        full_bqv,
        full_out,
        vec_sum[2],
        vec_sum[3],
        vec_sum[4],
        full_up,
        full_bup,
        full_down,
        vec_sum[5],
    )


def solution(mesh):
    fsdp, ctx, tp = (mesh.shape[a] for a in ("fsdp", "ctx", "tp"))
    split = Mesh(mesh.devices.reshape(fsdp, ctx // 2, 2, tp), ("fsdp", "y", "core", "tp"))
    rows = P("fsdp", CTX, None)
    shares = (
        P("fsdp"),
        P("fsdp"),
        P("fsdp", None, "tp"),
        P(None, "tp", "fsdp"),
        P("tp", "fsdp"),
        P("fsdp"),
        P("fsdp"),
        P("fsdp"),
        P("fsdp", "tp"),
        P("tp", "fsdp"),
        P("tp", "fsdp"),
        P("fsdp"),
    )
    return jax.shard_map(
        body,
        mesh=split,
        in_specs=(rows, P("fsdp", CTX), *shares, rows),
        out_specs=(rows, rows, *shares),
        check_vma=False,
    )
```

```python
from functools import partial

import jax
import jax.numpy as jnp
import numpy as np
from jax import lax
from jax.experimental import pallas as pl
from jax.experimental.pallas import tpu as pltpu
from jax.sharding import Mesh
from jax.sharding import PartitionSpec as P

HD = 64
DOC_MOST = 512
EPSILON = 1e-05
NEGATIVE = -1e30
F32 = jnp.float32
FLOPS_PER_US = 2e9
BF16 = jnp.bfloat16

CTX = ("y", "core")
CHIPS = ("y", "tp")


def size_of(axes):
    return int(np.prod([lax.axis_size(a) for a in axes]))


def swap(value, axes, bits):
    count = size_of(axes)
    return lax.ppermute(value, axes, [(i, i ^ bits) for i in range(count)])


def masks_of(axes):
    bits, at = [], 1
    for a in reversed(axes):
        mine = []
        while len(mine) < (lax.axis_size(a) - 1).bit_length():
            mine.append(at)
            at *= 2
        bits = mine + bits if a == "core" else bits + mine
    masks = [0]
    for r in range(1, size_of(axes)):
        low = r & -r
        masks.append(masks[r ^ low] | bits[low.bit_length() - 1])
    return masks


def after(value, *others):
    return lax.optimization_barrier((value, *others))[0]


class Place:
    def __getitem__(self, axis):
        return lax.axis_index(("fsdp", "y", "core", "tp")[axis])


def kernel_call(kernel, outs, arrays, scratch=(), cost=1.0, name=None, vmem=12, deps=(), anys=()):
    deps = list(deps)
    extra = len(deps)

    def run(*refs):
        kernel(Place(), *refs[extra:])

    def place(space):
        return pl.BlockSpec(memory_space=space)

    return pl.pallas_call(
        run,
        out_shape=[jax.ShapeDtypeStruct(s.shape, s.dtype) for s in outs],
        in_specs=[place(pl.ANY)] * extra
        + [place(pltpu.HBM)] * len(anys)
        + [place(pltpu.VMEM)] * len(arrays),
        out_specs=[place(pltpu.VMEM)] * len(outs),
        scratch_shapes=list(scratch),
        compiler_params=pltpu.CompilerParams(vmem_limit_bytes=vmem << 20),
        cost_estimate=pl.CostEstimate(
            flops=int(cost * FLOPS_PER_US), bytes_accessed=int(cost * 1e5), transcendentals=0
        ),
        name=name,
    )(*deps, *[pltpu.with_memory_space_constraint(a, pltpu.HBM) for a in anys], *arrays)


def shape(dims, dtype=BF16):
    return jax.ShapeDtypeStruct(tuple(dims), dtype)


NN = (((1,), (0,)), ((), ()))
NT = (((1,), (1,)), ((), ()))
TN = (((0,), (0,)), ((), ()))


def mm(a, b, dims):
    return lax.dot_general(a, b, dims, preferred_element_type=F32)


def at(start, size, unit=None):
    return pl.ds(pl.multiple_of(start, unit or size), size)


def normalise(values):
    centred = values - jnp.mean(values, axis=-1, keepdims=True)
    variance = jnp.mean(centred * centred, axis=-1, keepdims=True)
    scale = lax.rsqrt(variance + EPSILON)
    return centred * scale, scale


def norm_grad(vhat, scale, weighted):
    return scale * (
        weighted
        - jnp.mean(weighted, axis=-1, keepdims=True)
        - vhat * jnp.mean(weighted * vhat, axis=-1, keepdims=True)
    )


class Ids:
    def __init__(self, ref, t_count):
        self.z, self.y, self.core, self.t = ref[0], ref[1], ref[2], ref[3]
        self.c = self.y * 2 + self.core
        self.p = self.c * t_count + self.t
        self.t_count = t_count

    def rows(self, side, mask, own):
        c = (self.y ^ (mask // self.t_count)) * 2 + (self.core ^ side)
        return at((c * self.t_count + (self.t ^ (mask % self.t_count))) * own, own)


def small_rows(part, heads, z_count, rows_up, cols_up, wide):
    vec = 6 * part // wide
    q = 2 * heads * (HD // z_count)
    u = rows_up * cols_up
    q_rows, u_rows = -(-q // wide), -(-u // wide)
    total = vec + q_rows + u_rows
    return vec, q, q_rows, u, u_rows, -(-total // 16) * 16


def pick(table, index):
    row = lax.broadcasted_iota(jnp.int32, table.shape, 0)
    return jnp.sum(jnp.where(row == index, table.astype(F32), 0.0), axis=0, keepdims=True).astype(BF16)


def lay_rows(out, first, pieces, wide):
    line, used = [], 0
    for piece in [*pieces, None]:
        if piece is None or used + piece.shape[1] > wide:
            if line:
                gap = wide - used
                if gap:
                    line.append(jnp.zeros((1, gap), line[0].dtype))
                out[first : first + 1, :] = jnp.concatenate(line, axis=1) if len(line) > 1 else line[0]
                first, line, used = first + 1, [], 0
        if piece is not None:
            line.append(piece)
            used += piece.shape[1]


def copy_in(pairs, sems):
    copies = [pltpu.make_async_copy(a, b, sems.at[i]) for i, (a, b) in enumerate(pairs)]
    for copy in copies:
        copy.start()
    return copies


def pack_kernel(cfg, ids_ref, w_qkv, w_out, *refs):
    params, out, buf, bufs, sems = refs[:8], refs[8], refs[9], refs[10:18], refs[18]
    c = ids_ref[1] * 2 + ids_ref[2]
    feats = out.shape[1]
    part = w_out.shape[1]
    pairs = [
        (w_qkv.at[k, :, at(c * feats, feats)], out.at[k * part : (k + 1) * part, :]) for k in range(3)
    ]
    pairs.append((w_out.at[at(c * feats, feats), :], buf))
    copies = copy_in(pairs + list(zip(params, bufs)), sems)
    for copy in copies[3:]:
        copy.wait()
    out[3 * part : 4 * part, :] = buf[...].T
    pack_small(cfg, c, bufs[:6], bufs[6], bufs[7], out, 4 * part)
    for copy in copies[:3]:
        copy.wait()


def pack_rows_kernel(ids_ref, cot, mine, other, both, sems):
    t = ids_ref[3]
    own = mine.shape[0]
    near, far = cot.at[at(t * own, own), :], cot.at[at((1 - t) * own, own), :]
    pairs = [(near, mine), (far, other), (near, both.at[:own, :]), (far, both.at[own:, :])]
    for copy in copy_in(pairs, sems):
        copy.wait()


def pack_plain_kernel(cfg, ids_ref, w_qkv, w_out, *refs):
    z_count, heads, rows_up, cols_up = cfg
    vectors, (b_qv, b_up, out) = refs[:6], refs[6:]
    part = w_out.shape[1]
    for k in range(3):
        out[k * part : (k + 1) * part, :] = w_qkv[k]
    out[3 * part : 4 * part, :] = w_out[...].T
    pack_small(cfg, ids_ref[1] * 2 + ids_ref[2], vectors, b_qv, b_up, out, 4 * part)


def pack_small(cfg, c, vectors, b_qv, b_up, out, base):
    z_count, heads, rows_up, cols_up = cfg
    wide = out.shape[1]
    part = vectors[0].shape[-1]
    vec, q, q_rows, u, u_rows, total = small_rows(part, heads, z_count, rows_up, cols_up, wide)
    out[base : base + total, :] = jnp.zeros((total, wide), out.dtype)
    per = part // wide
    for i, ref in enumerate(vectors):
        line = ref[...].reshape(1, part)
        for j in range(per):
            row = base + i * per + j
            out[row : row + 1, :] = line[:, j * wide : (j + 1) * wide]
    q_lines = [pick(b_qv[k], c * heads + h) for k in range(2) for h in range(heads)]
    lay_rows(out, base + vec, q_lines, wide)
    lay_rows(out, base + vec + q_rows, [pick(b_up[...], c * rows_up + i) for i in range(rows_up)], wide)


def first_norm_kernel(cfg, ids_ref, *refs):
    c_masks, t_count = cfg
    me = Ids(ids_ref, t_count)
    count = len(c_masks)
    x, seg, (vhat_out, seg_row, seg_col) = refs[:count], refs[count : 2 * count], refs[2 * count :]
    span = x[0].shape[0]
    for r, mask in enumerate(c_masks):
        seg_row[:, at((me.c ^ mask) * span, span)] = seg[r][...].astype(F32)
    for i in range(seg_row.shape[1] // 128):
        block = jnp.broadcast_to(seg_row[:, i * 128 : (i + 1) * 128], (128, 128))
        seg_col[i * 128 : (i + 1) * 128, :] = block.T
    step = min(64, span)
    for r, mask in enumerate(c_masks):

        def chunk(i, carry, r=r, mask=mask):
            vhat, _ = normalise(x[r][at(i * step, step), :].astype(F32))
            vhat_out[at((me.c ^ mask) * span + i * step, step), :] = vhat
            return carry

        lax.fori_loop(0, span // step, chunk, 0, unroll=True)


def unpack_kernel(cfg, ids_ref, *refs):
    z_count, heads, rows_up, cols_up = cfg
    small, (weight, out_w, vecs, bias_qv, bias_up) = refs[:z_count], refs[z_count:]
    width = weight.shape[0]
    part = width // z_count
    feats = bias_qv.shape[1]
    units = bias_up.shape[1]
    each = HD // z_count
    wide = small[0].shape[1]
    vec, q, q_rows, u, u_rows, total = small_rows(part, heads, z_count, rows_up, cols_up, wide)
    base = 4 * part
    per = part // wide
    qv = [jnp.zeros((1, feats), F32), jnp.zeros((1, feats), F32)]
    ups = jnp.zeros((1, units), F32)
    if wide % 128:
        vecs[...] = jnp.zeros(vecs.shape, F32)
    for r in range(z_count):
        z = ids_ref[0] ^ r
        where = at(z * part, part)
        for k in range(3):
            weight[where, k * feats : (k + 1) * feats] = small[r][k * part : (k + 1) * part, :]
        out_w[where, :] = small[r][3 * part : 4 * part, :]
        for i in range(6):
            for j in range(per):
                row = base + i * per + j
                line = small[r][row : row + 1, :]
                if wide % 128 == 0:
                    vecs[i : i + 1, at(z * part + j * wide, wide)] = line.astype(F32)
                else:
                    lane = lax.broadcasted_iota(jnp.int32, (wide, width), 0)
                    goal = lax.broadcasted_iota(jnp.int32, (wide, width), 1)
                    move = jnp.where(goal == z * part + j * wide + lane, 1.0, 0.0).astype(BF16)
                    vecs[i : i + 1, :] += mm(line, move, NN)
        lane = lax.broadcasted_iota(jnp.int32, (wide, feats), 0)
        goal = lax.broadcasted_iota(jnp.int32, (wide, feats), 1)
        for k in range(2):
            for i in range(q_rows):
                place = lane + i * wide - k * heads * each
                move = (place >= 0) & (place < heads * each)
                move &= goal == (place // each) * HD + z * each + place % each
                row = base + vec + i
                qv[k] += mm(small[r][row : row + 1, :], jnp.where(move, 1.0, 0.0).astype(BF16), NN)
        lane = lax.broadcasted_iota(jnp.int32, (wide, units), 0)
        goal = lax.broadcasted_iota(jnp.int32, (wide, units), 1)
        for i in range(u_rows):
            place = lane + i * wide
            move = (place < u) & (goal == (place // cols_up) * 128 + z * cols_up + place % cols_up)
            row = base + vec + q_rows + i
            ups += mm(small[r][row : row + 1, :], jnp.where(move, 1.0, 0.0).astype(BF16), NN)
    for k in range(2):
        bias_qv[k : k + 1, :] = qv[k]
    bias_up[...] = ups


def head_mask(width, head):
    lane = lax.broadcasted_iota(jnp.int32, (1, width), 1)
    return (lane // HD) == head


def attend_kernel(
    cfg, ids_ref, vhat, weight, vecs, bias_qv, seg_row, seg_col, normed, qkv, attn, keep, give, k_heads, v_heads, mask
):
    chip_masks, t_count = cfg
    me = Ids(ids_ref, t_count)
    length, feats = attn.shape
    heads = feats // HD
    tile = min(256, length)

    def project(i, carry):
        rows = at(i * tile, tile)
        x = (vhat[rows, :] * vecs[0:1, :] + vecs[1:2, :]).astype(BF16)
        normed[rows, :] = x
        out = mm(x, weight[...], NN)
        q = (out[:, :feats] + bias_qv[0:1, :]).astype(BF16)
        k = out[:, feats : 2 * feats].astype(BF16)
        v = (out[:, 2 * feats :] + bias_qv[1:2, :]).astype(BF16)
        qkv[rows, :feats] = q
        qkv[rows, feats : 2 * feats] = k
        qkv[rows, 2 * feats :] = v
        for h in range(heads):
            lanes = head_mask(feats, h)
            k_heads[h, rows, :] = jnp.where(lanes, k, jnp.zeros_like(k))
            v_heads[h, rows, :] = jnp.where(lanes, v, jnp.zeros_like(v))
        return carry

    lax.fori_loop(0, length // tile, project, 0)
    back = -(-DOC_MOST // tile)
    for i in range(length // tile):
        first = max(0, i - back) * tile
        keys = (i + 1) * tile - first
        rows = slice(i * tile, (i + 1) * tile)
        q = qkv[rows, :feats] * BF16(HD ** (-0.5))
        same = seg_col[rows, 0:1] == seg_row[:, first : first + keys]
        q_pos = i * tile + lax.broadcasted_iota(jnp.int32, (tile, keys), 0)
        k_pos = first + lax.broadcasted_iota(jnp.int32, (tile, keys), 1)
        mask[:, :keys] = jnp.where(same & (k_pos <= q_pos), 0.0, NEGATIVE)
        total = jnp.zeros((tile, feats), F32)
        for h in range(heads):
            s = mm(q, k_heads[h, first : first + keys, :], NT) + mask[:, :keys]
            e = jnp.exp(s - jnp.max(s, axis=1, keepdims=True))
            scale = 1.0 / jnp.sum(e, axis=1, keepdims=True)
            total += mm((e * scale).astype(BF16), v_heads[h, first : first + keys, :], NN)
        attn[rows, :] = total.astype(BF16)
    own = keep.shape[0] // len(chip_masks)
    for side, out in ((1, give), (0, keep)):
        for k in range(len(chip_masks)):
            out[k * own : (k + 1) * own, :] = attn[me.rows(side, chip_masks[k], own), :]


def cat_kernel(ids_ref, *refs):
    rows = refs[0].shape[0]
    for k, ref in enumerate(refs[:-1]):
        refs[-1][k * rows : (k + 1) * rows, :] = ref[...]


def beside_kernel(ids_ref, keep, landed, *pieces):
    own, both = pieces[0].shape
    for k, piece in enumerate(pieces):
        rows = slice(k * own, (k + 1) * own)
        piece[:, : both // 2] = keep[rows, :]
        piece[:, both // 2 :] = landed[rows, :]


def apart_kernel(ids_ref, *refs):
    pieces, out = refs[:-1], refs[-1]
    own, feats = pieces[0].shape[0], out.shape[1]
    for k, piece in enumerate(pieces):
        out[k * own : (k + 1) * own, :] = piece[:, feats:]


def out_norm_kernel(t_count, ids_ref, *refs):
    me = Ids(ids_ref, t_count)
    w_mine, w_other, x, vecs, residual, normed = refs[-6:]
    own, width = residual.shape
    feats = w_mine.shape[1]
    total = x[at(me.t * own, own), :].astype(F32) + vecs[2:3, :]
    for k, piece in enumerate(refs[:-6]):
        rows = slice(k * width, (k + 1) * width)
        total += mm(piece[:, :feats], w_mine[rows, :], NT) + mm(piece[:, feats:], w_other[rows, :], NT)
    residual[...] = total
    vhat, _ = normalise(total)
    normed[...] = (vhat * vecs[3:4, :] + vecs[4:5, :]).astype(BF16)


def place_kernel(ids_ref, *refs):
    blocks, out = refs[:-1], refs[-1]
    part = blocks[0].shape[0]
    for r, block in enumerate(blocks):
        out[at((ids_ref[0] ^ r) * part, part), :] = block[...]


def cut_mlp_kernel(ids_ref, w_up, w_down, up, down, buf, sems):
    c = ids_ref[1] * 2 + ids_ref[2]
    units = up.shape[1]
    one = pltpu.make_async_copy(w_up.at[:, at(c * units, units)], up, sems.at[0])
    two = pltpu.make_async_copy(w_down.at[at(c * units, units), :], buf, sems.at[1])
    one.start()
    two.start()
    two.wait()
    down[...] = buf[...].T
    one.wait()


def cot_kernel(chip_masks, t_count, ids_ref, *refs):
    both, pieces, cot = refs[:2], refs[2:-1], refs[-1]
    chips = len(chip_masks)
    own = cot.shape[0] // (2 * chips)
    for side in range(2):
        for k, mask in enumerate(chip_masks):
            to = (side * chips + k) * own
            y, t = mask // t_count, mask % t_count
            if y == 0:
                cot[to : to + own, :] = both[side][t * own : (t + 1) * own, :]
            else:
                cot[to : to + own, :] = pieces[((y - 1) * t_count + t) * 2 + side][...]


def hidden_kernel(ids_ref, normed_a, normed_b, up, bias_up, act_a, act_b, slope_a, slope_b):
    step = min(512, normed_a.shape[0])
    for normed, act, slope in ((normed_a, act_a, slope_a), (normed_b, act_b, slope_b)):

        def chunk(i, carry, normed=normed, act=act, slope=slope):
            rows = at(i * step, step)
            u = mm(normed[rows, :], up[...], NN) + bias_up[...]
            square = u * u
            th = jnp.tanh(0.7978845608028654 * (u + 0.044715 * square * u))
            act[rows, :] = (0.5 * u * (1.0 + th)).astype(BF16)
            slope[rows, :] = 0.5 * (1.0 + th) + 0.5 * u * (1.0 - th * th) * (
                0.7978845608028654 * (1.0 + 3.0 * 0.044715 * square)
            )
            return carry

        lax.fori_loop(0, normed.shape[0] // step, chunk, 0, unroll=True)


def hidden_back_kernel(side, ids_ref, slope, cot, down, up, d_up, d_norm, grad_bias):
    half = slope.shape[0]
    step = min(512, half)

    def chunk(i, total):
        rows = at(i * step, step)
        d_act = mm(cot[at(side * half + i * step, step), :], down[...], NN)
        g = (d_act * slope[rows, :]).astype(BF16)
        d_up[rows, :] = g
        d_norm[rows, :] = mm(g, up[...], NT).astype(BF16)
        return total + jnp.sum(g.astype(F32), axis=0, keepdims=True)

    grad_bias[...] = lax.fori_loop(0, half // step, chunk, jnp.zeros(grad_bias.shape, F32), unroll=True)


def down_kernel(ids_ref, act_a, act_b, down, keep, give):
    step = min(512, act_a.shape[0])
    for act, out in ((act_b, give), (act_a, keep)):

        def chunk(i, carry, act=act, out=out):
            rows = at(i * step, step)
            out[rows, :] = mm(act[rows, :], down[...], NT).astype(BF16)
            return carry

        lax.fori_loop(0, act.shape[0] // step, chunk, 0, unroll=True)


def join_kernel(ids_ref, keep, landed, *pieces):
    own = pieces[0].shape[0]
    for k, piece in enumerate(pieces):
        rows = slice(k * own, (k + 1) * own)
        piece[...] = (keep[rows, :].astype(F32) + landed[rows, :].astype(F32)).astype(BF16)


def down_grad_kernel(ids_ref, cot, act_a, act_b, *outs):
    half = act_a.shape[0]
    part = outs[0].shape[0]
    for r in range(len(outs) - 1, -1, -1):
        cols = at((ids_ref[0] ^ r) * part, part)
        total = mm(cot[:half, cols], act_a[...], TN) + mm(cot[half:, cols], act_b[...], TN)
        outs[r][...] = total.astype(BF16)


def up_grad_kernel(ids_ref, normed_a, normed_b, d_up_a, d_up_b, near_down, *outs):
    part = outs[0].shape[0]
    for r in range(len(outs) - 1, -1, -1):
        cols = at((ids_ref[0] ^ r) * part, part)
        total = mm(normed_a[:, cols], d_up_a[...], TN) + mm(normed_b[:, cols], d_up_b[...], TN)
        outs[r][:part, :] = total.astype(BF16)
    outs[1][part:, :] = near_down[...]


def join_far_kernel(chips, ids_ref, keep, landed, near, far):
    own = keep.shape[0] // chips
    for k in range(chips):
        rows, to = slice(k * own, (k + 1) * own), slice(k // 2 * own, (k // 2 + 1) * own)
        total = keep[rows, :].astype(F32) + landed[rows, :].astype(F32)
        (far if k % 2 else near)[to, :] = total.astype(BF16)


def fold_kernel(ids_ref, near, landed, *pieces):
    own = pieces[0].shape[0]
    for k, piece in enumerate(pieces):
        rows = slice(k * own, (k + 1) * own)
        piece[...] = (near[rows, :].astype(F32) + landed[rows, :].astype(F32)).astype(BF16)


def add_kernel(ids_ref, a, b, out):
    out[...] = (a[...].astype(F32) + b[...].astype(F32)).astype(BF16)


def mlp_sums_kernel(ups, ids_ref, near, *refs):
    out = refs[-1]
    part = out.shape[0] // 2
    for base, terms in ((0, refs[:ups]), (part, refs[ups:-1])):
        total = near[base : base + part, :].astype(F32)
        for term in terms:
            total += term[...].astype(F32)
        out[base : base + part, :] = total.astype(BF16)


def sum_kernel(ids_ref, *refs):
    total = refs[0][...].astype(F32)
    for ref in refs[1:-1]:
        total += ref[...].astype(F32)
    refs[-1][...] = total.astype(BF16)


def second_back_kernel(cfg, ids_ref, *refs):
    chips = cfg
    landed, refs = refs[:chips], refs[chips:]
    residual, cot, vecs, w_mine, w_other, d_res, branch, grads = refs[:8]
    d_mix = refs[8:]
    own, width = residual.shape
    feats = w_mine.shape[1]
    d_norm = landed[0][...].astype(F32)
    for ref in landed[1:]:
        d_norm += ref[...].astype(F32)
    vhat, scale = normalise(residual[...])
    c = cot[...].astype(F32)
    d_residual = c + norm_grad(vhat, scale, vecs[3:4, :] * d_norm)
    d_res[...] = d_residual
    b = d_residual.astype(BF16)
    branch[...] = b
    for k, piece in enumerate(d_mix):
        rows = slice(k * width, (k + 1) * width)
        piece[:, :feats] = mm(b, w_mine[rows, :], NN).astype(BF16)
        piece[:, feats:] = mm(b, w_other[rows, :], NN).astype(BF16)
    grads[0:1, :] = jnp.sum(d_residual, axis=0, keepdims=True)
    grads[1:2, :] = jnp.sum(vhat * d_norm, axis=0, keepdims=True)
    grads[2:3, :] = jnp.sum(d_norm, axis=0, keepdims=True)
    grads[3:4, :] = jnp.sum(c, axis=0, keepdims=True)


def attend_back_kernel(cfg, ids_ref, qkv, seg_row, seg_col, *refs):
    chip_masks, t_count = cfg
    me = Ids(ids_ref, t_count)
    mixes, refs = refs[: len(chip_masks)], refs[len(chip_masks) :]
    landed, d_qkv, sums, k_heads, v_heads, q_heads, m_heads, dk, dv, mask = refs
    length, feats = qkv.shape[0], dk.shape[1]
    own = mixes[0].shape[0]
    heads = feats // HD
    tile = min(256, length)
    scale = HD ** (-0.5)
    for h in range(heads):
        lanes = head_mask(feats, h)
        for k, m in enumerate(chip_masks):
            piece = mixes[k][:, :feats]
            m_heads[h, me.rows(0, m, own), :] = jnp.where(lanes, piece, jnp.zeros_like(piece))
            piece = landed[k * own : (k + 1) * own, :]
            m_heads[h, me.rows(1, m, own), :] = jnp.where(lanes, piece, jnp.zeros_like(piece))

    def prepare(i, carry):
        rows = at(i * tile, tile)
        for h in range(heads):
            lanes = head_mask(feats, h)
            for k, ref in ((0, q_heads), (1, k_heads), (2, v_heads)):
                piece = qkv[rows, k * feats : (k + 1) * feats]
                if k == 0:
                    piece = piece * BF16(scale)
                ref[h, rows, :] = jnp.where(lanes, piece, jnp.zeros_like(piece))
        dk[rows, :] = jnp.zeros((tile, feats), F32)
        dv[rows, :] = jnp.zeros((tile, feats), F32)
        return carry

    lax.fori_loop(0, length // tile, prepare, 0)
    back = -(-DOC_MOST // tile)
    for i in range(length // tile):
        first = max(0, i - back) * tile
        keys = (i + 1) * tile - first
        rows = slice(i * tile, (i + 1) * tile)
        span = slice(first, first + keys)
        same = seg_col[span, 0:1] == seg_row[:, rows]
        k_pos = first + lax.broadcasted_iota(jnp.int32, (keys, tile), 0)
        q_pos = i * tile + lax.broadcasted_iota(jnp.int32, (keys, tile), 1)
        mask[:keys, :] = jnp.where(same & (k_pos <= q_pos), 0.0, NEGATIVE)
        dq = jnp.zeros((tile, feats), F32)
        dvs = jnp.zeros((keys, feats), F32)
        dks = jnp.zeros((keys, feats), F32)
        for h in range(heads):
            k, v, q, m = k_heads[h, span, :], v_heads[h, span, :], q_heads[h, rows, :], m_heads[h, rows, :]
            s = mm(k, q, NT) + mask[:keys, :]
            e = jnp.exp(s - jnp.max(s, axis=0, keepdims=True))
            p = e * (1.0 / jnp.sum(e, axis=0, keepdims=True))
            dp = mm(v, m, NT)
            row_dot = jnp.sum(p * dp, axis=0, keepdims=True)
            ds = (p * (dp - row_dot)).astype(BF16)
            dvs += mm(p.astype(BF16), m, NN)
            dks += mm(ds, q, NN)
            dq += mm(ds, k, TN)
        dv[span, :] += dvs
        dk[span, :] += dks
        d_qkv[rows, :feats] = (dq * scale).astype(BF16)

    def finish(i, carry):
        rows = at(i * tile, tile)
        d_qkv[rows, feats : 2 * feats] = dk[rows, :].astype(BF16)
        d_qkv[rows, 2 * feats :] = dv[rows, :].astype(BF16)
        return carry + jnp.sum(d_qkv[rows, :].astype(F32), axis=0, keepdims=True)

    sums[...] = lax.fori_loop(0, length // tile, finish, jnp.zeros((1, 3 * feats), F32))


def first_back_kernel(cfg, ids_ref, d_qkv, weight, vhat, keep, give, grads):
    chip_masks, own, t_count = cfg
    me = Ids(ids_ref, t_count)
    span = own * t_count
    gain = jnp.zeros((1, vhat.shape[1]), F32)
    bias = gain
    for out, side in ((give, 1), (keep, 0)):
        for k, mask in enumerate(chip_masks[::t_count]):
            c = (me.y ^ (mask // t_count)) * 2 + (me.core ^ side)
            rows = at(c * span, span)
            d = mm(d_qkv[rows, :], weight[...], NT)
            for t in range(t_count):
                to = at(k * span + (t ^ me.t) * own, own)
                out[to, :] = d[t * own : (t + 1) * own, :].astype(BF16)
            gain += jnp.sum(vhat[rows, :] * d, axis=0, keepdims=True)
            bias += jnp.sum(d, axis=0, keepdims=True)
    grads[0:1, :] = gain
    grads[1:2, :] = bias


def attn_grad_kernel(cfg, ids_ref, normed, d_qkv, attn, branch_a, branch_b, small, small_other, *refs):
    chip_masks, t_count, z_count, vec = cfg
    me = Ids(ids_ref, t_count)
    outs, branch = refs[:-1], refs[-1]
    own = branch_a.shape[0] // len(chip_masks)
    for side, ref in ((0, branch_a), (1, branch_b)):
        for k, mask in enumerate(chip_masks):
            branch[me.rows(side, mask, own), :] = ref[k * own : (k + 1) * own, :]
    count = small.shape[0] // z_count
    feats = attn.shape[1]
    part = normed.shape[1] // z_count
    row = lax.broadcasted_iota(jnp.int32, (count, feats), 0)
    for r in range(z_count - 1, -1, -1):
        out = outs[r]
        cols = at((me.z ^ r) * part, part)
        g = mm(normed[:, cols], d_qkv[...], TN)
        for k in range(3):
            out[k * part : (k + 1) * part, :] = g[:, k * feats : (k + 1) * feats].astype(BF16)
        out[3 * part : 4 * part, :] = mm(branch[:, cols], attn[...], TN).astype(BF16)
        mine = small[r * count : (r + 1) * count, :].astype(F32)
        both = mine + small_other[r * count : (r + 1) * count, :].astype(F32)
        out[4 * part :, :] = jnp.where(row < vec, both, mine).astype(BF16)


def last_kernel(t_count, ids_ref, *refs):
    me = Ids(ids_ref, t_count)
    x, vecs, d_res, out = refs[-4:]
    own = out.shape[0]
    d_norm = refs[0][...].astype(F32)
    for ref in refs[1:-4]:
        d_norm += ref[...].astype(F32)
    vhat, scale = normalise(x[at(me.t * own, own), :].astype(F32))
    out[...] = (d_res[...] + norm_grad(vhat, scale, vecs[0:1, :] * d_norm)).astype(BF16)


def output_kernel(ids_ref, *refs):
    residual, vecs, out = refs[-3:]
    total = residual[...] + vecs[5:6, :]
    for ref in refs[:-3]:
        total += ref[...].astype(F32)
    out[...] = total.astype(BF16)


def pair_kernel(ids_ref, mine, other, out):
    own = mine.shape[0]
    out[at(ids_ref[3] * own, own), :] = mine[...]
    out[at((1 - ids_ref[3]) * own, own), :] = other[...]


def small_grad_kernel(cfg, ids_ref, one, two, sums, bup_a, bup_b, out):
    z_count, heads, rows_up, cols_up = cfg
    width = one.shape[1]
    part = width // z_count
    feats = sums.shape[1] // 3
    units = bup_a.shape[1]
    each = HD // z_count
    wide = out.shape[1]
    vec, q, q_rows, u, u_rows, total = small_rows(part, heads, z_count, rows_up, cols_up, wide)
    per = part // wide
    bqv = (sums[:, :feats].astype(BF16), sums[:, 2 * feats :].astype(BF16))
    bup = (bup_a[...] + bup_b[...]).astype(BF16)
    out[...] = jnp.zeros(out.shape, out.dtype)
    for r in range(z_count):
        z = ids_ref[0] ^ r
        base = r * total
        for i in range(6):
            ref, row = (one, i) if i < 2 else (two, i - 2)
            for j in range(per):
                k = base + i * per + j
                if wide % 128 == 0:
                    out[k : k + 1, :] = ref[row : row + 1, at(z * part + j * wide, wide)].astype(BF16)
                else:
                    lane = lax.broadcasted_iota(jnp.int32, (wide, width), 0)
                    goal = lax.broadcasted_iota(jnp.int32, (wide, width), 1)
                    move = jnp.where(goal == z * part + j * wide + lane, 1.0, 0.0).astype(BF16)
                    out[k : k + 1, :] = mm(ref[row : row + 1, :].astype(BF16), move, NT).astype(BF16)
        lane = lax.broadcasted_iota(jnp.int32, (wide, feats), 0)
        goal = lax.broadcasted_iota(jnp.int32, (wide, feats), 1)
        for i in range(q_rows):
            line = jnp.zeros((1, wide), F32)
            for k in range(2):
                place = lane + i * wide - k * heads * each
                move = (place >= 0) & (place < heads * each)
                move &= goal == (place // each) * HD + z * each + place % each
                line += mm(bqv[k], jnp.where(move, 1.0, 0.0).astype(BF16), NT)
            out[base + vec + i : base + vec + i + 1, :] = line.astype(BF16)
        lane = lax.broadcasted_iota(jnp.int32, (wide, units), 0)
        goal = lax.broadcasted_iota(jnp.int32, (wide, units), 1)
        for i in range(u_rows):
            place = lane + i * wide
            move = (place < u) & (goal == (place // cols_up) * 128 + z * cols_up + place % cols_up)
            row = base + vec + q_rows + i
            out[row : row + 1, :] = mm(bup, jnp.where(move, 1.0, 0.0).astype(BF16), NT).astype(BF16)


def mlp_place_kernel(c_masks, ids_ref, *refs):
    blocks, (up, down) = refs[:-2], refs[-2:]
    c = ids_ref[1] * 2 + ids_ref[2]
    units = blocks[0].shape[1]
    part = blocks[0].shape[0] // 2
    for r, mask in enumerate(c_masks):
        where = at((c ^ mask) * units, units)
        up[:, where] = blocks[r][:part, :].astype(F32)
        down[where, :] = blocks[r][part:, :].astype(F32).T


def attn_place_kernel(cfg, ids_ref, *refs):
    c_masks, heads, rows_up, vec, q_rows = cfg
    blocks = refs[: len(c_masks)]
    qkv, out, *vecs, b_qv, b_up = refs[len(c_masks) :]
    c = ids_ref[1] * 2 + ids_ref[2]
    wide = blocks[0].shape[1]
    part = vecs[0].shape[0]
    each, cols_up = b_qv.shape[2], b_up.shape[1]
    aligned = wide % 128 == 0
    for r, mask in enumerate(c_masks):
        where = at((c ^ mask) * wide, wide)
        if aligned:
            for k in range(3):
                qkv[k, :, where] = blocks[r][k * part : (k + 1) * part, :].astype(F32)
        else:
            for k in range(3):
                qkv[c ^ mask, k] = blocks[r][k * part : (k + 1) * part, :].astype(F32)
        out[where, :] = blocks[r][3 * part : 4 * part, :].astype(F32).T
        base = 4 * part + vec
        for k in range(2):
            for h in range(heads):
                flat = (k * heads + h) * each
                row, lane = base + flat // wide, flat % wide
                b_qv[k, pl.ds((c ^ mask) * heads + h, 1), :] = blocks[r][
                    row : row + 1, lane : lane + each
                ].astype(F32)
        for i in range(rows_up):
            row, lane = base + q_rows + (i * cols_up) // wide, (i * cols_up) % wide
            b_up[pl.ds((c ^ mask) * rows_up + i, 1), :] = blocks[r][
                row : row + 1, lane : lane + cols_up
            ].astype(F32)
    total = blocks[0][4 * part : 4 * part + vec, :].astype(F32)
    for block in blocks[1:]:
        total += block[4 * part : 4 * part + vec, :].astype(F32)
    per = part // wide
    for i, ref in enumerate(vecs):
        lines = [total[i * per + j : i * per + j + 1, :] for j in range(per)]
        ref[...] = (jnp.concatenate(lines, axis=1) if per > 1 else lines[0]).reshape(part)


def body(
    tokens,
    segments,
    ln1_gain,
    ln1_bias,
    w_qkv,
    b_qv,
    w_out,
    b_out,
    ln2_gain,
    ln2_bias,
    w_up,
    b_up,
    w_down,
    b_down,
    cotangent,
):
    z_count, t_count, y_count = (lax.axis_size(a) for a in ("fsdp", "tp", "y"))
    z_me, y_me, core, t_me = (lax.axis_index(a) for a in ("fsdp", "y", "core", "tp"))
    c_me = y_me * 2 + core
    c_count = size_of(CTX)
    c_masks, chip_masks = masks_of(CTX), masks_of(CHIPS)
    chips = len(chip_masks)
    x_span, cot_span = tokens[0], cotangent[0]
    span, width = x_span.shape
    length = span * c_count
    half = length // 2
    own = span // t_count
    feats = w_qkv.shape[2] // c_count
    heads = feats // HD
    units = w_up.shape[1] // c_count
    part = width // z_count
    tile = min(256, length)
    keys = min(length, (-(-DOC_MOST // tile) + 1) * tile)
    rows_up, cols_up = b_up.shape[0] // c_count, b_up.shape[1]
    vec, _, q_rows, _, _, small_count = small_rows(part, heads, z_count, rows_up, cols_up, feats)
    Z, TP = ("fsdp",), ("tp",)
    turned = jnp.swapaxes(w_qkv, 0, 1)
    raw = [ln1_gain, ln1_bias, b_out, ln2_gain, ln2_bias, b_down, b_qv, b_up]
    pack_cfg = (z_count, heads, rows_up, cols_up)
    z_all, c_all = range(z_count), range(c_count)
    known, order, cost = {}, {}, {}

    def node(make):
        def value(*index):
            if (value, index) not in known:
                known[value, index] = make(*index)
            return known[value, index]

        value.title = make.__name__
        return value

    def waits(*key):
        return order[key]() if key in order else []

    def move(key, value, axes, bits):
        pins = waits(*key)
        return swap(after(value, *pins) if pins else value, axes, bits)

    def run(key, kernel, outs, arrays, index=(), **more):
        deps = waits(key, *index)
        declared = cost.get(key, 0.1)
        return kernel_call(kernel, outs, arrays, deps=deps, cost=declared, name=key.title, **more)

    def gathered(key, source, axes, r):
        low = r & -r
        return move((key, r), key(r ^ low), axes, low) if r else source

    def from_chip(key, source, k):
        return move((key, k), source, CHIPS, chip_masks[k]) if k else source

    @node
    def pack():
        out = [shape((4 * part + small_count, feats))]
        if feats % 128:
            cuts = [
                lax.dynamic_slice_in_dim(turned, c_me * feats, feats, 2),
                lax.dynamic_slice_in_dim(w_out, c_me * feats, feats, 0),
            ]
            return run(pack, partial(pack_plain_kernel, pack_cfg), out, [*cuts, *raw])
        scratch = [pltpu.VMEM((feats, part), BF16), *[pltpu.VMEM(v.shape, BF16) for v in raw]]
        return run(
            pack,
            partial(pack_kernel, pack_cfg),
            out,
            [],
            anys=[turned, w_out, *raw],
            scratch=[*scratch, pltpu.SemaphoreType.DMA((12,))],
        )

    @node
    def rows():
        return run(
            rows,
            pack_rows_kernel,
            [shape((own, width)), shape((own, width)), shape((span, width))],
            [],
            anys=[cot_span],
            scratch=[pltpu.SemaphoreType.DMA((4,))],
        )

    @node
    def norm():
        return run(
            norm,
            partial(first_norm_kernel, (c_masks, t_count)),
            [shape((length, width), F32), shape((1, length), F32), shape((length, 128), F32)],
            [x(r) for r in c_all] + [seg(r) for r in c_all],
        )

    @node
    def cut():
        return run(
            cut,
            cut_mlp_kernel,
            [shape((part, units))] * 2,
            [],
            anys=[w_up, w_down],
            scratch=[pltpu.VMEM((units, part), BF16), pltpu.SemaphoreType.DMA((2,))],
        )

    @node
    def unpack():
        return run(
            unpack,
            partial(unpack_kernel, pack_cfg),
            [
                shape((width, 3 * feats)),
                shape((width, feats)),
                shape((8, width), F32),
                shape((2, feats), F32),
                shape((1, units), F32),
            ],
            [attn(r) for r in z_all],
        )

    @node
    def attend():
        vhat, seg_row, seg_col = norm()
        qkv_full, _, vecs, bias_qv, _ = unpack()
        return run(
            attend,
            partial(attend_kernel, (chip_masks, t_count)),
            [
                shape((length, width)),
                shape((length, 3 * feats)),
                shape((length, feats)),
                shape((half, feats)),
                shape((half, feats)),
            ],
            [vhat, qkv_full, vecs, bias_qv, seg_row, seg_col],
            scratch=[pltpu.VMEM((heads, length, feats), BF16)] * 2 + [pltpu.VMEM((tile, keys), F32)],
        )

    def cat(key, blocks):
        size, cols = blocks[0].shape
        return run(key, cat_kernel, [shape((size * len(blocks), cols))], blocks)

    @node
    def wcat():
        return cat(wcat, [wout(k) for k in range(chips)])

    @node
    def beside():
        pieces = [shape((own, 2 * feats))] * chips
        return run(beside, beside_kernel, pieces, [attend()[3], give_mix()])

    @node
    def out_norm():
        return run(
            out_norm,
            partial(out_norm_kernel, t_count),
            [shape((own, width), F32), shape((own, width))],
            [*[mixed(k) for k in range(chips)], wcat()[0], w_other(), x_span, unpack()[2]],
        )

    @node
    def ncat():
        return cat(ncat, [normed(k) for k in range(chips)])

    @node
    def cots():
        pieces = []
        for y in range(1, y_count):
            pieces += [cot_a(y), cot_a_core(y), cot_b(y), cot_b_core(y)]
        return run(
            cots,
            partial(cot_kernel, chip_masks, t_count),
            [shape((length, width))],
            [rows()[2], cot_core(), *pieces],
        )

    @node
    def up_full():
        return run(up_full, place_kernel, [shape((width, units))], [up(r) for r in z_all])

    @node
    def down_full():
        return run(down_full, place_kernel, [shape((width, units))], [down_w(r) for r in z_all])

    @node
    def hidden():
        return run(
            hidden,
            hidden_kernel,
            [shape((half, units))] * 2 + [shape((half, units), F32)] * 2,
            [ncat()[0], normed_b(), up_full()[0], unpack()[4]],
        )

    def back(key, side):
        return run(
            key,
            partial(hidden_back_kernel, side),
            [shape((half, units)), shape((half, width)), shape((1, units), F32)],
            [hidden()[2 + side], cots()[0], down_full()[0], up_full()[0]],
        )

    def join(key, keep, give):
        return run(key, join_kernel, [shape((own, width))] * chips, [keep, give])

    def join_far(key, keep, give):
        outs = [shape((y_count * own, width))] * 2
        return run(key, partial(join_far_kernel, chips), outs, [keep, give])

    def fold(key, near, landed):
        return run(key, fold_kernel, [shape((own, width))] * y_count, [near, landed])

    @node
    def grad_down():
        return run(
            grad_down,
            down_grad_kernel,
            [shape((part, units))] * z_count,
            [cots()[0], hidden()[0], hidden()[1]],
        )

    @node
    def grad_up():
        return run(
            grad_up,
            up_grad_kernel,
            [shape((part if r != 1 else 2 * part, units)) for r in z_all],
            [ncat()[0], normed_b(), back_a()[0], back_b()[0], grad_down()[1]],
        )

    @node
    def down():
        return run(
            down,
            down_kernel,
            [shape((half, width))] * 2,
            [hidden()[0], hidden()[1], down_full()[0]],
        )

    def z_total(key, arrived, pieces, r):
        value = pieces[r]
        for low in (1, 2, 4):
            if low < (r & -r) and r | low < z_count:
                out = [shape(value.shape)]
                (value,) = run(key, add_kernel, out, [value, arrived(r | low)], index=(r,))
        return value

    def z_ends(arrived):
        return [arrived(r) for r in z_all if r > 1 and r == r & -r]

    @node
    def mlp_sums():
        ups = [grad_up()[0], *z_ends(du_in)]
        downs = [grad_down()[0], *z_ends(dd_in)]
        return run(
            mlp_sums,
            partial(mlp_sums_kernel, len(ups)),
            [shape((2 * part, units))],
            [near(), *ups, *downs],
        )

    @node
    def res_back():
        return run(
            res_back,
            partial(second_back_kernel, chips),
            [shape((own, width), F32), shape((own, width)), shape((4, width), F32)]
            + [shape((own, 2 * feats))] * chips,
            [
                *[two(k) for k in range(chips)],
                out_norm()[0],
                rows()[0],
                unpack()[2],
                wcat()[0],
                w_other(),
            ],
        )

    @node
    def apart():
        return run(apart, apart_kernel, [shape((half, feats))], [d_mix(k) for k in range(chips)])

    @node
    def attend_back():
        return run(
            attend_back,
            partial(attend_back_kernel, (chip_masks, t_count)),
            [shape((length, 3 * feats)), shape((1, 3 * feats), F32)],
            [
                attend()[1],
                norm()[1],
                norm()[2],
                *[d_mix(k) for k in range(chips)],
                d_mix_core(),
            ],
            scratch=[pltpu.VMEM((heads, length, feats), BF16)] * 4
            + [pltpu.VMEM((length, feats), F32)] * 2
            + [pltpu.VMEM((keys, tile), F32)],
        )

    @node
    def bcat():
        return cat(bcat, [branch(k) for k in range(chips)])

    @node
    def norm_back():
        return run(
            norm_back,
            partial(first_back_kernel, (chip_masks, own, t_count)),
            [shape((half, width)), shape((half, width)), shape((2, width), F32)],
            [attend_back()[0], unpack()[0], norm()[0]],
        )

    @node
    def small():
        return run(
            small,
            partial(small_grad_kernel, (z_count, heads, rows_up, cols_up)),
            [shape((z_count * small_count, feats))],
            [norm_back()[2], res_back()[2], attend_back()[1], back_a()[2], back_b()[2]],
        )

    @node
    def grad_attn():
        return run(
            grad_attn,
            partial(attn_grad_kernel, (chip_masks, t_count, z_count, vec)),
            [shape((4 * part + small_count, feats))] * z_count,
            [
                attend()[0],
                attend_back()[0],
                attend()[2],
                bcat()[0],
                branch_b(),
                small()[0],
                small_tp(),
            ],
            scratch=[pltpu.VMEM((length, width), BF16)],
        )

    @node
    def attn_sums():
        terms = [grad_attn()[0], da_in(1), *z_ends(da_in)]
        return run(attn_sums, sum_kernel, [shape(terms[0].shape)], terms)

    @node
    def last():
        return run(
            last,
            partial(last_kernel, t_count),
            [shape((own, width))],
            [fold_one()[0], *[one(y) for y in range(1, y_count)], x_span, unpack()[2], res_back()[0]],
        )

    @node
    def out():
        sums = [fold_down()[0], *[down_in(y) for y in range(1, y_count)]]
        arrays = [*sums, out_norm()[0], unpack()[2]]
        return run(out, output_kernel, [shape((own, width))], arrays)

    def pair(key, mine, other):
        return run(key, pair_kernel, [shape((span, width))], [mine, other])

    @node
    def mlp_place():
        return run(
            mlp_place,
            partial(mlp_place_kernel, c_masks),
            [shape((part, c_count * units), F32), shape((c_count * units, part), F32)],
            [mlp_all(r) for r in c_all],
        )

    @node
    def attn_place():
        return run(
            attn_place,
            partial(attn_place_kernel, (c_masks, heads, rows_up, vec, q_rows)),
            [
                shape((3, part, c_count * feats) if feats % 128 == 0 else (c_count, 3, part, feats), F32),
                shape((c_count * feats, part), F32),
                *[shape((part,), F32)] * 6,
                shape(b_qv.shape, F32),
                shape(b_up.shape, F32),
            ],
            [attn_all(r) for r in c_all],
        )

    @node
    def back_a():
        return back(back_a, 0)

    @node
    def back_b():
        return back(back_b, 1)

    @node
    def join_two():
        return join(join_two, back_a()[1], give_two())

    @node
    def join_down():
        return join_far(join_down, down()[0], give_down())

    @node
    def fold_down():
        return fold(fold_down, join_down()[0], down_x())

    @node
    def join_one():
        return join_far(join_one, norm_back()[0], give_one())

    @node
    def fold_one():
        return fold(fold_one, join_one()[0], one_x())

    @node
    def pair_out():
        return pair(pair_out, out()[0], out_tp())

    @node
    def pair_tok():
        return pair(pair_tok, last()[0], last_tp())

    @node
    def dd_sum(r):
        return z_total(dd_sum, dd_in, grad_down(), r)

    @node
    def du_sum(r):
        return z_total(du_sum, du_in, grad_up(), r)

    @node
    def da_sum(r):
        return z_total(da_sum, da_in, grad_attn(), r)

    attn = node(lambda r: gathered(attn, pack()[0], Z, r))
    x = node(lambda r: gathered(x, x_span, CTX, r))
    seg = node(lambda r: gathered(seg, segments, CTX, r))
    up = node(lambda r: gathered(up, cut()[0], Z, r))
    down_w = node(lambda r: gathered(down_w, cut()[1], Z, r))
    cot_core = node(lambda: move((cot_core,), rows()[2], CTX, 1))
    cot_a = node(lambda y: move((cot_a, y), rows()[0], CTX, 2 * y))
    cot_b = node(lambda y: move((cot_b, y), rows()[1], CTX, 2 * y))
    cot_a_core = node(lambda y: move((cot_a_core, y), cot_a(y), CTX, 1))
    cot_b_core = node(lambda y: move((cot_b_core, y), cot_b(y), CTX, 1))
    wout = node(lambda k: from_chip(wout, unpack()[1], k))
    w_other = node(lambda: move((w_other,), wcat()[0], CTX, 1))
    give_mix = node(lambda: move((give_mix,), attend()[4], CTX, 1))
    mixed = node(lambda k: from_chip(mixed, beside()[k], k))
    normed = node(lambda k: from_chip(normed, out_norm()[1], k))
    normed_b = node(lambda: move((normed_b,), ncat()[0], CTX, 1))
    give_two = node(lambda: move((give_two,), back_b()[1], CTX, 1))
    two = node(lambda k: from_chip(two, join_two()[k], k))
    give_down = node(lambda: move((give_down,), down()[1], CTX, 1))
    down_x = node(lambda: move((down_x,), join_down()[1], TP, 1))
    down_in = node(lambda y: move((down_in, y), fold_down()[y], CTX, 2 * y))
    give_one = node(lambda: move((give_one,), norm_back()[1], CTX, 1))
    one_x = node(lambda: move((one_x,), join_one()[1], TP, 1))
    one = node(lambda y: move((one, y), fold_one()[y], CTX, 2 * y))
    d_mix = node(lambda k: from_chip(d_mix, res_back()[3 + k], k))
    d_mix_core = node(lambda: move((d_mix_core,), apart()[0], CTX, 1))
    branch = node(lambda k: from_chip(branch, res_back()[1], k))
    branch_b = node(lambda: move((branch_b,), bcat()[0], CTX, 1))
    small_tp = node(lambda: move((small_tp,), small()[0], TP, 1))
    near = node(lambda: move((near,), grad_up()[1], Z, 1))
    dd_in = node(lambda r: move((dd_in, r), dd_sum(r), Z, r & -r))
    du_in = node(lambda r: move((du_in, r), du_sum(r), Z, r & -r))
    da_in = node(lambda r: move((da_in, r), da_sum(r), Z, r & -r))
    out_tp = node(lambda: move((out_tp,), out()[0], TP, 1))
    last_tp = node(lambda: move((last_tp,), last()[0], TP, 1))
    mlp_all = node(lambda r: gathered(mlp_all, mlp_sums()[0], CTX, r))
    attn_all = node(lambda r: gathered(attn_all, attn_sums()[0], CTX, r))

    order |= {
        (x, 3): lambda: [attn(1), attn(2), seg(1)],
        (cut,): lambda: [norm()[1]],
        (unpack,): lambda: [norm()[1], cut()[0], cot_a(1)],
        (attend,): lambda: [attn(3)],
        (wcat,): lambda: [up(1)],
        (out_norm,): lambda: [up(3)],
        (ncat,): lambda: [down_w(1), down_w(2)],
        (cots,): lambda: [ncat()[0]],
        (up_full,): lambda: [cots()[0]],
        (down_full,): lambda: [hidden()[0], normed(3)],
        (grad_up,): lambda: [join_two()[0]],
        (dd_sum, 2): lambda: [down()[0]],
        (branch, 2): lambda: [dd_sum(2)],
        (branch, 3): lambda: [apart()[0]],
        (attend_back,): lambda: [d_mix(3)],
        (join_one,): lambda: [grad_attn()[0], mlp_all(1), branch(3), small()[0]],
        (mlp_all, 3): lambda: [mlp_all(1), small_tp()],
        (last,): lambda: [mlp_all(1)],
        (small,): lambda: [branch(2)],
        (normed_b,): lambda: [mixed(2)],
        (two, 3): lambda: [normed_b()],
        (two, 2): lambda: [normed(2), join_two()[0]],
        (mixed, 2): lambda: [w_other()],
        (cot_a_core, 1): lambda: [wout(3)],
        (rows,): lambda: [pack()[0]],
        (dd_in, 2): lambda: [grad_up()[0]],
        (cot_a, 1): lambda: [cot_core()],
        (norm_back,): lambda: [mlp_sums()[0]],
        (down_w, 3): lambda: [normed(3)],
        (grad_attn,): lambda: [give_one()],
        (attn_place,): lambda: [attn_sums()[0]],
        (mixed, 3): lambda: [up(2), wout(2)],
        (du_in, 2): lambda: [res_back()[0]],
        (cot_core,): lambda: [seg(3), x(2)],
        (down_w, 1): lambda: [out_norm()[0]],
        (back_a,): lambda: [normed_b()],
        (mlp_sums,): lambda: [d_mix_core(), du_sum(2), d_mix(3)],
        (branch_b,): lambda: [d_mix_core(), branch(3)],
        (da_in, 3): lambda: [mlp_all(1)],
        (fold_one,): lambda: [join_one()[0]],
        (give_one,): lambda: [branch(2)],
        (branch, 1): lambda: [du_sum(2), d_mix(1)],
        (down_in, 1): lambda: [give_one()],
        (fold_down,): lambda: [join_one()[0]],
    }
    cost |= {
        pack: 8,
        rows: 0.01,
        norm: 8,
        cut: 1,
        unpack: 1,
        attend: 8,
        out_norm: 1,
        cots: 4,
        up_full: 2,
        down_full: 2,
        hidden: 0.3,
        back_b: 2,
        grad_up: 1.5,
        down: 1,
        res_back: 0.01,
        small: 8,
        grad_attn: 4,
        last: 1,
        out: 1,
        pair_out: 1,
        pair_tok: 16,
        mlp_place: 1,
        apart: 2,
        beside: 8,
        ncat: 16,
        attn_sums: 4,
        da_sum: 0.01,
        bcat: 4,
        dd_sum: 0.01,
        norm_back: 1,
        join_one: 1,
        du_sum: 8,
    }
    full_qkv, full_out, *vec_sum, full_bqv, full_bup = attn_place()
    if feats % 128:
        full_qkv = full_qkv.transpose(1, 2, 0, 3).reshape(3, part, c_count * feats)
    full_up, full_down = mlp_place()
    return (
        pair_out()[0][None],
        pair_tok()[0][None],
        vec_sum[0],
        vec_sum[1],
        jnp.swapaxes(full_qkv, 0, 1),
        full_bqv,
        full_out,
        vec_sum[2],
        vec_sum[3],
        vec_sum[4],
        full_up,
        full_bup,
        full_down,
        vec_sum[5],
    )


def solution(mesh):
    fsdp, ctx, tp = (mesh.shape[a] for a in ("fsdp", "ctx", "tp"))
    split = Mesh(mesh.devices.reshape(fsdp, ctx // 2, 2, tp), ("fsdp", "y", "core", "tp"))
    rows = P("fsdp", CTX, None)
    shares = (
        P("fsdp"),
        P("fsdp"),
        P("fsdp", None, "tp"),
        P(None, "tp", "fsdp"),
        P("tp", "fsdp"),
        P("fsdp"),
        P("fsdp"),
        P("fsdp"),
        P("fsdp", "tp"),
        P("tp", "fsdp"),
        P("tp", "fsdp"),
        P("fsdp"),
    )
    return jax.shard_map(
        body,
        mesh=split,
        in_specs=(rows, P("fsdp", CTX), *shares, rows),
        out_specs=(rows, rows, *shares),
        check_vma=False,
    )
```
